512 devices in a mesh: dp: 128 (over z, x, core), layer: 4 (over y).
Axes of the slice: x: 4, y: 4, z: 16, core: 2. Of those that a mesh axis runs over, the one named last changes fastest.
Arguments:
- micro_grads: bfloat16 [4, 128, 256, 2048], P('layer', 'dp')
- master: float32 [4, 384, 2, 2048], P('layer', 'dp'), may hold values from -6 to 6
- moment_one: float32 [4, 384, 2, 2048], P('layer', 'dp'), may hold values from -4 to 4
- moment_two: float32 [4, 384, 2, 2048], P('layer', 'dp'), may hold values from 0.01 to 1
- owner: int32 [4, 128], P('layer'), may hold values from 0 to 127, as said below
- slot: int32 [4, 128], P('layer'), may hold values from 0 to 2, as said below
Outputs:
- new_master: float32 [4, 384, 2, 2048], P('layer', 'dp')
- new_moment_one: float32 [4, 384, 2, 2048], P('layer', 'dp')
- new_moment_two: float32 [4, 384, 2, 2048], P('layer', 'dp')
- weights: bfloat16 [4, 256, 2048], P('layer')
- grad_rms: float32 [], replicated
The draws below stay inside these ranges and needn't reach their ends.
Inputs may be any that keep to these rules, and one draw needn't show every extreme that they name: In every layer no owner holds more than 3 blocks, and some owner holds exactly 3. The pairs (owner, slot) of one layer are all different.
All inputs are finite; a program needn't handle non-finite values.
Results may differ from the reference program's by a relative error of at most 0.0004.
Values may be sent and summed in bfloat16 or wider, within the bound.
No kernel may reach another device: no remote copies, remote signals or barrier semaphores. Data moves between devices by JAX's collectives and lax.ppermute only.
A program may use at most 64 MiB of HBM per device.

```python
import math
import jax
import jax.numpy as jnp
from jax import lax

D = 2048
SLAB = 2
MICRO = 1
CAP = 3
NMAT = 128
LAYERS = 4
N_DP = 128


def draw_micro_grads(key, part):
    first_key, second_key = jax.random.split(key, 2)
    row_count = NMAT * SLAB
    rising = 3.0 ** (0.5 * jnp.arange(row_count, dtype=jnp.float32) / (row_count - 1))
    spread = jnp.exp(jax.random.uniform(first_key, (LAYERS, 1, row_count, 1), jnp.float32, 0.0, math.log(10.0)))
    row_scale = spread * rising[None, None, :, None]
    shape = (LAYERS, N_DP * MICRO, row_count, D)
    values = jnp.clip(jax.random.normal(second_key, shape, jnp.float32), -6.0, 6.0) * row_scale
    return values.astype(jnp.bfloat16)


def owner_slot_ids(key):

    def one_layer(layer_key):
        first_key, second_key, third_key = jax.random.split(layer_key, 3)
        full_owner = jax.random.randint(first_key, (), 0, N_DP, jnp.int32)
        others = jax.random.permutation(second_key, N_DP * CAP - CAP)[:NMAT - CAP].astype(jnp.int32)
        others = others + CAP * (others >= full_owner * CAP).astype(jnp.int32)
        slot_order = jax.random.permutation(third_key, CAP).astype(jnp.int32)
        block_ids = jnp.arange(NMAT, dtype=jnp.int32)
        far_block = (full_owner + N_DP // 2) % N_DP
        next_block = (full_owner + 1) % N_DP
        prev_block = (full_owner + N_DP - 1) % N_DP
        is_far = block_ids == far_block
        is_next = block_ids == next_block
        is_prev = block_ids == prev_block
        special = is_far | is_next | is_prev
        special_slot = jnp.where(is_far, slot_order[0], jnp.where(is_next, slot_order[1], slot_order[2]))
        rank = jnp.cumsum((~special).astype(jnp.int32)) - 1
        rank = jnp.clip(rank, 0, NMAT - CAP - 1)
        return jnp.where(special, full_owner * CAP + special_slot, others[rank]).astype(jnp.int32)
    layer_keys = jax.random.split(jax.random.fold_in(key, 7), LAYERS)
    return jax.vmap(one_layer)(layer_keys)


def draw_owner(key, part):
    return owner_slot_ids(key) // CAP


def draw_slot(key, part):
    return owner_slot_ids(key) % CAP


def block_scale(stream_key, dims, cuts, smallest, high):
    factor_of, own = 1.0, jax.random.fold_in(stream_key, 6)
    for axis_at, blocks in cuts:
        heights = jnp.exp(jax.random.uniform(jax.random.fold_in(own, axis_at), (blocks,), jnp.float32, smallest / len(cuts), high / len(cuts)))
        factor_of = factor_of * jnp.repeat(heights, dims[axis_at] // blocks).reshape([-1 if axis == axis_at else 1 for axis in range(len(dims))])
    return factor_of


def bell_draw(stream_key, dims, width, reach, cuts=(), kind=jnp.bfloat16):
    values = width * jax.random.normal(stream_key, dims, jnp.float32)
    if cuts:
        values = values * block_scale(stream_key, dims, cuts, -0.22, 0.18)
    return jnp.clip(values, -reach, reach).astype(kind)


def setup_inputs(seed: int = 0) -> dict:
    keys = jax.random.split(jax.random.key(seed), 7)
    micro_grads = draw_micro_grads(jax.random.fold_in(keys[6], 71), 0)
    master = bell_draw(keys[1], (LAYERS, N_DP * CAP, SLAB, D), 1.0, 6.0, ((0, 4), (1, 128)), jnp.float32)
    moment_one = bell_draw(keys[2], (LAYERS, N_DP * CAP, SLAB, D), 0.5, 4.0, ((0, 4), (1, 128)), jnp.float32)
    moment_two = jnp.clip(jnp.exp(math.log(1.0) - 4.6051702 * jax.random.uniform(keys[3], (LAYERS, N_DP * CAP, SLAB, D), jnp.float32) ** block_scale(keys[3], (LAYERS, N_DP * CAP, SLAB, D), ((0, 4), (1, 128)), -0.2, 0.2)), 0.01, 1.0)
    owner = draw_owner(jax.random.fold_in(keys[6], 71), 0)
    slot = draw_slot(jax.random.fold_in(keys[6], 71), 0)
    return dict(micro_grads=micro_grads, master=master, moment_one=moment_one, moment_two=moment_two, owner=owner, slot=slot)


beta_one = 0.9
beta_two = 0.95
learn_rate = 0.0003
decay_rate = 0.1
adam_eps = 1e-08
step_number = 100.0

def adamw(param, first, second, grad):
    first_new = beta_one * first + (1.0 - beta_one) * grad
    second_new = beta_two * second + (1.0 - beta_two) * grad * grad
    corr_one = 1.0 - beta_one ** step_number
    corr_two = 1.0 - beta_two ** step_number
    update = first_new / corr_one / (jnp.sqrt(second_new / corr_two) + adam_eps) + decay_rate * param
    return (param - learn_rate * update, first_new, second_new)

def layer_sum(grads):

    def add_row(index, running):
        return running + grads[index].astype(jnp.float32)
    start = jnp.zeros(grads.shape[1:], jnp.float32)
    return lax.fori_loop(0, grads.shape[0], add_row, start)

def reference(micro_grads, master, moment_one, moment_two, owner, slot):
    totals = jnp.stack([layer_sum(micro_grads[layer_id]) for layer_id in range(LAYERS)])
    squares = jnp.sum(totals * totals)
    grad_rms = jnp.sqrt(squares / (LAYERS * NMAT * SLAB * D) + 1e-06)
    clip_factor = jnp.minimum(1.0, 1.0 / grad_rms)
    masters = []
    firsts = []
    seconds = []
    weight_list = []
    for layer_id in range(LAYERS):
        slot_index = (owner[layer_id] * CAP + slot[layer_id]).astype(jnp.int32)
        blocks = totals[layer_id].reshape(NMAT, SLAB, D) * clip_factor
        param, first, second = adamw(master[layer_id][slot_index], moment_one[layer_id][slot_index], moment_two[layer_id][slot_index], blocks)
        masters.append(master[layer_id].at[slot_index].set(param))
        firsts.append(moment_one[layer_id].at[slot_index].set(first))
        seconds.append(moment_two[layer_id].at[slot_index].set(second))
        weight_list.append(param.astype(jnp.bfloat16).reshape(NMAT * SLAB, D))
    return (jnp.stack(masters), jnp.stack(firsts), jnp.stack(seconds), jnp.stack(weight_list), grad_rms)
```

```python
import jax
import jax.numpy as jnp
from jax import lax
from jax.sharding import Mesh
from jax.sharding import PartitionSpec as P

beta_one = 0.9
beta_two = 0.95
learn_rate = 0.0003
decay_rate = 0.1
adam_eps = 1e-08
step_number = 100.0

RING = "z"
PLANE = ("x", "c")
PLANE_SHAPE = (4, 2)


def adamw(param, first, second, grad):
    first_new = beta_one * first + (1.0 - beta_one) * grad
    second_new = beta_two * second + (1.0 - beta_two) * grad * grad
    corr_one = 1.0 - beta_one**step_number
    corr_two = 1.0 - beta_two**step_number
    update = (
        first_new / corr_one / (jnp.sqrt(second_new / corr_two) + adam_eps) + decay_rate * param
    )
    return (param - learn_rate * update, first_new, second_new)


def exchange(chunks, axis):
    return lax.all_to_all(chunks, axis, 0, 0, tiled=True)


def share(value, axis):
    copies = jnp.broadcast_to(value[None], (lax.axis_size(axis), *value.shape))
    return exchange(lax.optimization_barrier(copies), axis)


def shards(micro_grads, master, moment_one, moment_two, owner, slot):
    rows, width = micro_grads.shape[2:]
    capacity, slab = master.shape[1:3]
    ring = lax.axis_size(RING)
    plane = lax.axis_size(PLANE)
    lines = capacity * slab
    wide = width // plane
    home = owner[0] * capacity + slot[0]
    home_row = (home[:, None] * slab + jnp.arange(slab, dtype=jnp.int32)[None, :]).reshape(rows)

    local = micro_grads[0, 0].reshape(rows, plane, wide).transpose(1, 0, 2)
    raw = exchange(local, PLANE)
    plane_sum = jnp.sum(raw.astype(jnp.float32), axis=0)
    piece = jnp.sum(exchange(plane_sum.reshape(ring, rows // ring, wide), RING), axis=0)
    totals = share(piece, RING).reshape(rows, wide)

    squares = jnp.broadcast_to(jnp.sum(totals * totals), (8, 128))
    squares = jnp.sum(share(squares, (*PLANE, "layer"))[:, 0, 0])
    element_total = lax.axis_size("layer") * rows * width
    grad_rms = jnp.sqrt(squares / element_total + 1e-06)
    clip_factor = jnp.minimum(1.0, 1.0 / grad_rms)

    states = jnp.stack([master[0], moment_one[0], moment_two[0]]).reshape(3 * lines, plane, wide)
    states = exchange(states.transpose(1, 0, 2), PLANE).reshape(plane, 3, lines, wide)
    old = [states[:, i].reshape(plane * lines, wide) for i in range(3)]
    slot_row = lax.axis_index(RING) * plane * lines + jnp.arange(plane * lines, dtype=jnp.int32)
    pick = slot_row[:, None] == home_row[None, :]
    grad_slots = jnp.dot(pick.astype(jnp.float32), totals, precision=lax.Precision.HIGHEST)
    new = adamw(*old, grad_slots * clip_factor)
    keep = jnp.any(pick, axis=1)[:, None]
    new = [jnp.where(keep, n, o) for n, o in zip(new, old, strict=True)]
    strip = new[0].astype(jnp.bfloat16)

    strips = share(strip, RING).reshape(ring * plane * lines, wide)
    place = home_row[:, None] == jnp.arange(ring * plane * lines, dtype=jnp.int32)[None, :]
    placed = jnp.dot(
        place.astype(jnp.bfloat16), strips, preferred_element_type=jnp.float32
    ).astype(jnp.bfloat16)
    halves = lax.all_gather(placed, "x", axis=0, tiled=False)
    others = lax.ppermute(halves, "c", [(0, 1), (1, 0)])
    first_core = lax.axis_index("c") == 0
    pair = [jnp.where(first_core, halves, others), jnp.where(first_core, others, halves)]
    weights = jnp.stack(pair, axis=1).transpose(2, 0, 1, 3).reshape(rows, width)

    back = jnp.stack([n.reshape(plane, lines, wide) for n in new], axis=1)
    back = exchange(back.reshape(plane, 3 * lines, wide), PLANE)
    back = back.transpose(1, 0, 2).reshape(3, 1, capacity, slab, width)
    return (back[0], back[1], back[2], weights[None], grad_rms)


def solution(mesh):
    ring = mesh.shape["dp"] // (PLANE_SHAPE[0] * PLANE_SHAPE[1])
    devices = mesh.devices.reshape(ring, *PLANE_SHAPE, mesh.shape["layer"])
    split = Mesh(devices, (RING, *PLANE, "layer"))
    dp = (RING, *PLANE)
    in_specs = (
        P("layer", dp, None, None),
        P("layer", dp, None, None),
        P("layer", dp, None, None),
        P("layer", dp, None, None),
        P("layer", None),
        P("layer", None),
    )
    out_specs = (
        P("layer", dp, None, None),
        P("layer", dp, None, None),
        P("layer", dp, None, None),
        P("layer", None, None),
        P(),
    )
    return jax.shard_map(
        shards, mesh=split, in_specs=in_specs, out_specs=out_specs, check_vma=False
    )
```

```python
import jax
import jax.numpy as jnp
from jax import lax
from jax.sharding import Mesh
from jax.sharding import PartitionSpec as P

beta_one = 0.9
beta_two = 0.95
learn_rate = 0.0003
decay_rate = 0.1
adam_eps = 1e-08
step_number = 100.0

RING = "z"
PLANE = ("x", "c")
PLANE_SHAPE = (4, 2)
SLOT_ROWS = 8


def adamw(param, first, second, grad):
    first_new = beta_one * first + (1.0 - beta_one) * grad
    second_new = beta_two * second + (1.0 - beta_two) * grad * grad
    corr_one = 1.0 - beta_one**step_number
    corr_two = 1.0 - beta_two**step_number
    update = (
        first_new / corr_one / (jnp.sqrt(second_new / corr_two) + adam_eps) + decay_rate * param
    )
    return (param - learn_rate * update, first_new, second_new)


def exchange(chunks, axis):
    return lax.all_to_all(chunks, axis, 0, 0, tiled=True)


def share(value, axis):
    copies = jnp.broadcast_to(value[None], (lax.axis_size(axis), *value.shape))
    return exchange(lax.optimization_barrier(copies), axis)


def split_terms(value):
    high = lax.reduce_precision(value, 8, 7)
    middle = lax.reduce_precision(value - high, 8, 7)
    return [high, middle, value - high - middle]


def shards(micro_grads, master, moment_one, moment_two, owner, slot):
    rows, width = micro_grads.shape[2:]
    capacity, slab = master.shape[1:3]
    ring = lax.axis_size(RING)
    plane = lax.axis_size(PLANE)
    lines = capacity * slab
    wide = width // plane
    layers = lax.axis_size("layer")
    bf16 = jnp.bfloat16
    home = (owner[0] * SLOT_ROWS + slot[0] * slab)[:, None]
    home = (home + jnp.arange(slab, dtype=jnp.int32)[None, :]).reshape(rows)

    states = [*split_terms(master[0]), moment_one[0], moment_two[0]]
    states = jnp.stack([s.astype(bf16) for s in states]).reshape(len(states), lines, width)
    states = jnp.pad(states, ((0, 0), (0, SLOT_ROWS - lines), (0, 0)))
    kinds = states.shape[0]
    local = jnp.concatenate([micro_grads[0, 0], states.reshape(kinds * SLOT_ROWS, width)])
    local = local.reshape(rows + kinds * SLOT_ROWS, plane, wide).transpose(1, 0, 2)
    raw = exchange(local, PLANE)
    plane_sum = jnp.sum(raw[:, :rows].astype(jnp.float32), axis=0)
    strips = raw[:, rows:].reshape(plane, kinds, SLOT_ROWS, wide).transpose(1, 0, 2, 3)
    strips = strips.reshape(kinds, plane * SLOT_ROWS, wide)

    strips = lax.all_gather(strips, RING, axis=0, tiled=False)

    piece = jnp.sum(exchange(plane_sum.reshape(ring, rows // ring, wide), RING), axis=0)
    totals = share(piece, RING).reshape(rows, wide)

    line = jnp.arange(plane * SLOT_ROWS, dtype=jnp.int32)
    pick = (lax.axis_index(RING) * plane * SLOT_ROWS + line)[:, None] == home[None, :]
    sent = jnp.dot(pick.astype(jnp.float32), totals, precision=lax.Precision.HIGHEST)
    sent = jnp.where((line % SLOT_ROWS == lines)[:, None], jnp.sum(totals * totals), sent)
    sent = jnp.broadcast_to(
        sent.reshape(plane, 1, SLOT_ROWS, wide), (plane, layers, SLOT_ROWS, wide)
    )
    got = exchange(sent.reshape(plane * layers, SLOT_ROWS, wide), (*PLANE, "layer"))
    squares = jnp.sum(got[:, lines, 0])
    grad_rms = jnp.sqrt(squares / (layers * rows * width) + 1e-06)
    clip_factor = jnp.minimum(1.0, 1.0 / grad_rms)

    strips = strips.transpose(1, 0, 2, 3).reshape(kinds, ring * plane * SLOT_ROWS, wide)
    place = home[:, None] == jnp.arange(strips.shape[1], dtype=jnp.int32)[None, :]
    place = place.astype(bf16)
    placed = [jnp.dot(place, s, preferred_element_type=jnp.float32) for s in strips]
    placed = [placed[0] + placed[1] + placed[2], placed[3], placed[4]]
    mine = adamw(*placed, totals * clip_factor)[0].astype(bf16)
    halves = share(mine, "x")
    others = lax.ppermute(halves, "c", [(0, 1), (1, 0)])
    first_core = lax.axis_index("c") == 0
    pair = [jnp.where(first_core, halves, others), jnp.where(first_core, others, halves)]
    weights = jnp.stack(pair, axis=1).transpose(2, 0, 1, 3).reshape(rows, width)

    own = got.reshape(plane, layers, SLOT_ROWS, wide)
    own = lax.dynamic_index_in_dim(own, lax.axis_index("layer"), 1, keepdims=False)
    own = own[:, :lines].transpose(1, 0, 2).reshape(capacity, slab, width) * clip_factor
    new = adamw(master[0], moment_one[0], moment_two[0], own)
    my_slots = lax.axis_index((RING, *PLANE)) * SLOT_ROWS
    my_slots = my_slots + slab * jnp.arange(capacity, dtype=jnp.int32)
    keep = jnp.any(home[None, :] == my_slots[:, None], axis=1)[:, None, None]
    old = (master[0], moment_one[0], moment_two[0])
    new = [jnp.where(keep, n, o)[None] for n, o in zip(new, old, strict=True)]
    return (*new, weights[None], grad_rms)


def solution(mesh):
    ring = mesh.shape["dp"] // (PLANE_SHAPE[0] * PLANE_SHAPE[1])
    devices = mesh.devices.reshape(ring, *PLANE_SHAPE, mesh.shape["layer"])
    split = Mesh(devices, (RING, *PLANE, "layer"))
    dp = (RING, *PLANE)
    in_specs = (
        P("layer", dp, None, None),
        P("layer", dp, None, None),
        P("layer", dp, None, None),
        P("layer", dp, None, None),
        P("layer", None),
        P("layer", None),
    )
    out_specs = (
        P("layer", dp, None, None),
        P("layer", dp, None, None),
        P("layer", dp, None, None),
        P("layer", None, None),
        P(),
    )
    return jax.shard_map(
        shards, mesh=split, in_specs=in_specs, out_specs=out_specs, check_vma=False
    )
```

```python
import jax
import jax.numpy as jnp
from jax import lax
from jax.experimental import pallas as pl
from jax.experimental.pallas import tpu as pltpu
from jax.sharding import Mesh
from jax.sharding import PartitionSpec as P

beta_one = 0.9
beta_two = 0.95
learn_rate = 0.0003
decay_rate = 0.1
adam_eps = 1e-08
step_number = 100.0

RING = "z"
PLANE = ("x", "c")
PLANE_SHAPE = (4, 2)
SLOT_ROWS = 8
KINDS = 5


def adamw(param, first, second, grad):
    first_new = beta_one * first + (1.0 - beta_one) * grad
    second_new = beta_two * second + (1.0 - beta_two) * grad * grad
    corr_one = 1.0 - beta_one**step_number
    corr_two = 1.0 - beta_two**step_number
    update = (
        first_new / corr_one / (jnp.sqrt(second_new / corr_two) + adam_eps) + decay_rate * param
    )
    return (param - learn_rate * update, first_new, second_new)


def exchange(chunks, axis):
    return lax.all_to_all(chunks, axis, 0, 0, tiled=True)


def share(value, axis):
    copies = jnp.broadcast_to(value[None], (lax.axis_size(axis), *value.shape))
    return exchange(lax.optimization_barrier(copies), axis)


def split_kernel(grads, master, first, second, out, rows):
    plane, _, wide = out.shape
    count = grads.shape[0]
    for k in range(plane):
        out[k, :count, :] = grads[:, k * wide : (k + 1) * wide]
    rows[...] = jnp.zeros_like(rows)
    capacity, slab, _ = master.shape
    for i, state in enumerate((master, first, second)):
        for s in range(capacity):
            rows[i, s * slab : (s + 1) * slab, :] = state[s]
    value = rows[0]
    high = value.astype(jnp.bfloat16)
    rest = value - high.astype(jnp.float32)
    middle = rest.astype(jnp.bfloat16)
    low = (rest - middle.astype(jnp.float32)).astype(jnp.bfloat16)
    terms = (high, middle, low, rows[1].astype(jnp.bfloat16), rows[2].astype(jnp.bfloat16))
    for t, term in enumerate(terms):
        at = count + t * SLOT_ROWS
        for k in range(plane):
            out[k, at : at + SLOT_ROWS, :] = term[:, k * wide : (k + 1) * wide]


def split(grads, master, first, second, plane):
    count, width = grads.shape
    return pl.pallas_call(
        split_kernel,
        out_shape=jax.ShapeDtypeStruct(
            (plane, count + KINDS * SLOT_ROWS, width // plane), grads.dtype
        ),
        in_specs=[pl.BlockSpec(memory_space=pltpu.VMEM)] * 4,
        out_specs=pl.BlockSpec(memory_space=pltpu.VMEM),
        scratch_shapes=[pltpu.VMEM((3, SLOT_ROWS, width), jnp.float32)],
        name="split",
    )(grads, master, first, second)


def join_kernel(core, mine, other, out):
    count, _, wide = mine.shape

    def put(first, second):
        for x in range(count):
            out[:, 2 * x * wide : (2 * x + 1) * wide] = first[x]
            out[:, (2 * x + 1) * wide : (2 * x + 2) * wide] = second[x]

    @pl.when(core[0] == 0)
    def _():
        put(mine, other)

    @pl.when(core[0] == 1)
    def _():
        put(other, mine)


def join(mine, other):
    count, rows, wide = mine.shape
    return pl.pallas_call(
        join_kernel,
        out_shape=jax.ShapeDtypeStruct((rows, 2 * count * wide), mine.dtype),
        in_specs=[
            pl.BlockSpec(memory_space=pltpu.SMEM),
            pl.BlockSpec(memory_space=pltpu.VMEM),
            pl.BlockSpec(memory_space=pltpu.VMEM),
        ],
        out_specs=pl.BlockSpec(memory_space=pltpu.VMEM),
        name="join",
    )(lax.axis_index("c").astype(jnp.int32).reshape(1), mine, other)


def shards(micro_grads, master, moment_one, moment_two, owner, slot):
    rows, width = micro_grads.shape[2:]
    capacity, slab = master.shape[1:3]
    ring = lax.axis_size(RING)
    plane = lax.axis_size(PLANE)
    lines = capacity * slab
    wide = width // plane
    layers = lax.axis_size("layer")
    bf16 = jnp.bfloat16
    home = (owner[0] * SLOT_ROWS + slot[0] * slab)[:, None]
    home = (home + jnp.arange(slab, dtype=jnp.int32)[None, :]).reshape(rows)
    tight = home // SLOT_ROWS * lines + home % SLOT_ROWS

    raw = exchange(split(micro_grads[0, 0], master[0], moment_one[0], moment_two[0], plane), PLANE)
    plane_sum = jnp.sum(raw[:, :rows].astype(jnp.float32), axis=0)
    strips = raw[:, rows:].reshape(plane, KINDS, SLOT_ROWS, wide)[:, :, :lines]
    strips = strips.transpose(1, 0, 2, 3).reshape(KINDS, plane * lines, wide).astype(jnp.float32)

    piece = jnp.sum(exchange(plane_sum.reshape(ring, rows // ring, wide), RING), axis=0)
    totals = share(piece, RING).reshape(rows, wide)

    line = jnp.arange(plane * SLOT_ROWS, dtype=jnp.int32)
    pick = (lax.axis_index(RING) * plane * SLOT_ROWS + line)[:, None] == home[None, :]
    sent = jnp.dot(pick.astype(jnp.float32), totals, precision=lax.Precision.HIGHEST)
    sent = jnp.where((line % SLOT_ROWS == lines)[:, None], jnp.sum(totals * totals), sent)
    sent = jnp.broadcast_to(
        sent.reshape(plane, 1, SLOT_ROWS, wide), (plane, layers, SLOT_ROWS, wide)
    )
    got = exchange(sent.reshape(plane * layers, SLOT_ROWS, wide), (*PLANE, "layer"))
    squares = jnp.sum(got[:, lines, 0])
    grad_rms = jnp.sqrt(squares / (layers * rows * width) + 1e-06)
    clip_factor = jnp.minimum(1.0, 1.0 / grad_rms)

    line = jnp.arange(plane * lines, dtype=jnp.int32)
    pick = (lax.axis_index(RING) * plane * lines + line)[:, None] == tight[None, :]
    grads = jnp.dot(pick.astype(jnp.float32), totals, precision=lax.Precision.HIGHEST)
    param = strips[0] + strips[1] + strips[2]
    param = adamw(param, strips[3], strips[4], grads * clip_factor)[0].astype(bf16)
    params = share(param, RING).reshape(ring * plane * lines, wide)
    place = tight[:, None] == jnp.arange(params.shape[0], dtype=jnp.int32)[None, :]
    placed = jnp.dot(place.astype(bf16), params, preferred_element_type=jnp.float32)
    halves = share(placed.astype(bf16), "x")
    weights = join(halves, lax.ppermute(halves, "c", [(0, 1), (1, 0)]))

    own = got.reshape(plane, layers, SLOT_ROWS, wide)
    own = lax.dynamic_index_in_dim(own, lax.axis_index("layer"), 1, keepdims=False)
    own = own[:, :lines].transpose(1, 0, 2).reshape(capacity, slab, width) * clip_factor
    new = adamw(master[0], moment_one[0], moment_two[0], own)
    my_slots = lax.axis_index((RING, *PLANE)) * SLOT_ROWS
    my_slots = my_slots + slab * jnp.arange(capacity, dtype=jnp.int32)
    keep = jnp.any(home[None, :] == my_slots[:, None], axis=1)[:, None, None]
    old = (master[0], moment_one[0], moment_two[0])
    new = [jnp.where(keep, n, o)[None] for n, o in zip(new, old, strict=True)]
    return (*new, weights[None], grad_rms)


def solution(mesh):
    ring = mesh.shape["dp"] // (PLANE_SHAPE[0] * PLANE_SHAPE[1])
    devices = mesh.devices.reshape(ring, *PLANE_SHAPE, mesh.shape["layer"])
    split_mesh = Mesh(devices, (RING, *PLANE, "layer"))
    dp = (RING, *PLANE)
    in_specs = (
        P("layer", dp, None, None),
        P("layer", dp, None, None),
        P("layer", dp, None, None),
        P("layer", dp, None, None),
        P("layer", None),
        P("layer", None),
    )
    out_specs = (
        P("layer", dp, None, None),
        P("layer", dp, None, None),
        P("layer", dp, None, None),
        P("layer", None, None),
        P(),
    )
    return jax.shard_map(
        shards, mesh=split_mesh, in_specs=in_specs, out_specs=out_specs, check_vma=False
    )
```

```python
import jax
import jax.numpy as jnp
from jax import lax
from jax.experimental import pallas as pl
from jax.experimental.pallas import tpu as pltpu
from jax.sharding import Mesh
from jax.sharding import PartitionSpec as P

beta_one = 0.9
beta_two = 0.95
learn_rate = 0.0003
decay_rate = 0.1
adam_eps = 1e-08
step_number = 100.0

RING = "z"
PLANE = ("x", "c")
PLANE_SHAPE = (4, 2)
SLOT_ROWS = 8
KINDS = 4


def adamw(param, first, second, grad):
    first_new = beta_one * first + (1.0 - beta_one) * grad
    second_new = beta_two * second + (1.0 - beta_two) * grad * grad
    corr_one = 1.0 - beta_one**step_number
    corr_two = 1.0 - beta_two**step_number
    update = (
        first_new / corr_one / (jnp.sqrt(second_new / corr_two) + adam_eps) + decay_rate * param
    )
    return (param - learn_rate * update, first_new, second_new)


def exchange(chunks, axis):
    return lax.all_to_all(chunks, axis, 0, 0, tiled=True)


def two_terms(value):
    high = value.astype(jnp.bfloat16)
    return high, (value - high.astype(jnp.float32)).astype(jnp.bfloat16)


def choose(matrix, values):
    return jnp.dot(matrix, values, preferred_element_type=jnp.float32)


VMEM = pl.BlockSpec(memory_space=pltpu.VMEM)


def split_kernel(grads, master, first, second, out, rows):
    plane, _, wide = out.shape
    count = grads.shape[0]
    for k in range(plane):
        out[k, :count, :] = grads[:, k * wide : (k + 1) * wide]
    rows[...] = jnp.zeros_like(rows)
    capacity, slab, _ = master.shape
    for i, state in enumerate((master, first, second)):
        for s in range(capacity):
            rows[i, s * slab : (s + 1) * slab, :] = state[s]
    high, low = two_terms(rows[0])
    terms = (high, low, rows[1].astype(jnp.bfloat16), rows[2].astype(jnp.bfloat16))
    for t, term in enumerate(terms):
        at = count + t * SLOT_ROWS
        for k in range(plane):
            out[k, at : at + SLOT_ROWS, :] = term[:, k * wide : (k + 1) * wide]


def split(grads, master, first, second, plane):
    count, width = grads.shape
    return pl.pallas_call(
        split_kernel,
        out_shape=jax.ShapeDtypeStruct(
            (plane, count + KINDS * SLOT_ROWS, width // plane), grads.dtype
        ),
        in_specs=[pl.BlockSpec(memory_space=pltpu.VMEM)] * 4,
        out_specs=pl.BlockSpec(memory_space=pltpu.VMEM),
        scratch_shapes=[pltpu.VMEM((3, SLOT_ROWS, width), jnp.float32)],
        name="split",
    )(grads, master, first, second)


def join_kernel(core, mine, other, out):
    count, _, wide = mine.shape

    def put(first, second):
        for x in range(count):
            out[:, 2 * x * wide : (2 * x + 1) * wide] = first[x]
            out[:, (2 * x + 1) * wide : (2 * x + 2) * wide] = second[x]

    @pl.when(core[0] == 0)
    def _():
        put(mine, other)

    @pl.when(core[0] == 1)
    def _():
        put(other, mine)


def join(mine, other):
    count, rows, wide = mine.shape
    return pl.pallas_call(
        join_kernel,
        out_shape=jax.ShapeDtypeStruct((rows, 2 * count * wide), mine.dtype),
        in_specs=[
            pl.BlockSpec(memory_space=pltpu.SMEM),
            pl.BlockSpec(memory_space=pltpu.VMEM),
            pl.BlockSpec(memory_space=pltpu.VMEM),
        ],
        out_specs=pl.BlockSpec(memory_space=pltpu.VMEM),
        name="join",
    )(lax.axis_index("c").astype(jnp.int32).reshape(1), mine, other)


def pack_kernel(raw, order, route, out):
    plane, count, _ = raw.shape
    ring = out.shape[0]
    rows = order.shape[0]
    part = rows // ring
    total = raw[0, :rows, :].astype(jnp.float32)
    for j in range(1, plane):
        total = total + raw[j, :rows, :].astype(jnp.float32)
    lines = [
        raw[j, at : at + SLOT_ROWS, :] for at in range(rows, count, SLOT_ROWS) for j in range(plane)
    ]
    high, low = two_terms(total)
    sources = ((order, high), (order, low), (route, jnp.concatenate(lines, axis=0)))
    for i, (matrix, source) in enumerate(sources):
        chosen = choose(matrix[...], source).astype(out.dtype)
        for z in range(ring):
            out[z, i * part : (i + 1) * part, :] = chosen[z * part : (z + 1) * part, :]


def reduce_kernel(got, take, out):
    ring, count, _ = got.shape
    part = count // 3
    total = got[0, :part, :].astype(jnp.float32) + got[0, part : 2 * part, :].astype(jnp.float32)
    for z in range(1, ring):
        total = total + (
            got[z, :part, :].astype(jnp.float32) + got[z, part : 2 * part, :].astype(jnp.float32)
        )
    high, low = two_terms(total)
    out[:part, :] = high
    out[part : 2 * part, :] = low
    lines = jnp.concatenate([got[z, 2 * part :, :] for z in range(ring)], axis=0)
    out[2 * part :, :] = choose(take[...], lines).astype(out.dtype)


def ordered(every, term, part):
    return jnp.concatenate(
        [every[z, term * part : (term + 1) * part, :] for z in range(every.shape[0])], axis=0
    )


def send_kernel(every, pick, out):
    plane, layers, _, wide = out.shape
    part = pick.shape[1] // every.shape[0]
    high, low = ordered(every, 0, part), ordered(every, 1, part)
    total = high.astype(jnp.float32) + low.astype(jnp.float32)
    squares = jnp.sum(total * total)
    sent = choose(pick[...], high) + choose(pick[...], low)
    line = lax.broadcasted_iota(jnp.int32, sent.shape, 0)
    sent = jnp.where(line % SLOT_ROWS == SLOT_ROWS - 1, squares, sent)
    for j in range(plane):
        for layer in range(layers):
            out[j, layer] = sent[j * SLOT_ROWS : (j + 1) * SLOT_ROWS, :]


def step_kernel(element_total, every, got, place, copies, rms):
    part = place.shape[1] // every.shape[0]
    squares = jnp.sum(got[...], axis=0)[SLOT_ROWS - 1 :, :]
    grad_rms = jnp.sqrt(squares / element_total + 1e-06)
    rms[...] = grad_rms
    clip_factor = jnp.minimum(1.0, 1.0 / grad_rms)
    terms = [ordered(every, t, part).astype(jnp.float32) for t in range(2 + KINDS)]
    grad = (terms[0] + terms[1]) * clip_factor
    param = adamw(terms[2] + terms[3], terms[4], terms[5], grad)[0]
    weights = choose(place[...], param.astype(copies.dtype)).astype(copies.dtype)
    for x in range(copies.shape[0]):
        copies[x] = weights


def shards(micro_grads, master, moment_one, moment_two, owner, slot):
    rows, width = micro_grads.shape[2:]
    capacity, slab = master.shape[1:3]
    ring = lax.axis_size(RING)
    plane = lax.axis_size(PLANE)
    lines = capacity * slab
    wide = width // plane
    layers = lax.axis_size("layer")
    my_z = lax.axis_index(RING)
    part = rows // ring
    plane_lines = plane * SLOT_ROWS
    bf16, f32, i32 = jnp.bfloat16, jnp.float32, jnp.int32
    count = jnp.arange(rows, dtype=i32)
    few = jnp.arange(plane_lines, dtype=i32)

    home = owner[0] * capacity + slot[0]
    rank = jnp.sum((home[None, :] < home[:, None]).astype(i32), axis=1)
    line = owner[0] * SLOT_ROWS + slot[0] * slab
    member, turn = rank % ring, rank // ring

    def per_row(value):
        return (value[:, None] + jnp.arange(slab, dtype=i32)[None, :]).reshape(rows)

    line_of = per_row(line)
    dealt = per_row(member * part + turn * slab)
    pair_of = per_row(member * 2 * slab + turn % 2 * slab)
    order = dealt[None, :] == count[:, None]
    place = dealt[:, None] == count[None, :]
    line_at = jnp.sum(jnp.where(order, line_of[None, :], 0), axis=1)
    pick = (my_z * plane_lines + few)[:, None] == line_at[None, :]
    mine = line_of[None, :] == (my_z * plane_lines + few)[:, None]
    pair_at = jnp.sum(jnp.where(mine, pair_of[None, :] + 1, 0), axis=1) - 1
    kind = jnp.arange(KINDS, dtype=i32)[:, None]
    goes = jnp.where(pair_at < 0, -1, pair_at)[None, :]
    goes = jnp.where(goes < 0, -1, goes // (2 * slab) * part + kind * 2 * slab + goes % (2 * slab))
    route = goes.reshape(1, KINDS * plane_lines) == count[:, None]
    own_line = lax.dynamic_slice_in_dim(line_at, my_z * part, part)
    within = jnp.arange(part, dtype=i32) % (2 * slab)
    comes = (own_line // plane_lines * part + within)[None, :] + kind * 2 * slab
    take = comes.reshape(KINDS * part, 1) == count[None, :]

    raw = exchange(split(micro_grads[0, 0], master[0], moment_one[0], moment_two[0], plane), PLANE)
    packed = pl.pallas_call(
        pack_kernel,
        out_shape=jax.ShapeDtypeStruct((ring, 3 * part, wide), bf16),
        in_specs=[VMEM] * 3,
        out_specs=VMEM,
        name="pack",
    )(raw, order.astype(bf16), route.astype(bf16))
    reduced = pl.pallas_call(
        reduce_kernel,
        out_shape=jax.ShapeDtypeStruct(((2 + KINDS) * part, wide), bf16),
        in_specs=[VMEM] * 2,
        out_specs=VMEM,
        name="reduce",
    )(exchange(packed, RING), take.astype(bf16))
    every = lax.all_gather(reduced, RING, axis=0, tiled=False)

    sent = pl.pallas_call(
        send_kernel,
        out_shape=jax.ShapeDtypeStruct((plane, layers, SLOT_ROWS, wide), f32),
        in_specs=[VMEM] * 2,
        out_specs=VMEM,
        name="send",
    )(every, pick.astype(bf16))
    got = exchange(sent.reshape(plane * layers, SLOT_ROWS, wide), (*PLANE, "layer"))

    copies, rms = pl.pallas_call(
        lambda *refs: step_kernel(float(layers * rows * width), *refs),
        out_shape=(
            jax.ShapeDtypeStruct((lax.axis_size("x"), rows, wide), bf16),
            jax.ShapeDtypeStruct((1, wide), f32),
        ),
        in_specs=[VMEM] * 3,
        out_specs=(VMEM, VMEM),
        name="step",
    )(every, got, place.astype(bf16))
    halves = exchange(copies, "x")
    weights = join(halves, lax.ppermute(halves, "c", [(0, 1), (1, 0)]))
    grad_rms = rms[0, 0]
    clip_factor = jnp.minimum(1.0, 1.0 / grad_rms)

    own = got.reshape(plane, layers, SLOT_ROWS, wide)
    own = lax.dynamic_index_in_dim(own, lax.axis_index("layer"), 1, keepdims=False)
    own = own[:, :lines].transpose(1, 0, 2).reshape(capacity, slab, width) * clip_factor
    new = adamw(master[0], moment_one[0], moment_two[0], own)
    my_slots = lax.axis_index((RING, *PLANE)) * SLOT_ROWS
    my_slots = my_slots + slab * jnp.arange(capacity, dtype=i32)
    keep = jnp.any(line[None, :] == my_slots[:, None], axis=1)[:, None, None]
    old = (master[0], moment_one[0], moment_two[0])
    new = [jnp.where(keep, n, o)[None] for n, o in zip(new, old, strict=True)]
    return (*new, weights[None], grad_rms)


def solution(mesh):
    ring = mesh.shape["dp"] // (PLANE_SHAPE[0] * PLANE_SHAPE[1])
    devices = mesh.devices.reshape(ring, *PLANE_SHAPE, mesh.shape["layer"])
    split_mesh = Mesh(devices, (RING, *PLANE, "layer"))
    dp = (RING, *PLANE)
    in_specs = (
        P("layer", dp, None, None),
        P("layer", dp, None, None),
        P("layer", dp, None, None),
        P("layer", dp, None, None),
        P("layer", None),
        P("layer", None),
    )
    out_specs = (
        P("layer", dp, None, None),
        P("layer", dp, None, None),
        P("layer", dp, None, None),
        P("layer", None, None),
        P(),
    )
    return jax.shard_map(
        shards, mesh=split_mesh, in_specs=in_specs, out_specs=out_specs, check_vma=False
    )
```

```python
import jax
import jax.numpy as jnp
from jax import lax
from jax.experimental import pallas as pl
from jax.experimental.pallas import tpu as pltpu
from jax.sharding import Mesh
from jax.sharding import PartitionSpec as P

beta_one = 0.9
beta_two = 0.95
learn_rate = 0.0003
decay_rate = 0.1
adam_eps = 1e-08
step_number = 100.0

RING = "z"
PLANE = ("x", "c")
PLANE_SHAPE = (4, 2)
SLOT_ROWS = 8
KINDS = 4


def adamw(param, first, second, grad):
    first_new = beta_one * first + (1.0 - beta_one) * grad
    second_new = beta_two * second + (1.0 - beta_two) * grad * grad
    corr_one = 1.0 - beta_one**step_number
    corr_two = 1.0 - beta_two**step_number
    update = (
        first_new / corr_one / (jnp.sqrt(second_new / corr_two) + adam_eps) + decay_rate * param
    )
    return (param - learn_rate * update, first_new, second_new)


def exchange(chunks, axis):
    return lax.all_to_all(chunks, axis, 0, 0, tiled=True)


def two_terms(value):
    high = value.astype(jnp.bfloat16)
    return high, (value - high.astype(jnp.float32)).astype(jnp.bfloat16)


def choose(matrix, values):
    return jnp.dot(matrix, values, preferred_element_type=jnp.float32)


VMEM = pl.BlockSpec(memory_space=pltpu.VMEM)


def near(value):
    return pltpu.with_memory_space_constraint(value, pltpu.VMEM)


def split_kernel(grads, master, first, second, out, rows):
    plane, _, wide = out.shape
    count = grads.shape[0]
    for k in range(plane):
        out[k, :count, :] = grads[:, k * wide : (k + 1) * wide]
    rows[...] = jnp.zeros_like(rows)
    capacity, slab, _ = master.shape
    for i, state in enumerate((master, first, second)):
        for s in range(capacity):
            rows[i, s * slab : (s + 1) * slab, :] = state[s]
    high, low = two_terms(rows[0])
    terms = (high, low, rows[1].astype(jnp.bfloat16), rows[2].astype(jnp.bfloat16))
    for t, term in enumerate(terms):
        at = count + t * SLOT_ROWS
        for k in range(plane):
            out[k, at : at + SLOT_ROWS, :] = term[:, k * wide : (k + 1) * wide]


def split(grads, master, first, second, plane):
    count, width = grads.shape
    return pl.pallas_call(
        split_kernel,
        out_shape=pltpu.VMEM((plane, count + KINDS * SLOT_ROWS, width // plane), grads.dtype),
        in_specs=[pl.BlockSpec(memory_space=pltpu.VMEM)] * 4,
        out_specs=pl.BlockSpec(memory_space=pltpu.VMEM),
        scratch_shapes=[pltpu.VMEM((3, SLOT_ROWS, width), jnp.float32)],
        name="split",
    )(grads, master, first, second)


def join_kernel(core, mine, other, out):
    count, _, wide = mine.shape

    def put(first, second):
        for x in range(count):
            out[:, 2 * x * wide : (2 * x + 1) * wide] = first[x]
            out[:, (2 * x + 1) * wide : (2 * x + 2) * wide] = second[x]

    @pl.when(core[0] == 0)
    def _():
        put(mine, other)

    @pl.when(core[0] == 1)
    def _():
        put(other, mine)


def join(mine, other):
    count, rows, wide = mine.shape
    return pl.pallas_call(
        join_kernel,
        out_shape=jax.ShapeDtypeStruct((rows, 2 * count * wide), mine.dtype),
        in_specs=[
            pl.BlockSpec(memory_space=pltpu.SMEM),
            pl.BlockSpec(memory_space=pltpu.VMEM),
            pl.BlockSpec(memory_space=pltpu.VMEM),
        ],
        out_specs=pl.BlockSpec(memory_space=pltpu.VMEM),
        name="join",
    )(lax.axis_index("c").astype(jnp.int32).reshape(1), near(mine), near(other))


def pack_kernel(raw, order, route, out):
    plane, count, _ = raw.shape
    ring = out.shape[0]
    rows = order.shape[0]
    part = rows // ring
    total = raw[0, :rows, :].astype(jnp.float32)
    for j in range(1, plane):
        total = total + raw[j, :rows, :].astype(jnp.float32)
    lines = [
        raw[j, at : at + SLOT_ROWS, :] for at in range(rows, count, SLOT_ROWS) for j in range(plane)
    ]
    high, low = two_terms(total)
    sources = ((order, high), (order, low), (route, jnp.concatenate(lines, axis=0)))
    for i, (matrix, source) in enumerate(sources):
        chosen = choose(matrix[...], source).astype(out.dtype)
        for z in range(ring):
            out[z, i * part : (i + 1) * part, :] = chosen[z * part : (z + 1) * part, :]


def reduce_kernel(got, take, out):
    ring, count, _ = got.shape
    part = count // 3
    total = got[0, :part, :].astype(jnp.float32) + got[0, part : 2 * part, :].astype(jnp.float32)
    for z in range(1, ring):
        total = total + (
            got[z, :part, :].astype(jnp.float32) + got[z, part : 2 * part, :].astype(jnp.float32)
        )
    high, low = two_terms(total)
    out[:part, :] = high
    out[part : 2 * part, :] = low
    lines = jnp.concatenate([got[z, 2 * part :, :] for z in range(ring)], axis=0)
    out[2 * part :, :] = choose(take[...], lines).astype(out.dtype)


def ordered(every, term, part):
    return jnp.concatenate(
        [every[z, term * part : (term + 1) * part, :] for z in range(every.shape[0])], axis=0
    )


def send_kernel(every, pick, out):
    plane, layers, _, wide = out.shape
    part = pick.shape[1] // every.shape[0]
    high, low = ordered(every, 0, part), ordered(every, 1, part)
    total = high.astype(jnp.float32) + low.astype(jnp.float32)
    squares = jnp.sum(total * total)
    sent = choose(pick[...], high) + choose(pick[...], low)
    line = lax.broadcasted_iota(jnp.int32, sent.shape, 0)
    sent = jnp.where(line % SLOT_ROWS == SLOT_ROWS - 1, squares, sent)
    for j in range(plane):
        for layer in range(layers):
            out[j, layer] = sent[j * SLOT_ROWS : (j + 1) * SLOT_ROWS, :]


def step_kernel(element_total, every, got, place, copies, rms):
    part = place.shape[1] // every.shape[0]
    squares = jnp.sum(got[...], axis=0)[SLOT_ROWS - 1 :, :]
    grad_rms = jnp.sqrt(squares / element_total + 1e-06)
    rms[...] = grad_rms
    clip_factor = jnp.minimum(1.0, 1.0 / grad_rms)
    terms = [ordered(every, t, part).astype(jnp.float32) for t in range(2 + KINDS)]
    grad = (terms[0] + terms[1]) * clip_factor
    param = adamw(terms[2] + terms[3], terms[4], terms[5], grad)[0]
    weights = choose(place[...], param.astype(copies.dtype)).astype(copies.dtype)
    for x in range(copies.shape[0]):
        copies[x] = weights


def shards(micro_grads, master, moment_one, moment_two, owner, slot):
    rows, width = micro_grads.shape[2:]
    capacity, slab = master.shape[1:3]
    ring = lax.axis_size(RING)
    plane = lax.axis_size(PLANE)
    lines = capacity * slab
    wide = width // plane
    layers = lax.axis_size("layer")
    my_z = lax.axis_index(RING)
    part = rows // ring
    plane_lines = plane * SLOT_ROWS
    bf16, f32, i32 = jnp.bfloat16, jnp.float32, jnp.int32
    count = jnp.arange(rows, dtype=i32)
    few = jnp.arange(plane_lines, dtype=i32)

    home = owner[0] * capacity + slot[0]
    rank = jnp.sum((home[None, :] < home[:, None]).astype(i32), axis=1)
    line = owner[0] * SLOT_ROWS + slot[0] * slab
    member, turn = rank % ring, rank // ring

    def per_row(value):
        return (value[:, None] + jnp.arange(slab, dtype=i32)[None, :]).reshape(rows)

    line_of = per_row(line)
    dealt = per_row(member * part + turn * slab)
    pair_of = per_row(member * 2 * slab + turn % 2 * slab)
    order = dealt[None, :] == count[:, None]
    place = dealt[:, None] == count[None, :]
    line_at = jnp.sum(jnp.where(order, line_of[None, :], 0), axis=1)
    pick = (my_z * plane_lines + few)[:, None] == line_at[None, :]
    mine = line_of[None, :] == (my_z * plane_lines + few)[:, None]
    pair_at = jnp.sum(jnp.where(mine, pair_of[None, :] + 1, 0), axis=1) - 1
    kind = jnp.arange(KINDS, dtype=i32)[:, None]
    goes = jnp.where(pair_at < 0, -1, pair_at)[None, :]
    goes = jnp.where(goes < 0, -1, goes // (2 * slab) * part + kind * 2 * slab + goes % (2 * slab))
    route = goes.reshape(1, KINDS * plane_lines) == count[:, None]
    own_line = lax.dynamic_slice_in_dim(line_at, my_z * part, part)
    within = jnp.arange(part, dtype=i32) % (2 * slab)
    comes = (own_line // plane_lines * part + within)[None, :] + kind * 2 * slab
    take = comes.reshape(KINDS * part, 1) == count[None, :]

    raw = exchange(split(micro_grads[0, 0], master[0], moment_one[0], moment_two[0], plane), PLANE)
    packed = pl.pallas_call(
        pack_kernel,
        out_shape=pltpu.VMEM((ring, 3 * part, wide), bf16),
        in_specs=[VMEM] * 3,
        out_specs=VMEM,
        name="pack",
    )(near(raw), near(order.astype(bf16)), near(route.astype(bf16)))
    reduced = pl.pallas_call(
        reduce_kernel,
        out_shape=pltpu.VMEM(((2 + KINDS) * part, wide), bf16),
        in_specs=[VMEM] * 2,
        out_specs=VMEM,
        name="reduce",
    )(near(exchange(packed, RING)), near(take.astype(bf16)))
    every = lax.all_gather(reduced, RING, axis=0, tiled=False)

    sent = pl.pallas_call(
        send_kernel,
        out_shape=pltpu.VMEM((plane, layers, SLOT_ROWS, wide), f32),
        in_specs=[VMEM] * 2,
        out_specs=VMEM,
        name="send",
    )(near(every), near(pick.astype(bf16)))
    got = exchange(sent.reshape(plane * layers, SLOT_ROWS, wide), (*PLANE, "layer"))

    copies, rms = pl.pallas_call(
        lambda *refs: step_kernel(float(layers * rows * width), *refs),
        out_shape=(
            pltpu.VMEM((lax.axis_size("x"), rows, wide), bf16),
            jax.ShapeDtypeStruct((1, wide), f32),
        ),
        in_specs=[VMEM] * 3,
        out_specs=(VMEM, VMEM),
        name="step",
    )(near(every), near(got), near(place.astype(bf16)))
    halves = exchange(copies, "x")
    weights = join(halves, lax.ppermute(halves, "c", [(0, 1), (1, 0)]))
    grad_rms = rms[0, 0]
    clip_factor = jnp.minimum(1.0, 1.0 / grad_rms)

    own = got.reshape(plane, layers, SLOT_ROWS, wide)
    own = lax.dynamic_index_in_dim(own, lax.axis_index("layer"), 1, keepdims=False)
    own = own[:, :lines].transpose(1, 0, 2).reshape(capacity, slab, width) * clip_factor
    new = adamw(master[0], moment_one[0], moment_two[0], own)
    my_slots = lax.axis_index((RING, *PLANE)) * SLOT_ROWS
    my_slots = my_slots + slab * jnp.arange(capacity, dtype=i32)
    keep = jnp.any(line[None, :] == my_slots[:, None], axis=1)[:, None, None]
    old = (master[0], moment_one[0], moment_two[0])
    new = [jnp.where(keep, n, o)[None] for n, o in zip(new, old, strict=True)]
    return (*new, weights[None], grad_rms)


def solution(mesh):
    ring = mesh.shape["dp"] // (PLANE_SHAPE[0] * PLANE_SHAPE[1])
    devices = mesh.devices.reshape(ring, *PLANE_SHAPE, mesh.shape["layer"])
    split_mesh = Mesh(devices, (RING, *PLANE, "layer"))
    dp = (RING, *PLANE)
    in_specs = (
        P("layer", dp, None, None),
        P("layer", dp, None, None),
        P("layer", dp, None, None),
        P("layer", dp, None, None),
        P("layer", None),
        P("layer", None),
    )
    out_specs = (
        P("layer", dp, None, None),
        P("layer", dp, None, None),
        P("layer", dp, None, None),
        P("layer", None, None),
        P(),
    )
    return jax.shard_map(
        shards, mesh=split_mesh, in_specs=in_specs, out_specs=out_specs, check_vma=False
    )
```

```python
import math

import jax
import jax.numpy as jnp
from jax import lax
from jax.experimental import pallas as pl
from jax.experimental.pallas import tpu as pltpu
from jax.sharding import Mesh
from jax.sharding import PartitionSpec as P

beta_one = 0.9
beta_two = 0.95
learn_rate = 0.0003
decay_rate = 0.1
adam_eps = 1e-08
step_number = 100.0

RING = "z"
PLANE = ("pair", "x", "c")
PLANE_SHAPE = (2, 4, 2)
HALF = ("pair", "x")
SLOT_ROWS = 8
KINDS = 4


def adamw(param, first, second, grad):
    first_new = beta_one * first + (1.0 - beta_one) * grad
    second_new = beta_two * second + (1.0 - beta_two) * grad * grad
    corr_one = 1.0 - beta_one**step_number
    corr_two = 1.0 - beta_two**step_number
    update = (
        first_new / corr_one / (jnp.sqrt(second_new / corr_two) + adam_eps) + decay_rate * param
    )
    return (param - learn_rate * update, first_new, second_new)


def exchange(chunks, axis):
    return lax.all_to_all(chunks, axis, 0, 0, tiled=True)


def two_terms(value):
    high = value.astype(jnp.bfloat16)
    return high, (value - high.astype(jnp.float32)).astype(jnp.bfloat16)


def choose(matrix, values):
    return jnp.dot(matrix, values, preferred_element_type=jnp.float32)


VMEM = pl.BlockSpec(memory_space=pltpu.VMEM)


def near(value):
    return pltpu.with_memory_space_constraint(value, pltpu.VMEM)


def split_kernel(grads, master, first, second, out, rows):
    plane, _, wide = out.shape
    count = grads.shape[0]
    for k in range(plane):
        out[k, :count, :] = grads[:, k * wide : (k + 1) * wide]
    rows[...] = jnp.zeros_like(rows)
    capacity, slab, _ = master.shape
    for i, state in enumerate((master, first, second)):
        for s in range(capacity):
            rows[i, s * slab : (s + 1) * slab, :] = state[s]
    high, low = two_terms(rows[0])
    terms = (high, low, rows[1].astype(jnp.bfloat16), rows[2].astype(jnp.bfloat16))
    for t, term in enumerate(terms):
        at = count + t * SLOT_ROWS
        for k in range(plane):
            out[k, at : at + SLOT_ROWS, :] = term[:, k * wide : (k + 1) * wide]


def split(grads, master, first, second, plane):
    count, width = grads.shape
    return pl.pallas_call(
        split_kernel,
        out_shape=pltpu.VMEM((plane, count + KINDS * SLOT_ROWS, width // plane), grads.dtype),
        in_specs=[pl.BlockSpec(memory_space=pltpu.VMEM)] * 4,
        out_specs=pl.BlockSpec(memory_space=pltpu.VMEM),
        scratch_shapes=[pltpu.VMEM((3, SLOT_ROWS, width), jnp.float32)],
        name="split",
    )(grads, master, first, second)


def join_kernel(core, mine, other, out):
    count, _, wide = mine.shape

    def put(first, second):
        for x in range(count):
            out[:, 2 * x * wide : (2 * x + 1) * wide] = first[x]
            out[:, (2 * x + 1) * wide : (2 * x + 2) * wide] = second[x]

    @pl.when(core[0] == 0)
    def _():
        put(mine, other)

    @pl.when(core[0] == 1)
    def _():
        put(other, mine)


def join(mine, other):
    count, rows, wide = mine.shape
    return pl.pallas_call(
        join_kernel,
        out_shape=jax.ShapeDtypeStruct((rows, 2 * count * wide), mine.dtype),
        in_specs=[
            pl.BlockSpec(memory_space=pltpu.SMEM),
            pl.BlockSpec(memory_space=pltpu.VMEM),
            pl.BlockSpec(memory_space=pltpu.VMEM),
        ],
        out_specs=pl.BlockSpec(memory_space=pltpu.VMEM),
        name="join",
    )(lax.axis_index("c").astype(jnp.int32).reshape(1), near(mine), near(other))


def pack_kernel(raw, order, route, out):
    plane, count, _ = raw.shape
    ring = out.shape[0]
    rows = order.shape[0]
    part = rows // ring
    total = raw[0, :rows, :].astype(jnp.float32)
    for j in range(1, plane):
        total = total + raw[j, :rows, :].astype(jnp.float32)
    lines = [
        raw[j, at : at + SLOT_ROWS, :] for at in range(rows, count, SLOT_ROWS) for j in range(plane)
    ]
    high, low = two_terms(total)
    sources = ((order, high), (order, low), (route, jnp.concatenate(lines, axis=0)))
    for i, (matrix, source) in enumerate(sources):
        chosen = choose(matrix[...], source).astype(out.dtype)
        size = chosen.shape[0] // ring
        for z in range(ring):
            out[z, i * part : i * part + size, :] = chosen[z * size : (z + 1) * size, :]


def reduce_kernel(got, take, out):
    ring = got.shape[0]
    part = out.shape[1] // (2 + KINDS)
    total = got[0, :part, :].astype(jnp.float32) + got[0, part : 2 * part, :].astype(jnp.float32)
    for z in range(1, ring):
        total = total + (
            got[z, :part, :].astype(jnp.float32) + got[z, part : 2 * part, :].astype(jnp.float32)
        )
    high, low = two_terms(total)
    lines = jnp.concatenate([got[z, 2 * part :, :] for z in range(ring)], axis=0)
    lines = choose(take[...], lines).astype(out.dtype)
    for z in range(ring):
        out[z, :part, :] = high
        out[z, part : 2 * part, :] = low
        out[z, 2 * part :, :] = lines


def ordered(every, term, part):
    return jnp.concatenate(
        [every[z, term * part : (term + 1) * part, :] for z in range(every.shape[0])], axis=0
    )


def send_kernel(every, pick, out):
    plane, layers, _, wide = out.shape
    part = pick.shape[1] // every.shape[0]
    high, low = ordered(every, 0, part), ordered(every, 1, part)
    total = high.astype(jnp.float32) + low.astype(jnp.float32)
    squares = jnp.sum(total * total)
    sent = choose(pick[...], high) + choose(pick[...], low)
    line = lax.broadcasted_iota(jnp.int32, sent.shape, 0)
    sent = jnp.where(line % SLOT_ROWS == SLOT_ROWS - 1, squares, sent)
    for j in range(plane):
        for layer in range(layers):
            out[j, layer] = sent[j * SLOT_ROWS : (j + 1) * SLOT_ROWS, :]


def step_kernel(element_total, every, got, place, copies, rms):
    part = place.shape[1] // every.shape[0]
    squares = jnp.sum(got[...], axis=0)[SLOT_ROWS - 1 :, :]
    grad_rms = jnp.sqrt(squares / element_total + 1e-06)
    rms[...] = grad_rms
    clip_factor = jnp.minimum(1.0, 1.0 / grad_rms)
    terms = [ordered(every, t, part).astype(jnp.float32) for t in range(2 + KINDS)]
    grad = (terms[0] + terms[1]) * clip_factor
    param = adamw(terms[2] + terms[3], terms[4], terms[5], grad)[0]
    weights = choose(place[...], param.astype(copies.dtype)).astype(copies.dtype)
    for x in range(copies.shape[0]):
        copies[x] = weights


def shards(micro_grads, master, moment_one, moment_two, owner, slot):
    rows, width = micro_grads.shape[2:]
    capacity, slab = master.shape[1:3]
    ring = lax.axis_size(RING)
    plane = lax.axis_size(PLANE)
    lines = capacity * slab
    wide = width // plane
    layers = lax.axis_size("layer")
    my_z = lax.axis_index(RING)
    part = rows // ring
    plane_lines = plane * SLOT_ROWS
    bf16, f32, i32 = jnp.bfloat16, jnp.float32, jnp.int32
    count = jnp.arange(rows, dtype=i32)
    few = jnp.arange(plane_lines, dtype=i32)

    deal = -(-plane * capacity // ring)
    pair = deal * slab
    home = owner[0] * capacity + slot[0]
    rank = jnp.sum((home[None, :] < home[:, None]).astype(i32), axis=1)
    line = owner[0] * SLOT_ROWS + slot[0] * slab
    member, turn = rank % ring, rank // ring

    def per_row(value):
        return (value[:, None] + jnp.arange(slab, dtype=i32)[None, :]).reshape(rows)

    line_of = per_row(line)
    dealt = per_row(member * part + turn * slab)
    pair_of = per_row(member * pair + turn % deal * slab)
    order = dealt[None, :] == count[:, None]
    place = dealt[:, None] == count[None, :]
    line_at = jnp.sum(jnp.where(order, line_of[None, :], 0), axis=1)
    pick = (my_z * plane_lines + few)[:, None] == line_at[None, :]
    mine = line_of[None, :] == (my_z * plane_lines + few)[:, None]
    pair_at = jnp.sum(jnp.where(mine, pair_of[None, :] + 1, 0), axis=1) - 1
    kind = jnp.arange(KINDS, dtype=i32)[:, None]
    goes = jnp.where(pair_at < 0, -1, pair_at)[None, :]
    goes = jnp.where(goes < 0, -1, (goes // pair * KINDS + kind) * pair + goes % pair)
    chunks = jnp.arange(ring * KINDS * pair, dtype=i32)
    route = goes.reshape(1, KINDS * plane_lines) == chunks[:, None]
    own_line = lax.dynamic_slice_in_dim(line_at, my_z * part, part)
    within = jnp.arange(part, dtype=i32) % pair
    comes = (own_line // plane_lines * KINDS + kind) * pair + within[None, :]
    take = comes.reshape(KINDS * part, 1) == chunks[None, :]

    raw = exchange(split(micro_grads[0, 0], master[0], moment_one[0], moment_two[0], plane), PLANE)
    packed = pl.pallas_call(
        pack_kernel,
        out_shape=pltpu.VMEM((ring, 2 * part + KINDS * pair, wide), bf16),
        in_specs=[VMEM] * 3,
        out_specs=VMEM,
        name="pack",
    )(near(raw), near(order.astype(bf16)), near(route.astype(bf16)))
    reduced = pl.pallas_call(
        reduce_kernel,
        out_shape=pltpu.VMEM((ring, (2 + KINDS) * part, wide), bf16),
        in_specs=[VMEM] * 2,
        out_specs=VMEM,
        name="reduce",
    )(near(exchange(packed, RING)), near(take.astype(bf16)))
    every = exchange(reduced, RING)

    sent = pl.pallas_call(
        send_kernel,
        out_shape=pltpu.VMEM((plane, layers, SLOT_ROWS, wide), f32),
        in_specs=[VMEM] * 2,
        out_specs=VMEM,
        name="send",
    )(near(every), near(pick.astype(bf16)))
    got = exchange(sent.reshape(plane * layers, SLOT_ROWS, wide), (*PLANE, "layer"))

    copies, rms = pl.pallas_call(
        lambda *refs: step_kernel(float(layers * rows * width), *refs),
        out_shape=(
            pltpu.VMEM((lax.axis_size(HALF), rows, wide), bf16),
            jax.ShapeDtypeStruct((1, wide), f32),
        ),
        in_specs=[VMEM] * 3,
        out_specs=(VMEM, VMEM),
        name="step",
    )(near(every), near(got), near(place.astype(bf16)))
    halves = exchange(copies, HALF)
    weights = join(halves, lax.ppermute(halves, "c", [(0, 1), (1, 0)]))
    grad_rms = rms[0, 0]
    clip_factor = jnp.minimum(1.0, 1.0 / grad_rms)

    own = got.reshape(plane, layers, SLOT_ROWS, wide)
    own = lax.dynamic_index_in_dim(own, lax.axis_index("layer"), 1, keepdims=False)
    own = own[:, :lines].transpose(1, 0, 2).reshape(capacity, slab, width) * clip_factor
    new = adamw(master[0], moment_one[0], moment_two[0], own)
    my_slots = lax.axis_index((RING, *PLANE)) * SLOT_ROWS
    my_slots = my_slots + slab * jnp.arange(capacity, dtype=i32)
    keep = jnp.any(line[None, :] == my_slots[:, None], axis=1)[:, None, None]
    old = (master[0], moment_one[0], moment_two[0])
    new = [jnp.where(keep, n, o)[None] for n, o in zip(new, old, strict=True)]
    return (*new, weights[None], grad_rms)


def solution(mesh):
    ring = mesh.shape["dp"] // math.prod(PLANE_SHAPE)
    devices = mesh.devices.reshape(ring, *PLANE_SHAPE, mesh.shape["layer"])
    split_mesh = Mesh(devices, (RING, *PLANE, "layer"))
    dp = (RING, *PLANE)
    in_specs = (
        P("layer", dp, None, None),
        P("layer", dp, None, None),
        P("layer", dp, None, None),
        P("layer", dp, None, None),
        P("layer", None),
        P("layer", None),
    )
    out_specs = (
        P("layer", dp, None, None),
        P("layer", dp, None, None),
        P("layer", dp, None, None),
        P("layer", None, None),
        P(),
    )
    return jax.shard_map(
        shards, mesh=split_mesh, in_specs=in_specs, out_specs=out_specs, check_vma=False
    )
```

```python
import math

import jax
import jax.numpy as jnp
from jax import lax
from jax.experimental import pallas as pl
from jax.experimental.pallas import tpu as pltpu
from jax.sharding import Mesh
from jax.sharding import PartitionSpec as P

beta_one = 0.9
beta_two = 0.95
learn_rate = 0.0003
decay_rate = 0.1
adam_eps = 1e-08
step_number = 100.0

RING = "z"
PLANE = ("pair", "x", "c")
PLANE_SHAPE = (2, 4, 2)
HALF = ("pair", "x")
SLOT_ROWS = 8
KINDS = 4


def adamw(param, first, second, grad):
    first_new = beta_one * first + (1.0 - beta_one) * grad
    second_new = beta_two * second + (1.0 - beta_two) * grad * grad
    corr_one = 1.0 - beta_one**step_number
    corr_two = 1.0 - beta_two**step_number
    update = (
        first_new / corr_one / (jnp.sqrt(second_new / corr_two) + adam_eps) + decay_rate * param
    )
    return (param - learn_rate * update, first_new, second_new)


def exchange(chunks, axis):
    return lax.all_to_all(chunks, axis, 0, 0, tiled=True)


def two_terms(value):
    high = value.astype(jnp.bfloat16)
    return high, (value - high.astype(jnp.float32)).astype(jnp.bfloat16)


def choose(matrix, values):
    return jnp.dot(matrix, values, preferred_element_type=jnp.float32)


VMEM = pl.BlockSpec(memory_space=pltpu.VMEM)
SMEM = pl.BlockSpec(memory_space=pltpu.SMEM)
ANY = pl.BlockSpec(memory_space=pl.ANY)


def near(value):
    return pltpu.with_memory_space_constraint(value, pltpu.VMEM)


def split_kernel(grads, master, first, second, out, rows, terms, grad_sem, term_sem):
    plane, _, wide = out.shape
    count = grads.shape[0]
    moves = [
        pltpu.make_async_copy(
            grads.at[:, pl.ds(k * wide, wide)], out.at[k, pl.ds(0, count), :], grad_sem.at[k]
        )
        for k in range(plane)
    ]
    for move in moves:
        move.start()
    rows[...] = jnp.zeros_like(rows)
    capacity, slab, _ = master.shape
    for i, state in enumerate((master, first, second)):
        for s in range(capacity):
            rows[i, s * slab : (s + 1) * slab, :] = state[s]
    high, low = two_terms(rows[0])
    values = (high, low, rows[1].astype(jnp.bfloat16), rows[2].astype(jnp.bfloat16))
    for t, value in enumerate(values):
        for k in range(plane):
            at = slice(t * SLOT_ROWS, (t + 1) * SLOT_ROWS)
            terms[k, at, :] = value[:, k * wide : (k + 1) * wide]
    last = pltpu.make_async_copy(terms, out.at[:, pl.ds(count, terms.shape[1]), :], term_sem)
    last.start()
    for move in moves:
        move.wait()
    last.wait()


def split(grads, master, first, second, plane):
    count, width = grads.shape
    wide = width // plane
    return pl.pallas_call(
        split_kernel,
        out_shape=jax.ShapeDtypeStruct((plane, count + KINDS * SLOT_ROWS, wide), grads.dtype),
        in_specs=[ANY, VMEM, VMEM, VMEM],
        out_specs=ANY,
        scratch_shapes=[
            pltpu.VMEM((3, SLOT_ROWS, width), jnp.float32),
            pltpu.VMEM((plane, KINDS * SLOT_ROWS, wide), grads.dtype),
            pltpu.SemaphoreType.DMA((plane,)),
            pltpu.SemaphoreType.DMA,
        ],
        name="split",
    )(grads, master, first, second)


def join_kernel(core, strips, *refs):
    out, sem = refs[-2:]
    count, _, wide = strips.shape
    moves = [
        pltpu.make_async_copy(
            strips.at[i],
            out.at[:, pl.ds(pl.multiple_of((2 * i + core[0]) * wide, wide), wide)],
            sem.at[i],
        )
        for i in range(count)
    ]
    for move in moves:
        move.start()
    for move in moves:
        move.wait()


def join(core, strips, *before):
    count, rows, wide = strips.shape
    return pl.pallas_call(
        join_kernel,
        out_shape=jax.ShapeDtypeStruct((rows, 2 * count * wide), strips.dtype),
        in_specs=[SMEM, VMEM] + [ANY] * len(before),
        out_specs=ANY,
        scratch_shapes=[pltpu.SemaphoreType.DMA((count,))],
        input_output_aliases={2: 0} if before else {},
        name="join",
    )(core.reshape(1), near(strips), *before)


def own_kernel(at, got, rms, master, first, second, *refs):
    outs, rows = refs[:3], refs[3]
    wide = got.shape[2]
    count = rows.shape[1] // wide
    layers = got.shape[0] // count
    for k in range(count):
        rows[:, k * wide : (k + 1) * wide] = got[k * layers + at[0]]
    clip_factor = jnp.minimum(1.0, 1.0 / rms[:, :1])
    capacity, slab, _ = master.shape
    for s in range(capacity):
        old = (master[s], first[s], second[s])
        new = adamw(*old, rows[s * slab : (s + 1) * slab, :] * clip_factor)
        keep = at[1 + s] > 0
        for out, n, o in zip(outs, new, old, strict=True):
            out[s] = jnp.where(keep, n, o)


def pack_kernel(raw, order, route, out):
    plane, count, _ = raw.shape
    ring = out.shape[0]
    rows = order.shape[0]
    part = rows // ring
    total = raw[0, :rows, :].astype(jnp.float32)
    for j in range(1, plane):
        total = total + raw[j, :rows, :].astype(jnp.float32)
    lines = [
        raw[j, at : at + SLOT_ROWS, :] for at in range(rows, count, SLOT_ROWS) for j in range(plane)
    ]
    high, low = two_terms(total)
    sources = ((order, high), (order, low), (route, jnp.concatenate(lines, axis=0)))
    for i, (matrix, source) in enumerate(sources):
        chosen = choose(matrix[...], source).astype(out.dtype)
        size = chosen.shape[0] // ring
        for z in range(ring):
            out[z, i * part : i * part + size, :] = chosen[z * size : (z + 1) * size, :]


def reduce_kernel(got, take, out):
    ring = got.shape[0]
    part = out.shape[1] // (2 + KINDS)
    total = got[0, :part, :].astype(jnp.float32) + got[0, part : 2 * part, :].astype(jnp.float32)
    for z in range(1, ring):
        total = total + (
            got[z, :part, :].astype(jnp.float32) + got[z, part : 2 * part, :].astype(jnp.float32)
        )
    high, low = two_terms(total)
    lines = jnp.concatenate([got[z, 2 * part :, :] for z in range(ring)], axis=0)
    lines = choose(take[...], lines).astype(out.dtype)
    for z in range(ring):
        out[z, :part, :] = high
        out[z, part : 2 * part, :] = low
        out[z, 2 * part :, :] = lines


def ordered(every, term, part):
    return jnp.concatenate(
        [every[z, term * part : (term + 1) * part, :] for z in range(every.shape[0])], axis=0
    )


def send_kernel(every, pick, out):
    plane, layers, _, wide = out.shape
    part = pick.shape[1] // every.shape[0]
    high, low = ordered(every, 0, part), ordered(every, 1, part)
    total = high.astype(jnp.float32) + low.astype(jnp.float32)
    squares = jnp.sum(total * total)
    sent = choose(pick[...], high) + choose(pick[...], low)
    line = lax.broadcasted_iota(jnp.int32, sent.shape, 0)
    sent = jnp.where(line % SLOT_ROWS == SLOT_ROWS - 1, squares, sent)
    for j in range(plane):
        for layer in range(layers):
            out[j, layer] = sent[j * SLOT_ROWS : (j + 1) * SLOT_ROWS, :]


def step_kernel(element_total, every, got, place, copies, rms):
    part = place.shape[1] // every.shape[0]
    squares = jnp.sum(got[...], axis=0)[SLOT_ROWS - 1 :, :]
    grad_rms = jnp.sqrt(squares / element_total + 1e-06)
    rms[...] = grad_rms
    clip_factor = jnp.minimum(1.0, 1.0 / grad_rms)
    terms = [ordered(every, t, part).astype(jnp.float32) for t in range(2 + KINDS)]
    grad = (terms[0] + terms[1]) * clip_factor
    param = adamw(terms[2] + terms[3], terms[4], terms[5], grad)[0]
    weights = choose(place[...], param.astype(copies.dtype)).astype(copies.dtype)
    for x in range(copies.shape[0]):
        copies[x] = weights


def shards(micro_grads, master, moment_one, moment_two, owner, slot):
    rows, width = micro_grads.shape[2:]
    capacity, slab = master.shape[1:3]
    ring = lax.axis_size(RING)
    plane = lax.axis_size(PLANE)
    lines = capacity * slab
    wide = width // plane
    layers = lax.axis_size("layer")
    my_z = lax.axis_index(RING)
    part = rows // ring
    plane_lines = plane * SLOT_ROWS
    bf16, f32, i32 = jnp.bfloat16, jnp.float32, jnp.int32
    count = jnp.arange(rows, dtype=i32)
    few = jnp.arange(plane_lines, dtype=i32)

    deal = -(-plane * capacity // ring)
    pair = deal * slab
    home = owner[0] * capacity + slot[0]
    rank = jnp.sum((home[None, :] < home[:, None]).astype(i32), axis=1)
    line = owner[0] * SLOT_ROWS + slot[0] * slab
    member, turn = rank % ring, rank // ring

    def per_row(value):
        return (value[:, None] + jnp.arange(slab, dtype=i32)[None, :]).reshape(rows)

    line_of = per_row(line)
    dealt = per_row(member * part + turn * slab)
    pair_of = per_row(member * pair + turn % deal * slab)
    order = dealt[None, :] == count[:, None]
    place = dealt[:, None] == count[None, :]
    line_at = jnp.sum(jnp.where(order, line_of[None, :], 0), axis=1)
    pick = (my_z * plane_lines + few)[:, None] == line_at[None, :]
    mine = line_of[None, :] == (my_z * plane_lines + few)[:, None]
    pair_at = jnp.sum(jnp.where(mine, pair_of[None, :] + 1, 0), axis=1) - 1
    kind = jnp.arange(KINDS, dtype=i32)[:, None]
    goes = jnp.where(pair_at < 0, -1, pair_at)[None, :]
    goes = jnp.where(goes < 0, -1, (goes // pair * KINDS + kind) * pair + goes % pair)
    chunks = jnp.arange(ring * KINDS * pair, dtype=i32)
    route = goes.reshape(1, KINDS * plane_lines) == chunks[:, None]
    own_line = lax.dynamic_slice_in_dim(line_at, my_z * part, part)
    within = jnp.arange(part, dtype=i32) % pair
    comes = (own_line // plane_lines * KINDS + kind) * pair + within[None, :]
    take = comes.reshape(KINDS * part, 1) == chunks[None, :]

    raw = exchange(split(micro_grads[0, 0], master[0], moment_one[0], moment_two[0], plane), PLANE)
    tables = [t.astype(bf16) for t in (order, route, take, pick, place)]
    raw, *tables = lax.optimization_barrier((raw, *tables))
    order, route, take, pick, place = [near(t) for t in tables]
    packed = pl.pallas_call(
        pack_kernel,
        out_shape=pltpu.VMEM((ring, 2 * part + KINDS * pair, wide), bf16),
        in_specs=[VMEM] * 3,
        out_specs=VMEM,
        name="pack",
    )(near(raw), order, route)
    reduced = pl.pallas_call(
        reduce_kernel,
        out_shape=pltpu.VMEM((ring, (2 + KINDS) * part, wide), bf16),
        in_specs=[VMEM] * 2,
        out_specs=VMEM,
        name="reduce",
    )(near(exchange(packed, RING)), take)
    every = exchange(reduced, RING)

    sent = pl.pallas_call(
        send_kernel,
        out_shape=pltpu.VMEM((plane, layers, SLOT_ROWS, wide), f32),
        in_specs=[VMEM] * 2,
        out_specs=VMEM,
        name="send",
    )(near(every), pick)
    got = exchange(sent.reshape(plane * layers, SLOT_ROWS, wide), (*PLANE, "layer"))

    copies, rms = pl.pallas_call(
        lambda *refs: step_kernel(float(layers * rows * width), *refs),
        out_shape=(
            pltpu.VMEM((lax.axis_size(HALF), rows, wide), bf16),
            jax.ShapeDtypeStruct((1, wide), f32),
        ),
        in_specs=[VMEM] * 3,
        out_specs=(VMEM, VMEM),
        name="step",
    )(near(every), near(got), place)
    core = lax.axis_index("c")
    halves, got, rms = lax.optimization_barrier((exchange(copies, HALF), got, rms))
    others = lax.ppermute(halves, "c", [(0, 1), (1, 0)])
    weights = join(core, halves)

    my_slots = lax.axis_index((RING, *PLANE)) * SLOT_ROWS
    my_slots = my_slots + slab * jnp.arange(capacity, dtype=i32)
    keep = jnp.any(line[None, :] == my_slots[:, None], axis=1).astype(i32)
    at = jnp.concatenate([lax.axis_index("layer").astype(i32).reshape(1), keep])
    new = pl.pallas_call(
        own_kernel,
        out_shape=(jax.ShapeDtypeStruct(master.shape[1:], f32),) * 3,
        in_specs=[SMEM] + [VMEM] * 5,
        out_specs=(VMEM,) * 3,
        scratch_shapes=[pltpu.VMEM((SLOT_ROWS, width), f32)],
        name="own",
    )(at, near(got), near(rms), master[0], moment_one[0], moment_two[0])
    others, weights = lax.optimization_barrier((others, weights))
    weights = join(1 - core, others, weights)
    return (new[0][None], new[1][None], new[2][None], weights[None], rms[0, 0])


def solution(mesh):
    ring = mesh.shape["dp"] // math.prod(PLANE_SHAPE)
    devices = mesh.devices.reshape(ring, *PLANE_SHAPE, mesh.shape["layer"])
    split_mesh = Mesh(devices, (RING, *PLANE, "layer"))
    dp = (RING, *PLANE)
    in_specs = (
        P("layer", dp, None, None),
        P("layer", dp, None, None),
        P("layer", dp, None, None),
        P("layer", dp, None, None),
        P("layer", None),
        P("layer", None),
    )
    out_specs = (
        P("layer", dp, None, None),
        P("layer", dp, None, None),
        P("layer", dp, None, None),
        P("layer", None, None),
        P(),
    )
    return jax.shard_map(
        shards, mesh=split_mesh, in_specs=in_specs, out_specs=out_specs, check_vma=False
    )
```

```python
import math

import jax
import jax.numpy as jnp
from jax import lax
from jax.experimental import pallas as pl
from jax.experimental.pallas import tpu as pltpu
from jax.sharding import Mesh
from jax.sharding import PartitionSpec as P

beta_one = 0.9
beta_two = 0.95
learn_rate = 0.0003
decay_rate = 0.1
adam_eps = 1e-08
step_number = 100.0

RING = "z"
PLANE = ("pair", "x", "c")
PLANE_SHAPE = (2, 4, 2)
HALF = ("pair", "x")
SLOT_ROWS = 8
KINDS = 4


def adamw(param, first, second, grad):
    first_new = beta_one * first + (1.0 - beta_one) * grad
    second_new = beta_two * second + (1.0 - beta_two) * grad * grad
    corr_one = 1.0 - beta_one**step_number
    corr_two = 1.0 - beta_two**step_number
    update = (
        first_new / corr_one / (jnp.sqrt(second_new / corr_two) + adam_eps) + decay_rate * param
    )
    return (param - learn_rate * update, first_new, second_new)


def exchange(chunks, axis):
    return lax.all_to_all(chunks, axis, 0, 0, tiled=True)


def two_terms(value):
    high = value.astype(jnp.bfloat16)
    return high, (value - high.astype(jnp.float32)).astype(jnp.bfloat16)


def choose(matrix, values):
    return jnp.dot(matrix, values, preferred_element_type=jnp.float32)


VMEM = pl.BlockSpec(memory_space=pltpu.VMEM)
SMEM = pl.BlockSpec(memory_space=pltpu.SMEM)
ANY = pl.BlockSpec(memory_space=pl.ANY)


def near(value):
    return pltpu.with_memory_space_constraint(value, pltpu.VMEM)


def split_kernel(grads, master, first, second, out, held, rows, terms, in_sem, out_sem, term_sem):
    plane, _, wide = out.shape
    count = grads.shape[0]
    pieces = in_sem.shape[0]
    size = count // pieces
    arrivals = [
        pltpu.make_async_copy(
            grads.at[pl.ds(i * size, size), :], held.at[pl.ds(i * size, size), :], in_sem.at[i]
        )
        for i in range(pieces)
    ]
    for arrival in arrivals:
        arrival.start()
    rows[...] = jnp.zeros_like(rows)
    capacity, slab, _ = master.shape
    for i, state in enumerate((master, first, second)):
        for s in range(capacity):
            rows[i, s * slab : (s + 1) * slab, :] = state[s]
    high, low = two_terms(rows[0])
    values = (high, low, rows[1].astype(jnp.bfloat16), rows[2].astype(jnp.bfloat16))
    for t, value in enumerate(values):
        for k in range(plane):
            at = slice(t * SLOT_ROWS, (t + 1) * SLOT_ROWS)
            terms[k, at, :] = value[:, k * wide : (k + 1) * wide]
    moves = [
        pltpu.make_async_copy(terms, out.at[:, pl.ds(count, terms.shape[1]), :], term_sem)
    ]
    moves[0].start()
    for i, arrival in enumerate(arrivals):
        arrival.wait()
        for k in range(plane):
            move = pltpu.make_async_copy(
                held.at[pl.ds(i * size, size), pl.ds(k * wide, wide)],
                out.at[k, pl.ds(i * size, size), :],
                out_sem.at[i, k],
            )
            move.start()
            moves.append(move)
    for move in moves:
        move.wait()


def split(grads, master, first, second, plane):
    count, width = grads.shape
    wide = width // plane
    pieces = 4
    return pl.pallas_call(
        split_kernel,
        out_shape=jax.ShapeDtypeStruct((plane, count + KINDS * SLOT_ROWS, wide), grads.dtype),
        in_specs=[ANY, VMEM, VMEM, VMEM],
        out_specs=ANY,
        scratch_shapes=[
            pltpu.VMEM((count, width), grads.dtype),
            pltpu.VMEM((3, SLOT_ROWS, width), jnp.float32),
            pltpu.VMEM((plane, KINDS * SLOT_ROWS, wide), grads.dtype),
            pltpu.SemaphoreType.DMA((pieces,)),
            pltpu.SemaphoreType.DMA((pieces, plane)),
            pltpu.SemaphoreType.DMA,
        ],
        name="split",
    )(grads, master, first, second)


def join_kernel(core, strips, *refs):
    out, sem = refs[-2:]
    count, _, wide = strips.shape
    moves = [
        pltpu.make_async_copy(
            strips.at[i],
            out.at[:, pl.ds(pl.multiple_of((2 * i + core[0]) * wide, wide), wide)],
            sem.at[i],
        )
        for i in range(count)
    ]
    for move in moves:
        move.start()
    for move in moves:
        move.wait()


def join(core, strips, *before):
    count, rows, wide = strips.shape
    return pl.pallas_call(
        join_kernel,
        out_shape=jax.ShapeDtypeStruct((rows, 2 * count * wide), strips.dtype),
        in_specs=[SMEM, VMEM] + [ANY] * len(before),
        out_specs=ANY,
        scratch_shapes=[pltpu.SemaphoreType.DMA((count,))],
        input_output_aliases={2: 0} if before else {},
        name="join",
    )(core.reshape(1), near(strips), *before)


def own_kernel(at, got, rms, master, first, second, *refs):
    outs, rows = refs[:3], refs[3]
    wide = got.shape[2]
    count = rows.shape[1] // wide
    layers = got.shape[0] // count
    for k in range(count):
        rows[:, k * wide : (k + 1) * wide] = got[k * layers + at[0]]
    clip_factor = jnp.minimum(1.0, 1.0 / rms[:, :1])
    capacity, slab, _ = master.shape
    for s in range(capacity):
        old = (master[s], first[s], second[s])
        new = adamw(*old, rows[s * slab : (s + 1) * slab, :] * clip_factor)
        keep = at[1 + s] > 0
        for out, n, o in zip(outs, new, old, strict=True):
            out[s] = jnp.where(keep, n, o)


def pack_kernel(raw, order, route, out):
    plane, count, _ = raw.shape
    ring = out.shape[0]
    rows = order.shape[0]
    part = rows // ring
    total = raw[0, :rows, :].astype(jnp.float32)
    for j in range(1, plane):
        total = total + raw[j, :rows, :].astype(jnp.float32)
    lines = [
        raw[j, at : at + SLOT_ROWS, :] for at in range(rows, count, SLOT_ROWS) for j in range(plane)
    ]
    high, low = two_terms(total)
    sources = ((order, high), (order, low), (route, jnp.concatenate(lines, axis=0)))
    for i, (matrix, source) in enumerate(sources):
        chosen = choose(matrix[...], source).astype(out.dtype)
        size = chosen.shape[0] // ring
        for z in range(ring):
            out[z, i * part : i * part + size, :] = chosen[z * size : (z + 1) * size, :]


def reduce_kernel(got, take, out):
    ring = got.shape[0]
    part = out.shape[1] // (2 + KINDS)
    total = got[0, :part, :].astype(jnp.float32) + got[0, part : 2 * part, :].astype(jnp.float32)
    for z in range(1, ring):
        total = total + (
            got[z, :part, :].astype(jnp.float32) + got[z, part : 2 * part, :].astype(jnp.float32)
        )
    high, low = two_terms(total)
    lines = jnp.concatenate([got[z, 2 * part :, :] for z in range(ring)], axis=0)
    lines = choose(take[...], lines).astype(out.dtype)
    for z in range(ring):
        out[z, :part, :] = high
        out[z, part : 2 * part, :] = low
        out[z, 2 * part :, :] = lines


def ordered(every, term, part):
    return jnp.concatenate(
        [every[z, term * part : (term + 1) * part, :] for z in range(every.shape[0])], axis=0
    )


def send_kernel(every, pick, out):
    plane, layers, _, wide = out.shape
    part = pick.shape[1] // every.shape[0]
    high, low = ordered(every, 0, part), ordered(every, 1, part)
    total = high.astype(jnp.float32) + low.astype(jnp.float32)
    squares = jnp.sum(total * total)
    sent = choose(pick[...], high) + choose(pick[...], low)
    line = lax.broadcasted_iota(jnp.int32, sent.shape, 0)
    sent = jnp.where(line % SLOT_ROWS == SLOT_ROWS - 1, squares, sent)
    for j in range(plane):
        for layer in range(layers):
            out[j, layer] = sent[j * SLOT_ROWS : (j + 1) * SLOT_ROWS, :]


def step_kernel(element_total, every, got, place, copies, rms):
    part = place.shape[1] // every.shape[0]
    squares = jnp.sum(got[...], axis=0)[SLOT_ROWS - 1 :, :]
    grad_rms = jnp.sqrt(squares / element_total + 1e-06)
    rms[...] = grad_rms
    clip_factor = jnp.minimum(1.0, 1.0 / grad_rms)
    terms = [ordered(every, t, part).astype(jnp.float32) for t in range(2 + KINDS)]
    grad = (terms[0] + terms[1]) * clip_factor
    param = adamw(terms[2] + terms[3], terms[4], terms[5], grad)[0]
    weights = choose(place[...], param.astype(copies.dtype)).astype(copies.dtype)
    for x in range(copies.shape[0]):
        copies[x] = weights


def shards(micro_grads, master, moment_one, moment_two, owner, slot):
    rows, width = micro_grads.shape[2:]
    capacity, slab = master.shape[1:3]
    ring = lax.axis_size(RING)
    plane = lax.axis_size(PLANE)
    lines = capacity * slab
    wide = width // plane
    layers = lax.axis_size("layer")
    my_z = lax.axis_index(RING)
    part = rows // ring
    plane_lines = plane * SLOT_ROWS
    bf16, f32, i32 = jnp.bfloat16, jnp.float32, jnp.int32
    count = jnp.arange(rows, dtype=i32)
    few = jnp.arange(plane_lines, dtype=i32)

    deal = -(-plane * capacity // ring)
    pair = deal * slab
    home = owner[0] * capacity + slot[0]
    rank = jnp.sum((home[None, :] < home[:, None]).astype(i32), axis=1)
    line = owner[0] * SLOT_ROWS + slot[0] * slab
    member, turn = rank % ring, rank // ring

    def per_row(value):
        return (value[:, None] + jnp.arange(slab, dtype=i32)[None, :]).reshape(rows)

    line_of = per_row(line)
    dealt = per_row(member * part + turn * slab)
    pair_of = per_row(member * pair + turn % deal * slab)
    order = dealt[None, :] == count[:, None]
    place = dealt[:, None] == count[None, :]
    line_at = jnp.sum(jnp.where(order, line_of[None, :], 0), axis=1)
    pick = (my_z * plane_lines + few)[:, None] == line_at[None, :]
    mine = line_of[None, :] == (my_z * plane_lines + few)[:, None]
    pair_at = jnp.sum(jnp.where(mine, pair_of[None, :] + 1, 0), axis=1) - 1
    kind = jnp.arange(KINDS, dtype=i32)[:, None]
    goes = jnp.where(pair_at < 0, -1, pair_at)[None, :]
    goes = jnp.where(goes < 0, -1, (goes // pair * KINDS + kind) * pair + goes % pair)
    chunks = jnp.arange(ring * KINDS * pair, dtype=i32)
    route = goes.reshape(1, KINDS * plane_lines) == chunks[:, None]
    own_line = lax.dynamic_slice_in_dim(line_at, my_z * part, part)
    within = jnp.arange(part, dtype=i32) % pair
    comes = (own_line // plane_lines * KINDS + kind) * pair + within[None, :]
    take = comes.reshape(KINDS * part, 1) == chunks[None, :]

    raw = exchange(split(micro_grads[0, 0], master[0], moment_one[0], moment_two[0], plane), PLANE)
    my_slots = lax.axis_index((RING, *PLANE)) * SLOT_ROWS
    my_slots = my_slots + slab * jnp.arange(capacity, dtype=i32)
    keep = jnp.any(line[None, :] == my_slots[:, None], axis=1).astype(i32)
    at = jnp.concatenate([lax.axis_index("layer").astype(i32).reshape(1), keep])
    tables = [t.astype(bf16) for t in (order, route, take, pick, place)]
    raw, at, *tables = lax.optimization_barrier((raw, at, *tables))
    order, route, take, pick, place = [near(t) for t in tables]
    packed = pl.pallas_call(
        pack_kernel,
        out_shape=pltpu.VMEM((ring, 2 * part + KINDS * pair, wide), bf16),
        in_specs=[VMEM] * 3,
        out_specs=VMEM,
        name="pack",
    )(near(raw), order, route)
    reduced = pl.pallas_call(
        reduce_kernel,
        out_shape=pltpu.VMEM((ring, (2 + KINDS) * part, wide), bf16),
        in_specs=[VMEM] * 2,
        out_specs=VMEM,
        name="reduce",
    )(near(exchange(packed, RING)), take)
    every = exchange(reduced, RING)

    sent = pl.pallas_call(
        send_kernel,
        out_shape=pltpu.VMEM((plane, layers, SLOT_ROWS, wide), f32),
        in_specs=[VMEM] * 2,
        out_specs=VMEM,
        name="send",
    )(near(every), pick)
    got = exchange(sent.reshape(plane * layers, SLOT_ROWS, wide), (*PLANE, "layer"))

    copies, rms = pl.pallas_call(
        lambda *refs: step_kernel(float(layers * rows * width), *refs),
        out_shape=(
            pltpu.VMEM((lax.axis_size(HALF), rows, wide), bf16),
            jax.ShapeDtypeStruct((1, wide), f32),
        ),
        in_specs=[VMEM] * 3,
        out_specs=(VMEM, VMEM),
        name="step",
    )(near(every), near(got), place)
    core = lax.axis_index("c")
    halves, got, rms = lax.optimization_barrier((exchange(copies, HALF), got, rms))
    others = lax.ppermute(halves, "c", [(0, 1), (1, 0)])
    weights = join(core, halves)

    new = pl.pallas_call(
        own_kernel,
        out_shape=(jax.ShapeDtypeStruct(master.shape[1:], f32),) * 3,
        in_specs=[SMEM] + [VMEM] * 5,
        out_specs=(VMEM,) * 3,
        scratch_shapes=[pltpu.VMEM((SLOT_ROWS, width), f32)],
        name="own",
    )(at, near(got), near(rms), *[near(o[0]) for o in (master, moment_one, moment_two)])
    others, weights = lax.optimization_barrier((others, weights))
    weights = join(1 - core, others, weights)
    return (new[0][None], new[1][None], new[2][None], weights[None], rms[0, 0])


def solution(mesh):
    ring = mesh.shape["dp"] // math.prod(PLANE_SHAPE)
    devices = mesh.devices.reshape(ring, *PLANE_SHAPE, mesh.shape["layer"])
    split_mesh = Mesh(devices, (RING, *PLANE, "layer"))
    dp = (RING, *PLANE)
    in_specs = (
        P("layer", dp, None, None),
        P("layer", dp, None, None),
        P("layer", dp, None, None),
        P("layer", dp, None, None),
        P("layer", None),
        P("layer", None),
    )
    out_specs = (
        P("layer", dp, None, None),
        P("layer", dp, None, None),
        P("layer", dp, None, None),
        P("layer", None, None),
        P(),
    )
    return jax.shard_map(
        shards, mesh=split_mesh, in_specs=in_specs, out_specs=out_specs, check_vma=False
    )
```

```python
import math

import jax
import jax.numpy as jnp
from jax import lax
from jax.experimental import pallas as pl
from jax.experimental.pallas import tpu as pltpu
from jax.sharding import Mesh
from jax.sharding import PartitionSpec as P

beta_one = 0.9
beta_two = 0.95
learn_rate = 0.0003
decay_rate = 0.1
adam_eps = 1e-08
step_number = 100.0

RING = "z"
PLANE = ("pair", "x", "c")
PLANE_SHAPE = (2, 4, 2)
HALF = ("pair", "x")
SLOT_ROWS = 8
KINDS = 4


def adamw(param, first, second, grad):
    first_new = beta_one * first + (1.0 - beta_one) * grad
    second_new = beta_two * second + (1.0 - beta_two) * grad * grad
    corr_one = 1.0 - beta_one**step_number
    corr_two = 1.0 - beta_two**step_number
    update = (
        first_new / corr_one / (jnp.sqrt(second_new / corr_two) + adam_eps) + decay_rate * param
    )
    return (param - learn_rate * update, first_new, second_new)


def exchange(chunks, axis):
    return lax.all_to_all(chunks, axis, 0, 0, tiled=True)


def two_terms(value):
    high = value.astype(jnp.bfloat16)
    return high, (value - high.astype(jnp.float32)).astype(jnp.bfloat16)


def choose(matrix, values):
    return jnp.dot(matrix, values, preferred_element_type=jnp.float32)


VMEM = pl.BlockSpec(memory_space=pltpu.VMEM)
SMEM = pl.BlockSpec(memory_space=pltpu.SMEM)
ANY = pl.BlockSpec(memory_space=pl.ANY)


def near(value):
    return pltpu.with_memory_space_constraint(value, pltpu.VMEM)


def fill_rows(rows, states):
    capacity, slab, _ = states[0].shape
    for i, state in enumerate(states):
        for s in range(capacity):
            rows[i, s * slab : (s + 1) * slab, :] = state[s]
        rows[i, capacity * slab :, :] = jnp.ones_like(rows[i, capacity * slab :, :])


def split_kernel(grads, master, first, second, out, held, rows, strips, in_sem, out_sem):
    plane, total, wide = out.shape
    count = grads.shape[0]
    pieces = in_sem.shape[0]
    size = count // pieces
    arrivals = [
        pltpu.make_async_copy(
            grads.at[pl.ds(i * size, size), :], held.at[pl.ds(i * size, size), :], in_sem.at[i]
        )
        for i in range(pieces)
    ]
    for arrival in arrivals:
        arrival.start()
    fill_rows(rows, (master, first, second))
    high, low = two_terms(rows[0])
    values = (high, low, rows[1].astype(jnp.bfloat16), rows[2].astype(jnp.bfloat16))
    for t, value in enumerate(values):
        at = count + t * SLOT_ROWS
        for k in range(plane):
            strips[k, at : at + SLOT_ROWS, :] = value[:, k * wide : (k + 1) * wide]
    moves = []
    for i in range(pieces + 1):
        at, length = i * size, size
        if i < pieces:
            arrivals[i].wait()
            for k in range(plane):
                strips[k, at : at + size, :] = held[at : at + size, k * wide : (k + 1) * wide]
        else:
            length = total - count
        here = pl.ds(at, length)
        moves.append(
            pltpu.make_async_copy(strips.at[:, here, :], out.at[:, here, :], out_sem.at[i])
        )
        moves[-1].start()
    for move in moves:
        move.wait()


def split(grads, master, first, second, plane):
    count, width = grads.shape
    shape = (plane, count + KINDS * SLOT_ROWS, width // plane)
    pieces = 4
    return pl.pallas_call(
        split_kernel,
        out_shape=jax.ShapeDtypeStruct(shape, grads.dtype),
        in_specs=[ANY, VMEM, VMEM, VMEM],
        out_specs=ANY,
        scratch_shapes=[
            pltpu.VMEM((count, width), grads.dtype),
            pltpu.VMEM((3, SLOT_ROWS, width), jnp.float32),
            pltpu.VMEM(shape, grads.dtype),
            pltpu.SemaphoreType.DMA((pieces,)),
            pltpu.SemaphoreType.DMA((pieces + 1,)),
        ],
        name="split",
    )(grads, master, first, second)


def join_kernel(core, strips, *refs):
    out, sem = refs[-2:]
    count, _, wide = strips.shape
    moves = [
        pltpu.make_async_copy(
            strips.at[i],
            out.at[:, pl.ds(pl.multiple_of((2 * i + core[0]) * wide, wide), wide)],
            sem.at[i],
        )
        for i in range(count)
    ]
    for move in moves:
        move.start()
    for move in moves:
        move.wait()


def join(core, strips, *before):
    count, rows, wide = strips.shape
    return pl.pallas_call(
        join_kernel,
        out_shape=jax.ShapeDtypeStruct((rows, 2 * count * wide), strips.dtype),
        in_specs=[SMEM, VMEM] + [ANY] * len(before),
        out_specs=ANY,
        scratch_shapes=[pltpu.SemaphoreType.DMA((count,))],
        input_output_aliases={2: 0} if before else {},
        name="join",
    )(core.reshape(1), near(strips), *before)


def own_kernel(at, got, rms, master, first, second, *refs):
    outs, rows, grads = refs[:3], refs[3], refs[4]
    wide = got.shape[2]
    count = grads.shape[1] // wide
    layers = got.shape[0] // count
    for k in range(count):
        grads[:, k * wide : (k + 1) * wide] = got[k * layers + at[0]]
    fill_rows(rows, (master, first, second))
    clip_factor = jnp.minimum(1.0, 1.0 / rms[:, :1])
    new = adamw(rows[0], rows[1], rows[2], grads[...] * clip_factor)
    capacity, slab, _ = master.shape
    for i, (out, old) in enumerate(zip(outs, (master, first, second), strict=True)):
        rows[i] = new[i]
        for s in range(capacity):
            out[s] = jnp.where(at[1 + s] > 0, rows[i, s * slab : (s + 1) * slab, :], old[s])


def pack_kernel(raw, order, route, out):
    plane, count, _ = raw.shape
    ring = out.shape[0]
    rows = order.shape[0]
    part = rows // ring
    total = raw[0, :rows, :].astype(jnp.float32)
    for j in range(1, plane):
        total = total + raw[j, :rows, :].astype(jnp.float32)
    lines = [
        raw[j, at : at + SLOT_ROWS, :] for at in range(rows, count, SLOT_ROWS) for j in range(plane)
    ]
    high, low = two_terms(total)
    sources = ((order, high), (order, low), (route, jnp.concatenate(lines, axis=0)))
    for i, (matrix, source) in enumerate(sources):
        chosen = choose(matrix[...], source).astype(out.dtype)
        size = chosen.shape[0] // ring
        for z in range(ring):
            out[z, i * part : i * part + size, :] = chosen[z * size : (z + 1) * size, :]


def reduce_kernel(got, take, out):
    ring = got.shape[0]
    part = out.shape[1] // (2 + KINDS)
    total = got[0, :part, :].astype(jnp.float32) + got[0, part : 2 * part, :].astype(jnp.float32)
    for z in range(1, ring):
        total = total + (
            got[z, :part, :].astype(jnp.float32) + got[z, part : 2 * part, :].astype(jnp.float32)
        )
    high, low = two_terms(total)
    lines = jnp.concatenate([got[z, 2 * part :, :] for z in range(ring)], axis=0)
    lines = choose(take[...], lines).astype(out.dtype)
    for z in range(ring):
        out[z, :part, :] = high
        out[z, part : 2 * part, :] = low
        out[z, 2 * part :, :] = lines


def ordered(every, term, part):
    return jnp.concatenate(
        [every[z, term * part : (term + 1) * part, :] for z in range(every.shape[0])], axis=0
    )


def send_kernel(every, pick, out):
    plane, layers, _, wide = out.shape
    part = pick.shape[1] // every.shape[0]
    high, low = ordered(every, 0, part), ordered(every, 1, part)
    total = high.astype(jnp.float32) + low.astype(jnp.float32)
    squares = jnp.sum(total * total)
    sent = choose(pick[...], high) + choose(pick[...], low)
    line = lax.broadcasted_iota(jnp.int32, sent.shape, 0)
    sent = jnp.where(line % SLOT_ROWS == SLOT_ROWS - 1, squares, sent)
    for j in range(plane):
        for layer in range(layers):
            out[j, layer] = sent[j * SLOT_ROWS : (j + 1) * SLOT_ROWS, :]


def step_kernel(element_total, every, got, place, copies, rms):
    part = place.shape[1] // every.shape[0]
    squares = jnp.sum(got[...], axis=0)[SLOT_ROWS - 1 :, :]
    grad_rms = jnp.sqrt(squares / element_total + 1e-06)
    rms[...] = grad_rms
    clip_factor = jnp.minimum(1.0, 1.0 / grad_rms)
    terms = [ordered(every, t, part).astype(jnp.float32) for t in range(2 + KINDS)]
    grad = (terms[0] + terms[1]) * clip_factor
    param = adamw(terms[2] + terms[3], terms[4], terms[5], grad)[0]
    weights = choose(place[...], param.astype(copies.dtype)).astype(copies.dtype)
    for x in range(copies.shape[0]):
        copies[x] = weights


def shards(micro_grads, master, moment_one, moment_two, owner, slot):
    rows, width = micro_grads.shape[2:]
    capacity, slab = master.shape[1:3]
    ring = lax.axis_size(RING)
    plane = lax.axis_size(PLANE)
    lines = capacity * slab
    wide = width // plane
    layers = lax.axis_size("layer")
    my_z = lax.axis_index(RING)
    part = rows // ring
    plane_lines = plane * SLOT_ROWS
    bf16, f32, i32 = jnp.bfloat16, jnp.float32, jnp.int32
    count = jnp.arange(rows, dtype=i32)
    few = jnp.arange(plane_lines, dtype=i32)

    deal = -(-plane * capacity // ring)
    pair = deal * slab
    home = owner[0] * capacity + slot[0]
    rank = jnp.sum((home[None, :] < home[:, None]).astype(i32), axis=1)
    line = owner[0] * SLOT_ROWS + slot[0] * slab
    member, turn = rank % ring, rank // ring

    def per_row(value):
        return (value[:, None] + jnp.arange(slab, dtype=i32)[None, :]).reshape(rows)

    line_of = per_row(line)
    dealt = per_row(member * part + turn * slab)
    pair_of = per_row(member * pair + turn % deal * slab)
    order = dealt[None, :] == count[:, None]
    place = dealt[:, None] == count[None, :]
    line_at = jnp.sum(jnp.where(order, line_of[None, :], 0), axis=1)
    pick = (my_z * plane_lines + few)[:, None] == line_at[None, :]
    mine = line_of[None, :] == (my_z * plane_lines + few)[:, None]
    pair_at = jnp.sum(jnp.where(mine, pair_of[None, :] + 1, 0), axis=1) - 1
    kind = jnp.arange(KINDS, dtype=i32)[:, None]
    goes = jnp.where(pair_at < 0, -1, pair_at)[None, :]
    goes = jnp.where(goes < 0, -1, (goes // pair * KINDS + kind) * pair + goes % pair)
    chunks = jnp.arange(ring * KINDS * pair, dtype=i32)
    route = goes.reshape(1, KINDS * plane_lines) == chunks[:, None]
    own_line = lax.dynamic_slice_in_dim(line_at, my_z * part, part)
    within = jnp.arange(part, dtype=i32) % pair
    comes = (own_line // plane_lines * KINDS + kind) * pair + within[None, :]
    take = comes.reshape(KINDS * part, 1) == chunks[None, :]

    raw = exchange(split(micro_grads[0, 0], master[0], moment_one[0], moment_two[0], plane), PLANE)
    my_slots = lax.axis_index((RING, *PLANE)) * SLOT_ROWS
    my_slots = my_slots + slab * jnp.arange(capacity, dtype=i32)
    keep = jnp.any(line[None, :] == my_slots[:, None], axis=1).astype(i32)
    at = jnp.concatenate([lax.axis_index("layer").astype(i32).reshape(1), keep])
    tables = [t.astype(bf16) for t in (order, route, take, pick, place)]
    raw, at, *tables = lax.optimization_barrier((raw, at, *tables))
    order, route, take, pick, place = [near(t) for t in tables]
    packed = pl.pallas_call(
        pack_kernel,
        out_shape=pltpu.VMEM((ring, 2 * part + KINDS * pair, wide), bf16),
        in_specs=[VMEM] * 3,
        out_specs=VMEM,
        name="pack",
    )(near(raw), order, route)
    reduced = pl.pallas_call(
        reduce_kernel,
        out_shape=pltpu.VMEM((ring, (2 + KINDS) * part, wide), bf16),
        in_specs=[VMEM] * 2,
        out_specs=VMEM,
        name="reduce",
    )(near(exchange(packed, RING)), take)
    every = exchange(reduced, RING)

    sent = pl.pallas_call(
        send_kernel,
        out_shape=pltpu.VMEM((plane, layers, SLOT_ROWS, wide), f32),
        in_specs=[VMEM] * 2,
        out_specs=VMEM,
        name="send",
    )(near(every), pick)
    got = exchange(sent.reshape(plane * layers, SLOT_ROWS, wide), (*PLANE, "layer"))

    copies, rms = pl.pallas_call(
        lambda *refs: step_kernel(float(layers * rows * width), *refs),
        out_shape=(
            pltpu.VMEM((lax.axis_size(HALF), rows, wide), bf16),
            jax.ShapeDtypeStruct((1, wide), f32),
        ),
        in_specs=[VMEM] * 3,
        out_specs=(VMEM, VMEM),
        name="step",
    )(near(every), near(got), place)
    core = lax.axis_index("c")
    halves, got, rms = lax.optimization_barrier((exchange(copies, HALF), got, rms))
    others = lax.ppermute(halves, "c", [(0, 1), (1, 0)])
    weights = join(core, halves)

    new = pl.pallas_call(
        own_kernel,
        out_shape=(jax.ShapeDtypeStruct(master.shape[1:], f32),) * 3,
        in_specs=[SMEM] + [VMEM] * 5,
        out_specs=(VMEM,) * 3,
        scratch_shapes=[
            pltpu.VMEM((3, SLOT_ROWS, width), f32),
            pltpu.VMEM((SLOT_ROWS, width), f32),
        ],
        name="own",
    )(at, near(got), near(rms), *[near(o[0]) for o in (master, moment_one, moment_two)])
    others, weights = lax.optimization_barrier((others, weights))
    weights = join(1 - core, others, weights)
    return (new[0][None], new[1][None], new[2][None], weights[None], rms[0, 0])


def solution(mesh):
    ring = mesh.shape["dp"] // math.prod(PLANE_SHAPE)
    devices = mesh.devices.reshape(ring, *PLANE_SHAPE, mesh.shape["layer"])
    split_mesh = Mesh(devices, (RING, *PLANE, "layer"))
    dp = (RING, *PLANE)
    in_specs = (
        P("layer", dp, None, None),
        P("layer", dp, None, None),
        P("layer", dp, None, None),
        P("layer", dp, None, None),
        P("layer", None),
        P("layer", None),
    )
    out_specs = (
        P("layer", dp, None, None),
        P("layer", dp, None, None),
        P("layer", dp, None, None),
        P("layer", None, None),
        P(),
    )
    return jax.shard_map(
        shards, mesh=split_mesh, in_specs=in_specs, out_specs=out_specs, check_vma=False
    )
```

```python
import math

import jax
import jax.numpy as jnp
from jax import lax
from jax.experimental import pallas as pl
from jax.experimental.pallas import tpu as pltpu
from jax.sharding import Mesh
from jax.sharding import PartitionSpec as P

beta_one = 0.9
beta_two = 0.95
learn_rate = 0.0003
decay_rate = 0.1
adam_eps = 1e-08
step_number = 100.0

RING = "z"
PLANE = ("pair", "x", "c")
PLANE_SHAPE = (2, 4, 2)
HALF = ("pair", "x")
SLOT_ROWS = 8
KINDS = 4


def adamw(param, first, second, grad):
    first_new = beta_one * first + (1.0 - beta_one) * grad
    second_new = beta_two * second + (1.0 - beta_two) * grad * grad
    corr_one = 1.0 - beta_one**step_number
    corr_two = 1.0 - beta_two**step_number
    update = (
        first_new / corr_one / (jnp.sqrt(second_new / corr_two) + adam_eps) + decay_rate * param
    )
    return (param - learn_rate * update, first_new, second_new)


def exchange(chunks, axis):
    return lax.all_to_all(chunks, axis, 0, 0, tiled=True)


def two_terms(value):
    high = value.astype(jnp.bfloat16)
    return high, (value - high.astype(jnp.float32)).astype(jnp.bfloat16)


def choose(matrix, values):
    return jnp.dot(matrix, values, preferred_element_type=jnp.float32)


VMEM = pl.BlockSpec(memory_space=pltpu.VMEM)
SMEM = pl.BlockSpec(memory_space=pltpu.SMEM)
ANY = pl.BlockSpec(memory_space=pl.ANY)


def near(value):
    return pltpu.with_memory_space_constraint(value, pltpu.VMEM)


def fill_rows(rows, states):
    capacity, slab, _ = states[0].shape
    for i, state in enumerate(states):
        for s in range(capacity):
            rows[i, s * slab : (s + 1) * slab, :] = state[s]
        rows[i, capacity * slab :, :] = jnp.ones_like(rows[i, capacity * slab :, :])


def split_kernel(grads, master, first, second, out, rows):
    plane, _, wide = out.shape
    count = grads.shape[0]
    for k in range(plane):
        out[k, :count, :] = grads[:, k * wide : (k + 1) * wide]
    fill_rows(rows, (master, first, second))
    high, low = two_terms(rows[0])
    values = (high, low, rows[1].astype(jnp.bfloat16), rows[2].astype(jnp.bfloat16))
    for t, value in enumerate(values):
        at = count + t * SLOT_ROWS
        for k in range(plane):
            out[k, at : at + SLOT_ROWS, :] = value[:, k * wide : (k + 1) * wide]


def split(grads, master, first, second, plane):
    count, width = grads.shape
    shape = (plane, count + KINDS * SLOT_ROWS, width // plane)
    return pl.pallas_call(
        split_kernel,
        out_shape=jax.ShapeDtypeStruct(shape, grads.dtype),
        in_specs=[VMEM] * 4,
        out_specs=VMEM,
        scratch_shapes=[pltpu.VMEM((3, SLOT_ROWS, width), jnp.float32)],
        name="split",
    )(grads, master, first, second)


def join_kernel(core, strips, *refs):
    out, sem = refs[-2:]
    count, _, wide = strips.shape
    moves = [
        pltpu.make_async_copy(
            strips.at[i],
            out.at[:, pl.ds(pl.multiple_of((2 * i + core[0]) * wide, wide), wide)],
            sem.at[i],
        )
        for i in range(count)
    ]
    for move in moves:
        move.start()
    for move in moves:
        move.wait()


def join(core, strips, *before):
    count, rows, wide = strips.shape
    return pl.pallas_call(
        join_kernel,
        out_shape=jax.ShapeDtypeStruct((rows, 2 * count * wide), strips.dtype),
        in_specs=[SMEM, VMEM] + [ANY] * len(before),
        out_specs=ANY,
        scratch_shapes=[pltpu.SemaphoreType.DMA((count,))],
        input_output_aliases={2: 0} if before else {},
        name="join",
    )(core.reshape(1), near(strips), *before)


def own_kernel(at, got, rms, master, first, second, *refs):
    outs, rows, grads = refs[:3], refs[3], refs[4]
    wide = got.shape[2]
    count = grads.shape[1] // wide
    layers = got.shape[0] // count
    for k in range(count):
        grads[:, k * wide : (k + 1) * wide] = got[k * layers + at[0]]
    fill_rows(rows, (master, first, second))
    clip_factor = jnp.minimum(1.0, 1.0 / rms[:, :1])
    new = adamw(rows[0], rows[1], rows[2], grads[...] * clip_factor)
    capacity, slab, _ = master.shape
    for i, (out, old) in enumerate(zip(outs, (master, first, second), strict=True)):
        rows[i] = new[i]
        for s in range(capacity):
            out[s] = jnp.where(at[1 + s] > 0, rows[i, s * slab : (s + 1) * slab, :], old[s])


def pack_kernel(raw, out, strips):
    plane, count, _ = raw.shape
    ring, part = out.shape[0], out.shape[1] // 2
    rows = ring * part
    total = raw[0, :rows, :].astype(jnp.float32)
    for j in range(1, plane):
        total = total + raw[j, :rows, :].astype(jnp.float32)
    for i, term in enumerate(two_terms(total)):
        for z in range(ring):
            out[z, i * part : (i + 1) * part, :] = term[z * part : (z + 1) * part, :]
    for t in range(KINDS):
        at = rows + t * SLOT_ROWS
        for j in range(plane):
            to = (t * plane + j) * SLOT_ROWS
            strips[to : to + SLOT_ROWS, :] = raw[j, at : at + SLOT_ROWS, :]


def reduce_kernel(got, out):
    ring = got.shape[0]
    part = out.shape[1] // 2
    total = jnp.zeros(out.shape[1:], jnp.float32)[:part]
    for z in range(ring):
        total = total + (
            got[z, :part, :].astype(jnp.float32) + got[z, part:, :].astype(jnp.float32)
        )
    high, low = two_terms(total)
    for z in range(ring):
        out[z, :part, :] = high
        out[z, part:, :] = low


def ordered(every, term, part):
    return jnp.concatenate(
        [every[z, term * part : (term + 1) * part, :] for z in range(every.shape[0])], axis=0
    )


def send_kernel(every, pick, out):
    plane, layers, _, wide = out.shape
    part = pick.shape[1] // every.shape[0]
    high, low = ordered(every, 0, part), ordered(every, 1, part)
    total = high.astype(jnp.float32) + low.astype(jnp.float32)
    squares = jnp.sum(total * total)
    sent = choose(pick[...], high) + choose(pick[...], low)
    line = lax.broadcasted_iota(jnp.int32, sent.shape, 0)
    sent = jnp.where(line % SLOT_ROWS == SLOT_ROWS - 1, squares, sent)
    for j in range(plane):
        for layer in range(layers):
            out[j, layer] = sent[j * SLOT_ROWS : (j + 1) * SLOT_ROWS, :]


def step_kernel(element_total, every, got, place, *refs):
    states, (copies, rms) = refs[:-2], refs[-2:]
    part = every.shape[1] // 2
    squares = jnp.sum(got[...], axis=0)[SLOT_ROWS - 1 :, :]
    grad_rms = jnp.sqrt(squares / element_total + 1e-06)
    rms[...] = grad_rms
    clip_factor = jnp.minimum(1.0, 1.0 / grad_rms)
    grad = sum(ordered(every, t, part).astype(jnp.float32) for t in range(2)) * clip_factor
    size = states[0].shape[0] // KINDS
    terms = []
    for t in range(KINDS):
        lines = jnp.concatenate([s[t * size : (t + 1) * size, :] for s in states], axis=0)
        terms.append(choose(place[...], lines))
    param = adamw(terms[0] + terms[1], terms[2], terms[3], grad)[0]
    for x in range(copies.shape[0]):
        copies[x] = param.astype(copies.dtype)


def shards(micro_grads, master, moment_one, moment_two, owner, slot):
    rows, width = micro_grads.shape[2:]
    capacity, slab = master.shape[1:3]
    ring = lax.axis_size(RING)
    plane = lax.axis_size(PLANE)
    lines = capacity * slab
    wide = width // plane
    layers = lax.axis_size("layer")
    my_z = lax.axis_index(RING)
    part = rows // ring
    plane_lines = plane * SLOT_ROWS
    bf16, f32, i32 = jnp.bfloat16, jnp.float32, jnp.int32
    few = jnp.arange(plane_lines, dtype=i32)

    line = owner[0] * SLOT_ROWS + slot[0] * slab
    line_of = (line[:, None] + jnp.arange(slab, dtype=i32)[None, :]).reshape(rows)
    pick = (my_z * plane_lines + few)[:, None] == line_of[None, :]
    steps = [0] + list(range(-1, -ring // 2 - 1, -1)) + list(range(1, (ring + 1) // 2))
    sources = lax.rem(my_z + ring + jnp.array(steps, dtype=i32), ring)
    from_line = (sources[:, None] * plane_lines + few[None, :]).reshape(1, ring * plane_lines)
    place = line_of[:, None] == from_line

    raw = exchange(split(micro_grads[0, 0], master[0], moment_one[0], moment_two[0], plane), PLANE)
    my_slots = lax.axis_index((RING, *PLANE)) * SLOT_ROWS
    my_slots = my_slots + slab * jnp.arange(capacity, dtype=i32)
    keep = jnp.any(line[None, :] == my_slots[:, None], axis=1).astype(i32)
    at = jnp.concatenate([lax.axis_index("layer").astype(i32).reshape(1), keep])
    tables = [t.astype(bf16) for t in (pick, place)]
    raw, at, *tables = lax.optimization_barrier((raw, at, *tables))
    pick, place = [near(t) for t in tables]
    packed, strips = pl.pallas_call(
        pack_kernel,
        out_shape=(
            pltpu.VMEM((ring, 2 * part, wide), bf16),
            pltpu.VMEM((KINDS * plane_lines, wide), bf16),
        ),
        in_specs=[VMEM],
        out_specs=(VMEM, VMEM),
        name="pack",
    )(near(raw))
    def shift(value, by):
        return lax.ppermute(value, RING, [(i, (i + by) % ring) for i in range(ring)])

    def two_steps(value, here):
        (right, left), steps = here, []
        for _ in range(2):
            right, left = shift(right, 1), shift(left, -1)
            steps.append((right, left))
        return lax.optimization_barrier((exchange(value, RING), steps))

    summed, near_by = two_steps(packed, (strips, strips))
    reduced = pl.pallas_call(
        reduce_kernel,
        out_shape=pltpu.VMEM((ring, 2 * part, wide), bf16),
        in_specs=[VMEM],
        out_specs=VMEM,
        name="reduce",
    )(near(summed))
    every, far = two_steps(reduced, near_by[-1])
    states = [strips, *[p[0] for p in near_by + far], *[p[1] for p in (near_by + far)[: ring // 2 - 1]]]

    sent = pl.pallas_call(
        send_kernel,
        out_shape=pltpu.VMEM((plane, layers, SLOT_ROWS, wide), f32),
        in_specs=[VMEM] * 2,
        out_specs=VMEM,
        name="send",
    )(near(every), pick)
    got = exchange(sent.reshape(plane * layers, SLOT_ROWS, wide), (*PLANE, "layer"))

    copies, rms = pl.pallas_call(
        lambda *refs: step_kernel(float(layers * rows * width), *refs),
        out_shape=(
            pltpu.VMEM((lax.axis_size(HALF), rows, wide), bf16),
            jax.ShapeDtypeStruct((1, wide), f32),
        ),
        in_specs=[VMEM] * (3 + ring),
        out_specs=(VMEM, VMEM),
        name="step",
    )(near(every), near(got), place, *[near(s) for s in states])
    core = lax.axis_index("c")
    halves, got, rms = lax.optimization_barrier((exchange(copies, HALF), got, rms))
    others = lax.ppermute(halves, "c", [(0, 1), (1, 0)])
    weights = join(core, halves)

    new = pl.pallas_call(
        own_kernel,
        out_shape=(jax.ShapeDtypeStruct(master.shape[1:], f32),) * 3,
        in_specs=[SMEM] + [VMEM] * 5,
        out_specs=(VMEM,) * 3,
        scratch_shapes=[
            pltpu.VMEM((3, SLOT_ROWS, width), f32),
            pltpu.VMEM((SLOT_ROWS, width), f32),
        ],
        name="own",
    )(at, near(got), near(rms), *[near(o[0]) for o in (master, moment_one, moment_two)])
    others, weights = lax.optimization_barrier((others, weights))
    weights = join(1 - core, others, weights)
    return (new[0][None], new[1][None], new[2][None], weights[None], rms[0, 0])


def solution(mesh):
    ring = mesh.shape["dp"] // math.prod(PLANE_SHAPE)
    devices = mesh.devices.reshape(ring, *PLANE_SHAPE, mesh.shape["layer"])
    split_mesh = Mesh(devices, (RING, *PLANE, "layer"))
    dp = (RING, *PLANE)
    in_specs = (
        P("layer", dp, None, None),
        P("layer", dp, None, None),
        P("layer", dp, None, None),
        P("layer", dp, None, None),
        P("layer", None),
        P("layer", None),
    )
    out_specs = (
        P("layer", dp, None, None),
        P("layer", dp, None, None),
        P("layer", dp, None, None),
        P("layer", None, None),
        P(),
    )
    return jax.shard_map(
        shards, mesh=split_mesh, in_specs=in_specs, out_specs=out_specs, check_vma=False
    )
```

```python
import math

import jax
import jax.numpy as jnp
from jax import lax
from jax.experimental import pallas as pl
from jax.experimental.pallas import tpu as pltpu
from jax.sharding import Mesh
from jax.sharding import PartitionSpec as P

beta_one = 0.9
beta_two = 0.95
learn_rate = 0.0003
decay_rate = 0.1
adam_eps = 1e-08
step_number = 100.0

RING = ("z", "side")
SIDES = 2
PLANE = ("pair", "x", "c")
PLANE_SHAPE = (2, 4, 2)
FORM = ("side", "pair", "x")
SLOT_ROWS = 8
KINDS = 4


def adamw(param, first, second, grad):
    first_new = beta_one * first + (1.0 - beta_one) * grad
    second_new = beta_two * second + (1.0 - beta_two) * grad * grad
    corr_one = 1.0 - beta_one**step_number
    corr_two = 1.0 - beta_two**step_number
    update = (
        first_new / corr_one / (jnp.sqrt(second_new / corr_two) + adam_eps) + decay_rate * param
    )
    return (param - learn_rate * update, first_new, second_new)


def exchange(chunks, axis):
    return lax.all_to_all(chunks, axis, 0, 0, tiled=True)


def two_terms(value):
    high = value.astype(jnp.bfloat16)
    return high, (value - high.astype(jnp.float32)).astype(jnp.bfloat16)


def choose(matrix, values):
    return jnp.dot(matrix, values, preferred_element_type=jnp.float32)


VMEM = pl.BlockSpec(memory_space=pltpu.VMEM)
SMEM = pl.BlockSpec(memory_space=pltpu.SMEM)
ANY = pl.BlockSpec(memory_space=pl.ANY)


def near(value):
    return pltpu.with_memory_space_constraint(value, pltpu.VMEM)


def fill_rows(rows, states):
    capacity, slab, _ = states[0].shape
    for i, state in enumerate(states):
        for s in range(capacity):
            rows[i, s * slab : (s + 1) * slab, :] = state[s]
        rows[i, capacity * slab :, :] = jnp.ones_like(rows[i, capacity * slab :, :])


def split_kernel(grads, master, first, second, out, rows):
    plane, _, wide = out.shape
    count = grads.shape[0]
    for k in range(plane):
        out[k, :count, :] = grads[:, k * wide : (k + 1) * wide]
    fill_rows(rows, (master, first, second))
    high, low = two_terms(rows[0])
    values = (high, low, rows[1].astype(jnp.bfloat16), rows[2].astype(jnp.bfloat16))
    for t, value in enumerate(values):
        at = count + t * SLOT_ROWS
        for k in range(plane):
            out[k, at : at + SLOT_ROWS, :] = value[:, k * wide : (k + 1) * wide]


def split(grads, master, first, second, plane):
    count, width = grads.shape
    shape = (plane, count + KINDS * SLOT_ROWS, width // plane)
    return pl.pallas_call(
        split_kernel,
        out_shape=jax.ShapeDtypeStruct(shape, grads.dtype),
        in_specs=[VMEM] * 4,
        out_specs=VMEM,
        scratch_shapes=[pltpu.VMEM((3, SLOT_ROWS, width), jnp.float32)],
        name="split",
    )(grads, master, first, second)


def join_kernel(core, strips, place, *refs):
    out, placed, sem = refs[-3:]
    count, _, wide = placed.shape
    moves = []
    for i in range(count):
        rows = jnp.concatenate([strips[side * count + i] for side in range(SIDES)], axis=0)
        placed[i] = choose(place[...], rows).astype(placed.dtype)
        lane = pl.multiple_of((2 * i + core[0]) * wide, wide)
        moves.append(pltpu.make_async_copy(placed.at[i], out.at[:, pl.ds(lane, wide)], sem.at[i]))
        moves[-1].start()
    for move in moves:
        move.wait()


def join(core, strips, place, *before):
    count, wide = strips.shape[0] // SIDES, strips.shape[2]
    rows = place.shape[0]
    return pl.pallas_call(
        join_kernel,
        out_shape=jax.ShapeDtypeStruct((rows, 2 * count * wide), strips.dtype),
        in_specs=[SMEM, VMEM, VMEM] + [ANY] * len(before),
        out_specs=ANY,
        scratch_shapes=[
            pltpu.VMEM((count, rows, wide), strips.dtype),
            pltpu.SemaphoreType.DMA((count,)),
        ],
        input_output_aliases={3: 0} if before else {},
        name="join",
    )(core.reshape(1), near(strips), place, *before)


def own_kernel(at, got, rms, master, first, second, *refs):
    outs, rows, grads = refs[:3], refs[3], refs[4]
    wide = got.shape[2]
    count = grads.shape[1] // wide
    layers = got.shape[0] // count
    for k in range(count):
        grads[:, k * wide : (k + 1) * wide] = got[k * layers + at[0]]
    fill_rows(rows, (master, first, second))
    clip_factor = jnp.minimum(1.0, 1.0 / rms[:, :1])
    new = adamw(rows[0], rows[1], rows[2], grads[...] * clip_factor)
    capacity, slab, _ = master.shape
    for i, (out, old) in enumerate(zip(outs, (master, first, second), strict=True)):
        rows[i] = new[i]
        for s in range(capacity):
            out[s] = jnp.where(at[1 + s] > 0, rows[i, s * slab : (s + 1) * slab, :], old[s])


def pack_kernel(raw, order, route, out):
    plane, count, _ = raw.shape
    ring = out.shape[0]
    rows = order.shape[0]
    part = rows // ring
    total = raw[0, :rows, :].astype(jnp.float32)
    for j in range(1, plane):
        total = total + raw[j, :rows, :].astype(jnp.float32)
    lines = [
        raw[j, at : at + SLOT_ROWS, :] for at in range(rows, count, SLOT_ROWS) for j in range(plane)
    ]
    high, low = two_terms(total)
    sources = ((order, high), (order, low), (route, jnp.concatenate(lines, axis=0)))
    for i, (matrix, source) in enumerate(sources):
        chosen = choose(matrix[...], source).astype(out.dtype)
        size = chosen.shape[0] // ring
        for z in range(ring):
            out[z, i * part : i * part + size, :] = chosen[z * size : (z + 1) * size, :]


def reduce_kernel(got, take, out):
    ring = got.shape[0]
    part = take.shape[0] // KINDS
    half = part // SIDES
    total = got[0, :part, :].astype(jnp.float32) + got[0, part : 2 * part, :].astype(jnp.float32)
    for z in range(1, ring):
        total = total + (
            got[z, :part, :].astype(jnp.float32) + got[z, part : 2 * part, :].astype(jnp.float32)
        )
    high, low = two_terms(total)
    lines = jnp.concatenate([got[z, 2 * part :, :] for z in range(ring)], axis=0)
    lines = choose(take[...], lines).astype(out.dtype)
    for z in range(ring):
        out[z, :part, :] = high
        out[z, part : 2 * part, :] = low
        for t in range(KINDS):
            at = t * part + z % SIDES * half
            to = 2 * part + t * half
            out[z, to : to + half, :] = lines[at : at + half, :]


def ordered(every, term, part):
    return jnp.concatenate(
        [every[z, term * part : (term + 1) * part, :] for z in range(every.shape[0])], axis=0
    )


def send_kernel(every, pick, out):
    plane, layers, _, wide = out.shape
    part = pick.shape[1] // every.shape[0]
    high, low = ordered(every, 0, part), ordered(every, 1, part)
    total = high.astype(jnp.float32) + low.astype(jnp.float32)
    squares = jnp.sum(total * total)
    sent = choose(pick[...], high) + choose(pick[...], low)
    line = lax.broadcasted_iota(jnp.int32, sent.shape, 0)
    sent = jnp.where(line % SLOT_ROWS == SLOT_ROWS - 1, squares, sent)
    for j in range(plane):
        for layer in range(layers):
            out[j, layer] = sent[j * SLOT_ROWS : (j + 1) * SLOT_ROWS, :]


def step_kernel(element_total, side, every, got, copies, rms):
    ring = every.shape[0]
    half = copies.shape[1] // ring
    part = half * SIDES
    squares = jnp.sum(got[...], axis=0)[SLOT_ROWS - 1 :, :]
    grad_rms = jnp.sqrt(squares / element_total + 1e-06)
    rms[...] = grad_rms
    clip_factor = jnp.minimum(1.0, 1.0 / grad_rms)

    def stack(at):
        rows = [every[z, pl.ds(at, half), :] for z in range(ring)]
        return jnp.concatenate(rows, axis=0).astype(jnp.float32)

    mine = pl.multiple_of(side[0] * half, half)
    grad = (stack(mine) + stack(pl.multiple_of(part + mine, half))) * clip_factor
    terms = [stack(2 * part + t * half) for t in range(KINDS)]
    param = adamw(terms[0] + terms[1], terms[2], terms[3], grad)[0].astype(copies.dtype)
    for i in range(copies.shape[0]):
        copies[i] = param


def shards(micro_grads, master, moment_one, moment_two, owner, slot):
    rows, width = micro_grads.shape[2:]
    capacity, slab = master.shape[1:3]
    ring = lax.axis_size(RING)
    plane = lax.axis_size(PLANE)
    lines = capacity * slab
    wide = width // plane
    layers = lax.axis_size("layer")
    my_z = lax.axis_index(RING)
    part = rows // ring
    plane_lines = plane * SLOT_ROWS
    bf16, f32, i32 = jnp.bfloat16, jnp.float32, jnp.int32
    count = jnp.arange(rows, dtype=i32)
    few = jnp.arange(plane_lines, dtype=i32)

    deal = -(-plane * capacity // ring)
    pair = deal * slab
    home = owner[0] * capacity + slot[0]
    rank = jnp.sum((home[None, :] < home[:, None]).astype(i32), axis=1)
    line = owner[0] * SLOT_ROWS + slot[0] * slab
    member, turn = rank % ring, rank // ring

    def per_row(value):
        return (value[:, None] + jnp.arange(slab, dtype=i32)[None, :]).reshape(rows)

    line_of = per_row(line)
    dealt = per_row(member * part + turn * slab)
    pair_of = per_row(member * pair + turn % deal * slab)
    order = dealt[None, :] == count[:, None]
    half = part // SIDES
    formed = dealt % part // half * (rows // SIDES) + dealt // part * half + dealt % half
    place = formed[:, None] == count[None, :]
    line_at = jnp.sum(jnp.where(order, line_of[None, :], 0), axis=1)
    pick = (my_z * plane_lines + few)[:, None] == line_at[None, :]
    mine = line_of[None, :] == (my_z * plane_lines + few)[:, None]
    pair_at = jnp.sum(jnp.where(mine, pair_of[None, :] + 1, 0), axis=1) - 1
    kind = jnp.arange(KINDS, dtype=i32)[:, None]
    goes = jnp.where(pair_at < 0, -1, pair_at)[None, :]
    goes = jnp.where(goes < 0, -1, (goes // pair * KINDS + kind) * pair + goes % pair)
    chunks = jnp.arange(ring * KINDS * pair, dtype=i32)
    route = goes.reshape(1, KINDS * plane_lines) == chunks[:, None]
    own_line = lax.dynamic_slice_in_dim(line_at, my_z * part, part)
    within = jnp.arange(part, dtype=i32) % pair
    comes = (own_line // plane_lines * KINDS + kind) * pair + within[None, :]
    take = comes.reshape(KINDS * part, 1) == chunks[None, :]

    raw = exchange(split(micro_grads[0, 0], master[0], moment_one[0], moment_two[0], plane), PLANE)
    my_slots = lax.axis_index((*RING, *PLANE)) * SLOT_ROWS
    my_slots = my_slots + slab * jnp.arange(capacity, dtype=i32)
    keep = jnp.any(line[None, :] == my_slots[:, None], axis=1).astype(i32)
    at = jnp.concatenate([lax.axis_index("layer").astype(i32).reshape(1), keep])
    tables = [t.astype(bf16) for t in (order, route, take, pick, place)]
    raw, at, *tables = lax.optimization_barrier((raw, at, *tables))
    order, route, take, pick, place = [near(t) for t in tables]
    packed = pl.pallas_call(
        pack_kernel,
        out_shape=pltpu.VMEM((ring, 2 * part + KINDS * pair, wide), bf16),
        in_specs=[VMEM] * 3,
        out_specs=VMEM,
        name="pack",
    )(near(raw), order, route)
    reduced = pl.pallas_call(
        reduce_kernel,
        out_shape=pltpu.VMEM((ring, 2 * part + KINDS * part // SIDES, wide), bf16),
        in_specs=[VMEM] * 2,
        out_specs=VMEM,
        name="reduce",
    )(near(exchange(packed, RING)), take)
    every = exchange(reduced, RING)

    sent = pl.pallas_call(
        send_kernel,
        out_shape=pltpu.VMEM((plane, layers, SLOT_ROWS, wide), f32),
        in_specs=[VMEM] * 2,
        out_specs=VMEM,
        name="send",
    )(near(every), pick)
    got = exchange(sent.reshape(plane * layers, SLOT_ROWS, wide), (*PLANE, "layer"))

    copies, rms = pl.pallas_call(
        lambda *refs: step_kernel(float(layers * rows * width), *refs),
        out_shape=(
            pltpu.VMEM((lax.axis_size(FORM), rows // SIDES, wide), bf16),
            jax.ShapeDtypeStruct((1, wide), f32),
        ),
        in_specs=[SMEM] + [VMEM] * 2,
        out_specs=(VMEM, VMEM),
        name="step",
    )(lax.axis_index("side").astype(i32).reshape(1), near(every), near(got))
    core = lax.axis_index("c")
    halves, got, rms = lax.optimization_barrier((exchange(copies, FORM), got, rms))
    others = lax.ppermute(halves, "c", [(0, 1), (1, 0)])
    weights = join(core, halves, place)

    new = pl.pallas_call(
        own_kernel,
        out_shape=(jax.ShapeDtypeStruct(master.shape[1:], f32),) * 3,
        in_specs=[SMEM] + [VMEM] * 5,
        out_specs=(VMEM,) * 3,
        scratch_shapes=[
            pltpu.VMEM((3, SLOT_ROWS, width), f32),
            pltpu.VMEM((SLOT_ROWS, width), f32),
        ],
        name="own",
    )(at, near(got), near(rms), *[near(o[0]) for o in (master, moment_one, moment_two)])
    others, weights = lax.optimization_barrier((others, weights))
    weights = join(1 - core, others, place, weights)
    return (new[0][None], new[1][None], new[2][None], weights[None], rms[0, 0])


def solution(mesh):
    ring = mesh.shape["dp"] // math.prod(PLANE_SHAPE)
    devices = mesh.devices.reshape(ring // SIDES, SIDES, *PLANE_SHAPE, mesh.shape["layer"])
    split_mesh = Mesh(devices, (*RING, *PLANE, "layer"))
    dp = (*RING, *PLANE)
    in_specs = (
        P("layer", dp, None, None),
        P("layer", dp, None, None),
        P("layer", dp, None, None),
        P("layer", dp, None, None),
        P("layer", None),
        P("layer", None),
    )
    out_specs = (
        P("layer", dp, None, None),
        P("layer", dp, None, None),
        P("layer", dp, None, None),
        P("layer", None, None),
        P(),
    )
    return jax.shard_map(
        shards, mesh=split_mesh, in_specs=in_specs, out_specs=out_specs, check_vma=False
    )
```

```python
import math

import jax
import jax.numpy as jnp
from jax import lax
from jax.experimental import pallas as pl
from jax.experimental.pallas import tpu as pltpu
from jax.sharding import Mesh
from jax.sharding import PartitionSpec as P

beta_one = 0.9
beta_two = 0.95
learn_rate = 0.0003
decay_rate = 0.1
adam_eps = 1e-08
step_number = 100.0

RING = "z"
PLANE = ("pair", "x", "c")
PLANE_SHAPE = (2, 4, 2)
HALF = ("pair", "x")
SLOT_ROWS = 8
KINDS = 4


def adamw(param, first, second, grad):
    first_new = beta_one * first + (1.0 - beta_one) * grad
    second_new = beta_two * second + (1.0 - beta_two) * grad * grad
    corr_one = 1.0 - beta_one**step_number
    corr_two = 1.0 - beta_two**step_number
    update = (
        first_new / corr_one / (jnp.sqrt(second_new / corr_two) + adam_eps) + decay_rate * param
    )
    return (param - learn_rate * update, first_new, second_new)


def exchange(chunks, axis):
    return lax.all_to_all(chunks, axis, 0, 0, tiled=True)


def two_terms(value):
    high = value.astype(jnp.bfloat16)
    return high, (value - high.astype(jnp.float32)).astype(jnp.bfloat16)


def choose(matrix, values):
    return jnp.dot(matrix, values, preferred_element_type=jnp.float32)


VMEM = pl.BlockSpec(memory_space=pltpu.VMEM)
SMEM = pl.BlockSpec(memory_space=pltpu.SMEM)
ANY = pl.BlockSpec(memory_space=pl.ANY)


def near(value):
    return pltpu.with_memory_space_constraint(value, pltpu.VMEM)


def fill_rows(rows, states):
    capacity, slab, _ = states[0].shape
    for i, state in enumerate(states):
        for s in range(capacity):
            rows[i, s * slab : (s + 1) * slab, :] = state[s]
        rows[i, capacity * slab :, :] = jnp.ones_like(rows[i, capacity * slab :, :])


def split_kernel(grads, master, first, second, out, rows):
    plane, _, wide = out.shape
    count = grads.shape[0]
    for k in range(plane):
        out[k, :count, :] = grads[:, k * wide : (k + 1) * wide]
    fill_rows(rows, (master, first, second))
    high, low = two_terms(rows[0])
    values = (high, low, rows[1].astype(jnp.bfloat16), rows[2].astype(jnp.bfloat16))
    for t, value in enumerate(values):
        at = count + t * SLOT_ROWS
        for k in range(plane):
            out[k, at : at + SLOT_ROWS, :] = value[:, k * wide : (k + 1) * wide]


def split(grads, master, first, second, plane):
    count, width = grads.shape
    shape = (plane, count + KINDS * SLOT_ROWS, width // plane)
    return pl.pallas_call(
        split_kernel,
        out_shape=jax.ShapeDtypeStruct(shape, grads.dtype),
        in_specs=[VMEM] * 4,
        out_specs=VMEM,
        scratch_shapes=[pltpu.VMEM((3, SLOT_ROWS, width), jnp.float32)],
        name="split",
    )(grads, master, first, second)


def join_kernel(core, strips, *refs):
    out, sem = refs[-2:]
    count, _, wide = strips.shape
    moves = [
        pltpu.make_async_copy(
            strips.at[i],
            out.at[:, pl.ds(pl.multiple_of((2 * i + core[0]) * wide, wide), wide)],
            sem.at[i],
        )
        for i in range(count)
    ]
    for move in moves:
        move.start()
    for move in moves:
        move.wait()


def join(core, strips, *before):
    count, rows, wide = strips.shape
    return pl.pallas_call(
        join_kernel,
        out_shape=jax.ShapeDtypeStruct((rows, 2 * count * wide), strips.dtype),
        in_specs=[SMEM, VMEM] + [ANY] * len(before),
        out_specs=ANY,
        scratch_shapes=[pltpu.SemaphoreType.DMA((count,))],
        input_output_aliases={2: 0} if before else {},
        name="join",
    )(core.reshape(1), near(strips), *before)


def own_kernel(at, got, rms, master, first, second, *refs):
    outs, rows, grads = refs[:3], refs[3], refs[4]
    wide = got.shape[2]
    count = grads.shape[1] // wide
    layers = got.shape[0] // count
    for k in range(count):
        grads[:, k * wide : (k + 1) * wide] = got[k * layers + at[0]]
    fill_rows(rows, (master, first, second))
    clip_factor = jnp.minimum(1.0, 1.0 / rms[:, :1])
    new = adamw(rows[0], rows[1], rows[2], grads[...] * clip_factor)
    capacity, slab, _ = master.shape
    for i, (out, old) in enumerate(zip(outs, (master, first, second), strict=True)):
        rows[i] = new[i]
        for s in range(capacity):
            out[s] = jnp.where(at[1 + s] > 0, rows[i, s * slab : (s + 1) * slab, :], old[s])


def pack_kernel(raw, order, route, out):
    plane, count, _ = raw.shape
    ring = out.shape[0]
    rows = order.shape[0]
    part = rows // ring
    total = raw[0, :rows, :].astype(jnp.float32)
    for j in range(1, plane):
        total = total + raw[j, :rows, :].astype(jnp.float32)
    lines = [
        raw[j, at : at + SLOT_ROWS, :] for at in range(rows, count, SLOT_ROWS) for j in range(plane)
    ]
    high, low = two_terms(total)
    sources = ((order, high), (order, low), (route, jnp.concatenate(lines, axis=0)))
    for i, (matrix, source) in enumerate(sources):
        chosen = choose(matrix[...], source).astype(out.dtype)
        size = chosen.shape[0] // ring
        for z in range(ring):
            out[z, i * part : i * part + size, :] = chosen[z * size : (z + 1) * size, :]


def reduce_kernel(got, take, out):
    ring = got.shape[0]
    part = out.shape[1] // (2 + KINDS)
    total = got[0, :part, :].astype(jnp.float32) + got[0, part : 2 * part, :].astype(jnp.float32)
    for z in range(1, ring):
        total = total + (
            got[z, :part, :].astype(jnp.float32) + got[z, part : 2 * part, :].astype(jnp.float32)
        )
    high, low = two_terms(total)
    lines = jnp.concatenate([got[z, 2 * part :, :] for z in range(ring)], axis=0)
    lines = choose(take[...], lines).astype(out.dtype)
    for z in range(ring):
        out[z, :part, :] = high
        out[z, part : 2 * part, :] = low
        out[z, 2 * part :, :] = lines


def ordered(every, term, part):
    return jnp.concatenate(
        [every[z, term * part : (term + 1) * part, :] for z in range(every.shape[0])], axis=0
    )


def send_kernel(every, pick, out):
    plane, layers, _, wide = out.shape
    part = pick.shape[1] // every.shape[0]
    high, low = ordered(every, 0, part), ordered(every, 1, part)
    total = high.astype(jnp.float32) + low.astype(jnp.float32)
    squares = jnp.sum(total * total)
    sent = choose(pick[...], high) + choose(pick[...], low)
    line = lax.broadcasted_iota(jnp.int32, sent.shape, 0)
    sent = jnp.where(line % SLOT_ROWS == SLOT_ROWS - 1, squares, sent)
    for j in range(plane):
        for layer in range(layers):
            out[j, layer] = sent[j * SLOT_ROWS : (j + 1) * SLOT_ROWS, :]


def step_kernel(element_total, every, got, place, copies, rms):
    part = place.shape[1] // every.shape[0]
    squares = jnp.sum(got[...], axis=0)[SLOT_ROWS - 1 :, :]
    grad_rms = jnp.sqrt(squares / element_total + 1e-06)
    rms[...] = grad_rms
    clip_factor = jnp.minimum(1.0, 1.0 / grad_rms)
    terms = [ordered(every, t, part).astype(jnp.float32) for t in range(2 + KINDS)]
    grad = (terms[0] + terms[1]) * clip_factor
    param = adamw(terms[2] + terms[3], terms[4], terms[5], grad)[0]
    weights = choose(place[...], param.astype(copies.dtype)).astype(copies.dtype)
    for x in range(copies.shape[0]):
        copies[x] = weights


def shards(micro_grads, master, moment_one, moment_two, owner, slot):
    rows, width = micro_grads.shape[2:]
    capacity, slab = master.shape[1:3]
    ring = lax.axis_size(RING)
    plane = lax.axis_size(PLANE)
    lines = capacity * slab
    wide = width // plane
    layers = lax.axis_size("layer")
    my_z = lax.axis_index(RING)
    part = rows // ring
    plane_lines = plane * SLOT_ROWS
    bf16, f32, i32 = jnp.bfloat16, jnp.float32, jnp.int32
    count = jnp.arange(rows, dtype=i32)
    few = jnp.arange(plane_lines, dtype=i32)

    deal = -(-plane * capacity // ring)
    pair = deal * slab
    home = owner[0] * capacity + slot[0]
    rank = jnp.sum((home[None, :] < home[:, None]).astype(i32), axis=1)
    line = owner[0] * SLOT_ROWS + slot[0] * slab
    member, turn = rank % ring, rank // ring

    def per_row(value):
        return (value[:, None] + jnp.arange(slab, dtype=i32)[None, :]).reshape(rows)

    line_of = per_row(line)
    dealt = per_row(member * part + turn * slab)
    pair_of = per_row(member * pair + turn % deal * slab)
    order = dealt[None, :] == count[:, None]
    place = dealt[:, None] == count[None, :]
    line_at = jnp.sum(jnp.where(order, line_of[None, :], 0), axis=1)
    pick = (my_z * plane_lines + few)[:, None] == line_at[None, :]
    mine = line_of[None, :] == (my_z * plane_lines + few)[:, None]
    pair_at = jnp.sum(jnp.where(mine, pair_of[None, :] + 1, 0), axis=1) - 1
    kind = jnp.arange(KINDS, dtype=i32)[:, None]
    goes = jnp.where(pair_at < 0, -1, pair_at)[None, :]
    goes = jnp.where(goes < 0, -1, (goes // pair * KINDS + kind) * pair + goes % pair)
    chunks = jnp.arange(ring * KINDS * pair, dtype=i32)
    route = goes.reshape(1, KINDS * plane_lines) == chunks[:, None]
    own_line = lax.dynamic_slice_in_dim(line_at, my_z * part, part)
    within = jnp.arange(part, dtype=i32) % pair
    comes = (own_line // plane_lines * KINDS + kind) * pair + within[None, :]
    take = comes.reshape(KINDS * part, 1) == chunks[None, :]

    raw = exchange(split(micro_grads[0, 0], master[0], moment_one[0], moment_two[0], plane), PLANE)
    my_slots = lax.axis_index((RING, *PLANE)) * SLOT_ROWS
    my_slots = my_slots + slab * jnp.arange(capacity, dtype=i32)
    keep = jnp.any(line[None, :] == my_slots[:, None], axis=1).astype(i32)
    at = jnp.concatenate([lax.axis_index("layer").astype(i32).reshape(1), keep])
    tables = [t.astype(bf16) for t in (order, route, take, pick, place)]
    raw, at, *tables = lax.optimization_barrier((raw, at, *tables))
    order, route, take, pick, place = [near(t) for t in tables]
    packed = pl.pallas_call(
        pack_kernel,
        out_shape=pltpu.VMEM((ring, 2 * part + KINDS * pair, wide), bf16),
        in_specs=[VMEM] * 3,
        out_specs=VMEM,
        name="pack",
    )(near(raw), order, route)
    reduced = pl.pallas_call(
        reduce_kernel,
        out_shape=pltpu.VMEM((ring, (2 + KINDS) * part, wide), bf16),
        in_specs=[VMEM] * 2,
        out_specs=VMEM,
        name="reduce",
    )(near(exchange(packed, RING)), take)
    every = exchange(reduced, RING)

    sent = pl.pallas_call(
        send_kernel,
        out_shape=pltpu.VMEM((plane, layers, SLOT_ROWS, wide), f32),
        in_specs=[VMEM] * 2,
        out_specs=VMEM,
        name="send",
    )(near(every), pick)
    got = exchange(sent.reshape(plane * layers, SLOT_ROWS, wide), (*PLANE, "layer"))

    copies, rms = pl.pallas_call(
        lambda *refs: step_kernel(float(layers * rows * width), *refs),
        out_shape=(
            pltpu.VMEM((lax.axis_size(HALF), rows, wide), bf16),
            jax.ShapeDtypeStruct((1, wide), f32),
        ),
        in_specs=[VMEM] * 3,
        out_specs=(VMEM, VMEM),
        name="step",
    )(near(every), near(got), place)
    core = lax.axis_index("c")
    halves, got, rms = lax.optimization_barrier((exchange(copies, HALF), got, rms))
    others = lax.ppermute(halves, "c", [(0, 1), (1, 0)])
    weights = join(core, halves)

    new = pl.pallas_call(
        own_kernel,
        out_shape=(jax.ShapeDtypeStruct(master.shape[1:], f32),) * 3,
        in_specs=[SMEM] + [VMEM] * 5,
        out_specs=(VMEM,) * 3,
        scratch_shapes=[
            pltpu.VMEM((3, SLOT_ROWS, width), f32),
            pltpu.VMEM((SLOT_ROWS, width), f32),
        ],
        name="own",
    )(at, near(got), near(rms), *[near(o[0]) for o in (master, moment_one, moment_two)])
    others, weights = lax.optimization_barrier((others, weights))
    weights = join(1 - core, others, weights)
    return (new[0][None], new[1][None], new[2][None], weights[None], rms[0, 0])


def solution(mesh):
    ring = mesh.shape["dp"] // math.prod(PLANE_SHAPE)
    devices = mesh.devices.reshape(ring, *PLANE_SHAPE, mesh.shape["layer"])
    split_mesh = Mesh(devices, (RING, *PLANE, "layer"))
    dp = (RING, *PLANE)
    in_specs = (
        P("layer", dp, None, None),
        P("layer", dp, None, None),
        P("layer", dp, None, None),
        P("layer", dp, None, None),
        P("layer", None),
        P("layer", None),
    )
    out_specs = (
        P("layer", dp, None, None),
        P("layer", dp, None, None),
        P("layer", dp, None, None),
        P("layer", None, None),
        P(),
    )
    return jax.shard_map(
        shards, mesh=split_mesh, in_specs=in_specs, out_specs=out_specs, check_vma=False
    )
```

```python
import math

import jax
import jax.numpy as jnp
from jax import lax
from jax.experimental import pallas as pl
from jax.experimental.pallas import tpu as pltpu
from jax.sharding import Mesh
from jax.sharding import PartitionSpec as P

beta_one = 0.9
beta_two = 0.95
learn_rate = 0.0003
decay_rate = 0.1
adam_eps = 1e-08
step_number = 100.0

RING = "z"
PLANE = ("pair", "x", "c")
PLANE_SHAPE = (2, 4, 2)
HALF = ("pair", "x")
SLOT_ROWS = 8
KINDS = 4
EXTRA = 4


def adamw(param, first, second, grad):
    first_new = beta_one * first + (1.0 - beta_one) * grad
    second_new = beta_two * second + (1.0 - beta_two) * grad * grad
    corr_one = 1.0 - beta_one**step_number
    corr_two = 1.0 - beta_two**step_number
    update = (
        first_new / corr_one / (jnp.sqrt(second_new / corr_two) + adam_eps) + decay_rate * param
    )
    return (param - learn_rate * update, first_new, second_new)


def exchange(chunks, axis):
    return lax.all_to_all(chunks, axis, 0, 0, tiled=True)


def two_terms(value):
    high = value.astype(jnp.bfloat16)
    return high, (value - high.astype(jnp.float32)).astype(jnp.bfloat16)


def choose(matrix, values):
    return jnp.dot(matrix, values, preferred_element_type=jnp.float32)


VMEM = pl.BlockSpec(memory_space=pltpu.VMEM)
SMEM = pl.BlockSpec(memory_space=pltpu.SMEM)
ANY = pl.BlockSpec(memory_space=pl.ANY)


def near(value):
    return pltpu.with_memory_space_constraint(value, pltpu.VMEM)


def fill_rows(rows, states):
    capacity, slab, _ = states[0].shape
    for i, state in enumerate(states):
        for s in range(capacity):
            rows[i, s * slab : (s + 1) * slab, :] = state[s]
        rows[i, capacity * slab :, :] = jnp.ones_like(rows[i, capacity * slab :, :])


def split_kernel(grads, master, first, second, out, rows):
    plane, _, wide = out.shape
    count = grads.shape[0]
    for k in range(plane):
        out[k, :count, :] = grads[:, k * wide : (k + 1) * wide]
    fill_rows(rows, (master, first, second))
    high, low = two_terms(rows[0])
    values = (high, low, rows[1].astype(jnp.bfloat16), rows[2].astype(jnp.bfloat16))
    for t, value in enumerate(values):
        at = count + t * SLOT_ROWS
        for k in range(plane):
            out[k, at : at + SLOT_ROWS, :] = value[:, k * wide : (k + 1) * wide]


def split(grads, master, first, second, plane):
    count, width = grads.shape
    shape = (plane, count + KINDS * SLOT_ROWS, width // plane)
    return pl.pallas_call(
        split_kernel,
        out_shape=jax.ShapeDtypeStruct(shape, grads.dtype),
        in_specs=[VMEM] * 4,
        out_specs=VMEM,
        scratch_shapes=[pltpu.VMEM((3, SLOT_ROWS, width), jnp.float32)],
        name="split",
    )(grads, master, first, second)


def join_kernel(core, strips, *refs):
    out, sem = refs[-2:]
    count, _, wide = strips.shape
    moves = [
        pltpu.make_async_copy(
            strips.at[i],
            out.at[:, pl.ds(pl.multiple_of((2 * i + core[0]) * wide, wide), wide)],
            sem.at[i],
        )
        for i in range(count)
    ]
    for move in moves:
        move.start()
    for move in moves:
        move.wait()


def join(core, strips, *before):
    count, rows, wide = strips.shape
    return pl.pallas_call(
        join_kernel,
        out_shape=jax.ShapeDtypeStruct((rows, 2 * count * wide), strips.dtype),
        in_specs=[SMEM, VMEM] + [ANY] * len(before),
        out_specs=ANY,
        scratch_shapes=[pltpu.SemaphoreType.DMA((count,))],
        input_output_aliases={2: 0} if before else {},
        name="join",
    )(core.reshape(1), near(strips), *before)


def own_kernel(at, got, rms, master, first, second, *refs):
    outs, rows, grads = refs[:3], refs[3], refs[4]
    wide = got.shape[2]
    count = grads.shape[1] // wide
    layers = got.shape[0] // count
    for k in range(count):
        grads[:, k * wide : (k + 1) * wide] = got[k * layers + at[0]]
    fill_rows(rows, (master, first, second))
    clip_factor = jnp.minimum(1.0, 1.0 / rms[:, :1])
    new = adamw(rows[0], rows[1], rows[2], grads[...] * clip_factor)
    capacity, slab, _ = master.shape
    for i, (out, old) in enumerate(zip(outs, (master, first, second), strict=True)):
        rows[i] = new[i]
        for s in range(capacity):
            out[s] = jnp.where(at[1 + s] > 0, rows[i, s * slab : (s + 1) * slab, :], old[s])


def pack_kernel(raw, order, route, out):
    plane, count, _ = raw.shape
    ring = out.shape[0]
    rows = order.shape[0]
    part = rows // ring
    total = raw[0, :rows, :].astype(jnp.float32)
    for j in range(1, plane):
        total = total + raw[j, :rows, :].astype(jnp.float32)
    lines = [
        raw[j, at : at + SLOT_ROWS, :] for at in range(rows, count, SLOT_ROWS) for j in range(plane)
    ]
    high, low = two_terms(total)
    sources = ((order, high), (order, low), (route, jnp.concatenate(lines, axis=0)))
    for i, (matrix, source) in enumerate(sources):
        chosen = choose(matrix[...], source).astype(out.dtype)
        size = chosen.shape[0] // ring
        for z in range(ring):
            out[z, i * part : i * part + size, :] = chosen[z * size : (z + 1) * size, :]


def reduce_kernel(got, take, spread, out):
    ring = got.shape[0]
    part = take.shape[0] // KINDS
    extra = spread.shape[0] // ring
    total = got[0, :part, :].astype(jnp.float32) + got[0, part : 2 * part, :].astype(jnp.float32)
    for z in range(1, ring):
        total = total + (
            got[z, :part, :].astype(jnp.float32) + got[z, part : 2 * part, :].astype(jnp.float32)
        )
    high, low = two_terms(total)
    lows = choose(spread[...], low)
    squares = jnp.sum(total * total) + jnp.zeros((extra, total.shape[1]), jnp.float32)
    first, _ = two_terms(squares)
    second, _ = two_terms(squares - first.astype(jnp.float32))
    third = squares - first.astype(jnp.float32) - second.astype(jnp.float32)
    row = lax.broadcasted_iota(jnp.int32, squares.shape, 0)
    parts = (first.astype(jnp.float32), second.astype(jnp.float32), third)
    lines = jnp.concatenate([got[z, 2 * part :, :] for z in range(ring)], axis=0)
    lines = choose(take[...], lines).astype(out.dtype)
    for z in range(ring):
        block = lows[z * extra : (z + 1) * extra, :]
        for i, value in enumerate(parts):
            block = jnp.where(row == extra - EXTRA + i, value, block)
        out[z, :part, :] = high
        out[z, part : part + extra, :] = block.astype(out.dtype)
        out[z, part + extra :, :] = lines


def stack(every, at, size):
    return jnp.concatenate([every[z, at : at + size, :] for z in range(every.shape[0])], axis=0)


def send_kernel(every, pick, pick_low, out):
    plane, layers, _, wide = out.shape
    ring = every.shape[0]
    part, extra = pick.shape[1] // ring, pick_low.shape[1] // ring
    high, low = stack(every, 0, part), stack(every, part, extra)
    row = lax.broadcasted_iota(jnp.int32, low.shape, 0) % extra
    counted = (row >= extra - EXTRA) & (row < extra - EXTRA + 3)
    squares = jnp.where(counted, low.astype(jnp.float32), 0.0)
    squares = jnp.sum(squares, axis=0, keepdims=True)
    sent = choose(pick[...], high) + choose(pick_low[...], low)
    line = lax.broadcasted_iota(jnp.int32, sent.shape, 0)
    sent = jnp.where(line % SLOT_ROWS == SLOT_ROWS - 1, squares, sent)
    for j in range(plane):
        for layer in range(layers):
            out[j, layer] = sent[j * SLOT_ROWS : (j + 1) * SLOT_ROWS, :]


def step_kernel(element_total, every, got, place, copies, rms):
    part = place.shape[1] // every.shape[0]
    states = every.shape[1] - KINDS * part
    squares = jnp.sum(got[...], axis=0)[SLOT_ROWS - 1 :, :]
    grad_rms = jnp.sqrt(squares / element_total + 1e-06)
    rms[...] = grad_rms
    clip_factor = jnp.minimum(1.0, 1.0 / grad_rms)
    grad = stack(every, 0, part).astype(jnp.float32) * clip_factor
    terms = [stack(every, states + t * part, part).astype(jnp.float32) for t in range(KINDS)]
    param = adamw(terms[0] + terms[1], terms[2], terms[3], grad)[0]
    weights = choose(place[...], param.astype(copies.dtype)).astype(copies.dtype)
    for x in range(copies.shape[0]):
        copies[x] = weights


def shards(micro_grads, master, moment_one, moment_two, owner, slot):
    rows, width = micro_grads.shape[2:]
    capacity, slab = master.shape[1:3]
    ring = lax.axis_size(RING)
    plane = lax.axis_size(PLANE)
    lines = capacity * slab
    wide = width // plane
    layers = lax.axis_size("layer")
    my_z = lax.axis_index(RING)
    part = rows // ring
    plane_lines = plane * SLOT_ROWS
    bf16, f32, i32 = jnp.bfloat16, jnp.float32, jnp.int32
    count = jnp.arange(rows, dtype=i32)
    few = jnp.arange(plane_lines, dtype=i32)

    deal = -(-plane * capacity // ring)
    pair = deal * slab
    home = owner[0] * capacity + slot[0]
    rank = jnp.sum((home[None, :] < home[:, None]).astype(i32), axis=1)
    line = owner[0] * SLOT_ROWS + slot[0] * slab
    member, turn = rank % ring, rank // ring

    def per_row(value):
        return (value[:, None] + jnp.arange(slab, dtype=i32)[None, :]).reshape(rows)

    line_of = per_row(line)
    dealt = per_row(member * part + turn * slab)
    pair_of = per_row(member * pair + turn % deal * slab)
    order = dealt[None, :] == count[:, None]
    place = dealt[:, None] == count[None, :]
    line_at = jnp.sum(jnp.where(order, line_of[None, :], 0), axis=1)
    pick = (my_z * plane_lines + few)[:, None] == line_at[None, :]
    mine = line_of[None, :] == (my_z * plane_lines + few)[:, None]
    pair_at = jnp.sum(jnp.where(mine, pair_of[None, :] + 1, 0), axis=1) - 1
    kind = jnp.arange(KINDS, dtype=i32)[:, None]
    goes = jnp.where(pair_at < 0, -1, pair_at)[None, :]
    goes = jnp.where(goes < 0, -1, (goes // pair * KINDS + kind) * pair + goes % pair)
    chunks = jnp.arange(ring * KINDS * pair, dtype=i32)
    route = goes.reshape(1, KINDS * plane_lines) == chunks[:, None]
    own_line = lax.dynamic_slice_in_dim(line_at, my_z * part, part)
    within = jnp.arange(part, dtype=i32) % pair
    comes = (own_line // plane_lines * KINDS + kind) * pair + within[None, :]
    take = comes.reshape(KINDS * part, 1) == chunks[None, :]
    extra = pair + EXTRA
    special = jnp.arange(ring * extra, dtype=i32)
    spread = special[:, None] == (own_line // plane_lines * extra + within)[None, :]
    low_at = jnp.where(pair_at < 0, -1, pair_at // pair * extra + pair_at % pair)
    pick_low = low_at[:, None] == special[None, :]

    raw = exchange(split(micro_grads[0, 0], master[0], moment_one[0], moment_two[0], plane), PLANE)
    my_slots = lax.axis_index((RING, *PLANE)) * SLOT_ROWS
    my_slots = my_slots + slab * jnp.arange(capacity, dtype=i32)
    keep = jnp.any(line[None, :] == my_slots[:, None], axis=1).astype(i32)
    at = jnp.concatenate([lax.axis_index("layer").astype(i32).reshape(1), keep])
    tables = [t.astype(bf16) for t in (order, route, take, spread, pick, pick_low, place)]
    raw, at, *tables = lax.optimization_barrier((raw, at, *tables))
    order, route, take, spread, pick, pick_low, place = [near(t) for t in tables]
    packed = pl.pallas_call(
        pack_kernel,
        out_shape=pltpu.VMEM((ring, 2 * part + KINDS * pair, wide), bf16),
        in_specs=[VMEM] * 3,
        out_specs=VMEM,
        name="pack",
    )(near(raw), order, route)
    reduced = pl.pallas_call(
        reduce_kernel,
        out_shape=pltpu.VMEM((ring, (1 + KINDS) * part + extra, wide), bf16),
        in_specs=[VMEM] * 3,
        out_specs=VMEM,
        name="reduce",
    )(near(exchange(packed, RING)), take, spread)
    every = exchange(reduced, RING)

    sent = pl.pallas_call(
        send_kernel,
        out_shape=pltpu.VMEM((plane, layers, SLOT_ROWS, wide), f32),
        in_specs=[VMEM] * 3,
        out_specs=VMEM,
        name="send",
    )(near(every), pick, pick_low)
    got = exchange(sent.reshape(plane * layers, SLOT_ROWS, wide), (*PLANE, "layer"))

    copies, rms = pl.pallas_call(
        lambda *refs: step_kernel(float(layers * rows * width), *refs),
        out_shape=(
            pltpu.VMEM((lax.axis_size(HALF), rows, wide), bf16),
            jax.ShapeDtypeStruct((1, wide), f32),
        ),
        in_specs=[VMEM] * 3,
        out_specs=(VMEM, VMEM),
        name="step",
    )(near(every), near(got), place)
    core = lax.axis_index("c")
    halves, got, rms = lax.optimization_barrier((exchange(copies, HALF), got, rms))
    others = lax.ppermute(halves, "c", [(0, 1), (1, 0)])
    weights = join(core, halves)

    new = pl.pallas_call(
        own_kernel,
        out_shape=(jax.ShapeDtypeStruct(master.shape[1:], f32),) * 3,
        in_specs=[SMEM] + [VMEM] * 5,
        out_specs=(VMEM,) * 3,
        scratch_shapes=[
            pltpu.VMEM((3, SLOT_ROWS, width), f32),
            pltpu.VMEM((SLOT_ROWS, width), f32),
        ],
        name="own",
    )(at, near(got), near(rms), *[near(o[0]) for o in (master, moment_one, moment_two)])
    others, weights = lax.optimization_barrier((others, weights))
    weights = join(1 - core, others, weights)
    return (new[0][None], new[1][None], new[2][None], weights[None], rms[0, 0])


def solution(mesh):
    ring = mesh.shape["dp"] // math.prod(PLANE_SHAPE)
    devices = mesh.devices.reshape(ring, *PLANE_SHAPE, mesh.shape["layer"])
    split_mesh = Mesh(devices, (RING, *PLANE, "layer"))
    dp = (RING, *PLANE)
    in_specs = (
        P("layer", dp, None, None),
        P("layer", dp, None, None),
        P("layer", dp, None, None),
        P("layer", dp, None, None),
        P("layer", None),
        P("layer", None),
    )
    out_specs = (
        P("layer", dp, None, None),
        P("layer", dp, None, None),
        P("layer", dp, None, None),
        P("layer", None, None),
        P(),
    )
    return jax.shard_map(
        shards, mesh=split_mesh, in_specs=in_specs, out_specs=out_specs, check_vma=False
    )
```

```python
import math

import jax
import jax.numpy as jnp
from jax import lax
from jax.experimental import pallas as pl
from jax.experimental.pallas import tpu as pltpu
from jax.sharding import Mesh
from jax.sharding import PartitionSpec as P

beta_one = 0.9
beta_two = 0.95
learn_rate = 0.0003
decay_rate = 0.1
adam_eps = 1e-08
step_number = 100.0

RING = "z"
PLANE = ("pair", "x", "c")
PLANE_SHAPE = (2, 4, 2)
HALF = ("pair", "x")
SLOT_ROWS = 8
KINDS = 4
EXTRA = 4


def adamw(param, first, second, grad):
    first_new = beta_one * first + (1.0 - beta_one) * grad
    second_new = beta_two * second + (1.0 - beta_two) * grad * grad
    corr_one = 1.0 - beta_one**step_number
    corr_two = 1.0 - beta_two**step_number
    update = (
        first_new / corr_one / (jnp.sqrt(second_new / corr_two) + adam_eps) + decay_rate * param
    )
    return (param - learn_rate * update, first_new, second_new)


def exchange(chunks, axis):
    return lax.all_to_all(chunks, axis, 0, 0, tiled=True)


def two_terms(value):
    high = value.astype(jnp.bfloat16)
    return high, (value - high.astype(jnp.float32)).astype(jnp.bfloat16)


def choose(matrix, values):
    return jnp.dot(matrix, values, preferred_element_type=jnp.float32)


VMEM = pl.BlockSpec(memory_space=pltpu.VMEM)
SMEM = pl.BlockSpec(memory_space=pltpu.SMEM)
ANY = pl.BlockSpec(memory_space=pl.ANY)


def near(value):
    return pltpu.with_memory_space_constraint(value, pltpu.VMEM)


def fill_rows(rows, states):
    capacity, slab, _ = states[0].shape
    for i, state in enumerate(states):
        for s in range(capacity):
            rows[i, s * slab : (s + 1) * slab, :] = state[s]
        rows[i, capacity * slab :, :] = jnp.ones_like(rows[i, capacity * slab :, :])


def split_kernel(grads, master, first, second, out, rows, tight):
    plane, total, wide = out.shape
    count = grads.shape[0]
    lines = (total - count) // KINDS
    for k in range(plane):
        out[k, :count, :] = grads[:, k * wide : (k + 1) * wide]
    fill_rows(rows, (master, first, second))
    high, low = two_terms(rows[0])
    values = (high.astype(jnp.float32), low.astype(jnp.float32), rows[1], rows[2])
    for t, value in enumerate(values):
        tight[t * lines : (t + 1) * lines, :] = value[:lines]
    terms = tight[...].astype(jnp.bfloat16)
    for k in range(plane):
        out[k, count:, :] = terms[:, k * wide : (k + 1) * wide]


def split(grads, master, first, second, plane):
    count, width = grads.shape
    lines = KINDS * master.shape[0] * master.shape[1]
    return pl.pallas_call(
        split_kernel,
        out_shape=jax.ShapeDtypeStruct((plane, count + lines, width // plane), grads.dtype),
        in_specs=[VMEM] * 4,
        out_specs=VMEM,
        scratch_shapes=[
            pltpu.VMEM((3, SLOT_ROWS, width), jnp.float32),
            pltpu.VMEM((lines, width), jnp.float32),
        ],
        name="split",
    )(grads, master, first, second)


def join_kernel(core, strips, *refs):
    out, sem = refs[-2:]
    count, _, wide = strips.shape
    moves = [
        pltpu.make_async_copy(
            strips.at[i],
            out.at[:, pl.ds(pl.multiple_of((2 * i + core[0]) * wide, wide), wide)],
            sem.at[i],
        )
        for i in range(count)
    ]
    for move in moves:
        move.start()
    for move in moves:
        move.wait()


def join(core, strips, *before):
    count, rows, wide = strips.shape
    return pl.pallas_call(
        join_kernel,
        out_shape=jax.ShapeDtypeStruct((rows, 2 * count * wide), strips.dtype),
        in_specs=[SMEM, VMEM] + [ANY] * len(before),
        out_specs=ANY,
        scratch_shapes=[pltpu.SemaphoreType.DMA((count,))],
        input_output_aliases={2: 0} if before else {},
        name="join",
    )(core.reshape(1), near(strips), *before)


def own_kernel(at, got, rms, master, first, second, *refs):
    outs, rows, grads = refs[:3], refs[3], refs[4]
    wide = got.shape[2]
    count = grads.shape[1] // wide
    layers = got.shape[0] // count
    for k in range(count):
        grads[:, k * wide : (k + 1) * wide] = got[k * layers + at[0]]
    fill_rows(rows, (master, first, second))
    clip_factor = jnp.minimum(1.0, 1.0 / rms[:, :1])
    new = adamw(rows[0], rows[1], rows[2], grads[...] * clip_factor)
    capacity, slab, _ = master.shape
    for i, (out, old) in enumerate(zip(outs, (master, first, second), strict=True)):
        rows[i] = new[i]
        for s in range(capacity):
            out[s] = jnp.where(at[1 + s] > 0, rows[i, s * slab : (s + 1) * slab, :], old[s])


def pack_kernel(raw, order, route, out):
    plane = raw.shape[0]
    ring = out.shape[0]
    rows = order.shape[0]
    part = rows // ring
    total = raw[0, :rows, :].astype(jnp.float32)
    for j in range(1, plane):
        total = total + raw[j, :rows, :].astype(jnp.float32)
    lines = [raw[j, rows:, :] for j in range(plane)]
    high, low = two_terms(total)
    sources = ((order, high), (order, low), (route, jnp.concatenate(lines, axis=0)))
    for i, (matrix, source) in enumerate(sources):
        chosen = choose(matrix[...], source).astype(out.dtype)
        size = chosen.shape[0] // ring
        for z in range(ring):
            out[z, i * part : i * part + size, :] = chosen[z * size : (z + 1) * size, :]


def reduce_kernel(got, take, spread, out):
    ring = got.shape[0]
    part = take.shape[0] // KINDS
    extra = spread.shape[0] // ring
    total = got[0, :part, :].astype(jnp.float32) + got[0, part : 2 * part, :].astype(jnp.float32)
    for z in range(1, ring):
        total = total + (
            got[z, :part, :].astype(jnp.float32) + got[z, part : 2 * part, :].astype(jnp.float32)
        )
    high, low = two_terms(total)
    lows = choose(spread[...], low)
    squares = jnp.sum(total * total) + jnp.zeros((extra, total.shape[1]), jnp.float32)
    parts = []
    for _ in range(3):
        parts.append(squares.astype(jnp.bfloat16).astype(jnp.float32))
        squares = jnp.where(jnp.abs(parts[-1]) < jnp.inf, squares - parts[-1], 0.0)
    row = lax.broadcasted_iota(jnp.int32, squares.shape, 0)
    lines = jnp.concatenate([got[z, 2 * part :, :] for z in range(ring)], axis=0)
    lines = choose(take[...], lines).astype(out.dtype)
    for z in range(ring):
        block = lows[z * extra : (z + 1) * extra, :]
        for i, value in enumerate(parts):
            block = jnp.where(row == extra - EXTRA + i, value, block)
        out[z, :part, :] = high
        out[z, part : part + extra, :] = block.astype(out.dtype)
        out[z, part + extra :, :] = lines


def stack(every, at, size):
    return jnp.concatenate([every[z, at : at + size, :] for z in range(every.shape[0])], axis=0)


def send_kernel(every, pick, pick_low, out):
    plane, layers, _, wide = out.shape
    ring = every.shape[0]
    part, extra = pick.shape[1] // ring, pick_low.shape[1] // ring
    high, low = stack(every, 0, part), stack(every, part, extra)
    row = lax.broadcasted_iota(jnp.int32, low.shape, 0) % extra
    counted = (row >= extra - EXTRA) & (row < extra - EXTRA + 3)
    squares = jnp.where(counted, low.astype(jnp.float32), 0.0)
    squares = jnp.sum(squares, axis=0, keepdims=True)
    sent = choose(pick[...], high) + choose(pick_low[...], low)
    line = lax.broadcasted_iota(jnp.int32, sent.shape, 0)
    sent = jnp.where(line % SLOT_ROWS == SLOT_ROWS - 1, squares, sent)
    for j in range(plane):
        for layer in range(layers):
            out[j, layer] = sent[j * SLOT_ROWS : (j + 1) * SLOT_ROWS, :]


def step_kernel(element_total, every, got, place, copies, rms):
    part = place.shape[1] // every.shape[0]
    states = every.shape[1] - KINDS * part
    squares = jnp.sum(got[...], axis=0)[SLOT_ROWS - 1 :, :]
    grad_rms = jnp.sqrt(squares / element_total + 1e-06)
    rms[...] = grad_rms
    clip_factor = jnp.minimum(1.0, 1.0 / grad_rms)
    grad = stack(every, 0, part).astype(jnp.float32) * clip_factor
    terms = [stack(every, states + t * part, part).astype(jnp.float32) for t in range(KINDS)]
    param = adamw(terms[0] + terms[1], terms[2], terms[3], grad)[0]
    weights = choose(place[...], param.astype(copies.dtype)).astype(copies.dtype)
    for x in range(copies.shape[0]):
        copies[x] = weights


def shards(micro_grads, master, moment_one, moment_two, owner, slot):
    rows, width = micro_grads.shape[2:]
    capacity, slab = master.shape[1:3]
    ring = lax.axis_size(RING)
    plane = lax.axis_size(PLANE)
    lines = capacity * slab
    wide = width // plane
    layers = lax.axis_size("layer")
    my_z = lax.axis_index(RING)
    part = rows // ring
    plane_lines = plane * SLOT_ROWS
    bf16, f32, i32 = jnp.bfloat16, jnp.float32, jnp.int32
    count = jnp.arange(rows, dtype=i32)
    few = jnp.arange(plane_lines, dtype=i32)

    deal = -(-plane * capacity // ring)
    pair = deal * slab
    home = owner[0] * capacity + slot[0]
    rank = jnp.sum((home[None, :] < home[:, None]).astype(i32), axis=1)
    line = owner[0] * SLOT_ROWS + slot[0] * slab
    member, turn = rank % ring, rank // ring

    def per_row(value):
        return (value[:, None] + jnp.arange(slab, dtype=i32)[None, :]).reshape(rows)

    line_of = per_row(line)
    dealt = per_row(member * part + turn * slab)
    pair_of = per_row(member * pair + turn % deal * slab)
    order = dealt[None, :] == count[:, None]
    place = dealt[:, None] == count[None, :]
    line_at = jnp.sum(jnp.where(order, line_of[None, :], 0), axis=1)
    pick = (my_z * plane_lines + few)[:, None] == line_at[None, :]
    mine = line_of[None, :] == (my_z * plane_lines + few)[:, None]
    pair_at = jnp.sum(jnp.where(mine, pair_of[None, :] + 1, 0), axis=1) - 1
    kind = jnp.arange(KINDS, dtype=i32)[:, None]
    goes = jnp.where(pair_at < 0, -1, pair_at)[None, :]
    goes = jnp.where(goes < 0, -1, (goes // pair * KINDS + kind) * pair + goes % pair)
    chunks = jnp.arange(ring * KINDS * pair, dtype=i32)
    goes = goes.reshape(KINDS, plane, SLOT_ROWS)[:, :, :lines].transpose(1, 0, 2)
    route = goes.reshape(1, plane * KINDS * lines) == chunks[:, None]
    own_line = lax.dynamic_slice_in_dim(line_at, my_z * part, part)
    within = jnp.arange(part, dtype=i32) % pair
    comes = (own_line // plane_lines * KINDS + kind) * pair + within[None, :]
    take = comes.reshape(KINDS * part, 1) == chunks[None, :]
    extra = pair + EXTRA
    special = jnp.arange(ring * extra, dtype=i32)
    spread = special[:, None] == (own_line // plane_lines * extra + within)[None, :]
    low_at = jnp.where(pair_at < 0, -1, pair_at // pair * extra + pair_at % pair)
    pick_low = low_at[:, None] == special[None, :]

    raw = exchange(split(micro_grads[0, 0], master[0], moment_one[0], moment_two[0], plane), PLANE)
    my_slots = lax.axis_index((RING, *PLANE)) * SLOT_ROWS
    my_slots = my_slots + slab * jnp.arange(capacity, dtype=i32)
    keep = jnp.any(line[None, :] == my_slots[:, None], axis=1).astype(i32)
    at = jnp.concatenate([lax.axis_index("layer").astype(i32).reshape(1), keep])
    tables = [t.astype(bf16) for t in (order, route, take, spread, pick, pick_low, place)]
    raw, at, *tables = lax.optimization_barrier((raw, at, *tables))
    order, route, take, spread, pick, pick_low, place = [near(t) for t in tables]
    packed = pl.pallas_call(
        pack_kernel,
        out_shape=pltpu.VMEM((ring, 2 * part + KINDS * pair, wide), bf16),
        in_specs=[VMEM] * 3,
        out_specs=VMEM,
        name="pack",
    )(near(raw), order, route)
    reduced = pl.pallas_call(
        reduce_kernel,
        out_shape=pltpu.VMEM((ring, (1 + KINDS) * part + extra, wide), bf16),
        in_specs=[VMEM] * 3,
        out_specs=VMEM,
        name="reduce",
    )(near(exchange(packed, RING)), take, spread)
    every = exchange(reduced, RING)

    sent = pl.pallas_call(
        send_kernel,
        out_shape=pltpu.VMEM((plane, layers, SLOT_ROWS, wide), f32),
        in_specs=[VMEM] * 3,
        out_specs=VMEM,
        name="send",
    )(near(every), pick, pick_low)
    got = exchange(sent.reshape(plane * layers, SLOT_ROWS, wide), (*PLANE, "layer"))

    copies, rms = pl.pallas_call(
        lambda *refs: step_kernel(float(layers * rows * width), *refs),
        out_shape=(
            pltpu.VMEM((lax.axis_size(HALF), rows, wide), bf16),
            jax.ShapeDtypeStruct((1, wide), f32),
        ),
        in_specs=[VMEM] * 3,
        out_specs=(VMEM, VMEM),
        name="step",
    )(near(every), near(got), place)
    core = lax.axis_index("c")
    halves, got, rms = lax.optimization_barrier((exchange(copies, HALF), got, rms))
    others = lax.ppermute(halves, "c", [(0, 1), (1, 0)])
    weights = join(core, halves)

    new = pl.pallas_call(
        own_kernel,
        out_shape=(jax.ShapeDtypeStruct(master.shape[1:], f32),) * 3,
        in_specs=[SMEM] + [VMEM] * 5,
        out_specs=(VMEM,) * 3,
        scratch_shapes=[
            pltpu.VMEM((3, SLOT_ROWS, width), f32),
            pltpu.VMEM((SLOT_ROWS, width), f32),
        ],
        name="own",
    )(at, near(got), near(rms), *[near(o[0]) for o in (master, moment_one, moment_two)])
    others, weights = lax.optimization_barrier((others, weights))
    weights = join(1 - core, others, weights)
    return (new[0][None], new[1][None], new[2][None], weights[None], rms[0, 0])


def solution(mesh):
    ring = mesh.shape["dp"] // math.prod(PLANE_SHAPE)
    devices = mesh.devices.reshape(ring, *PLANE_SHAPE, mesh.shape["layer"])
    split_mesh = Mesh(devices, (RING, *PLANE, "layer"))
    dp = (RING, *PLANE)
    in_specs = (
        P("layer", dp, None, None),
        P("layer", dp, None, None),
        P("layer", dp, None, None),
        P("layer", dp, None, None),
        P("layer", None),
        P("layer", None),
    )
    out_specs = (
        P("layer", dp, None, None),
        P("layer", dp, None, None),
        P("layer", dp, None, None),
        P("layer", None, None),
        P(),
    )
    return jax.shard_map(
        shards, mesh=split_mesh, in_specs=in_specs, out_specs=out_specs, check_vma=False
    )
```

```python
import math

import jax
import jax.numpy as jnp
from jax import lax
from jax.experimental import pallas as pl
from jax.experimental.pallas import tpu as pltpu
from jax.sharding import Mesh
from jax.sharding import PartitionSpec as P

beta_one = 0.9
beta_two = 0.95
learn_rate = 0.0003
decay_rate = 0.1
adam_eps = 1e-08
step_number = 100.0

RING = "z"
PLANE = ("pair", "x", "c")
PLANE_SHAPE = (2, 4, 2)
HALF = ("pair", "x")
SLOT_ROWS = 8
KINDS = 4
EXTRA = 4


def adamw(param, first, second, grad):
    first_new = beta_one * first + (1.0 - beta_one) * grad
    second_new = beta_two * second + (1.0 - beta_two) * grad * grad
    corr_one = 1.0 - beta_one**step_number
    corr_two = 1.0 - beta_two**step_number
    update = (
        first_new / corr_one / (jnp.sqrt(second_new / corr_two) + adam_eps) + decay_rate * param
    )
    return (param - learn_rate * update, first_new, second_new)


def exchange(chunks, axis):
    return lax.all_to_all(chunks, axis, 0, 0, tiled=True)


def two_terms(value):
    high = value.astype(jnp.bfloat16)
    return high, (value - high.astype(jnp.float32)).astype(jnp.bfloat16)


def choose(matrix, values):
    return jnp.dot(matrix, values, preferred_element_type=jnp.float32)


VMEM = pl.BlockSpec(memory_space=pltpu.VMEM)
SMEM = pl.BlockSpec(memory_space=pltpu.SMEM)
ANY = pl.BlockSpec(memory_space=pl.ANY)


def near(value):
    return pltpu.with_memory_space_constraint(value, pltpu.VMEM)


def fill_rows(rows, states):
    capacity, slab, _ = states[0].shape
    for i, state in enumerate(states):
        for s in range(capacity):
            rows[i, s * slab : (s + 1) * slab, :] = state[s]
        rows[i, capacity * slab :, :] = jnp.ones_like(rows[i, capacity * slab :, :])


def split_kernel(grads, master, first, second, out, rows, tight):
    plane, total, wide = out.shape
    count = grads.shape[0]
    lines = (total - count) // KINDS
    for k in range(plane):
        out[k, :count, :] = grads[:, k * wide : (k + 1) * wide]
    fill_rows(rows, (master, first, second))
    high, low = two_terms(rows[0])
    values = (high.astype(jnp.float32), low.astype(jnp.float32), rows[1], rows[2])
    for t, value in enumerate(values):
        tight[t * lines : (t + 1) * lines, :] = value[:lines]
    terms = tight[...].astype(jnp.bfloat16)
    for k in range(plane):
        out[k, count:, :] = terms[:, k * wide : (k + 1) * wide]


def split(grads, master, first, second, plane):
    count, width = grads.shape
    capacity, slab, _ = master.shape
    lines = KINDS * capacity * slab
    steps = 2
    part = width // steps
    state = pl.BlockSpec((capacity, slab, part), lambda i: (0, 0, i))
    return pl.pallas_call(
        split_kernel,
        grid=(steps,),
        out_shape=jax.ShapeDtypeStruct((plane, count + lines, width // plane), grads.dtype),
        in_specs=[pl.BlockSpec((count, part), lambda i: (0, i)), state, state, state],
        out_specs=pl.BlockSpec(
            (plane // steps, count + lines, width // plane), lambda i: (i, 0, 0)
        ),
        scratch_shapes=[
            pltpu.VMEM((3, SLOT_ROWS, part), jnp.float32),
            pltpu.VMEM((lines, part), jnp.float32),
        ],
        name="split",
    )(grads, master, first, second)


def put_strips(core, strips, out, sem):
    count, _, wide = strips.shape
    moves = []
    for i in range(count):
        lane = pl.multiple_of((2 * i + core[0]) * wide, wide)
        moves.append(pltpu.make_async_copy(strips.at[i], out.at[:, pl.ds(lane, wide)], sem.at[i]))
        moves[-1].start()
    return moves


def join_kernel(core, strips, before, out, sem):
    del before
    for move in put_strips(core, strips, out, sem):
        move.wait()


def join(core, strips, before):
    return pl.pallas_call(
        join_kernel,
        out_shape=jax.ShapeDtypeStruct(before.shape, before.dtype),
        in_specs=[SMEM, VMEM, ANY],
        out_specs=ANY,
        scratch_shapes=[pltpu.SemaphoreType.DMA(strips.shape[:1])],
        input_output_aliases={2: 0},
        name="join",
    )(core.reshape(1), near(strips), before)


def own_kernel(at, core, got, rms, master, first, second, strips, *refs):
    outs, weights, rows, grads, sem = refs[:3], refs[3], refs[4], refs[5], refs[6]
    moves = put_strips(core, strips, weights, sem)
    wide = got.shape[2]
    count = grads.shape[1] // wide
    layers = got.shape[0] // count
    for k in range(count):
        grads[:, k * wide : (k + 1) * wide] = got[k * layers + at[0]]
    fill_rows(rows, (master, first, second))
    clip_factor = jnp.minimum(1.0, 1.0 / rms[:, :1])
    new = adamw(rows[0], rows[1], rows[2], grads[...] * clip_factor)
    capacity, slab, _ = master.shape
    for i, (out, old) in enumerate(zip(outs, (master, first, second), strict=True)):
        rows[i] = new[i]
        for s in range(capacity):
            out[s] = jnp.where(at[1 + s] > 0, rows[i, s * slab : (s + 1) * slab, :], old[s])
    for move in moves:
        move.wait()


def pack_kernel(raw, order, route, out):
    plane = raw.shape[0]
    ring = out.shape[0]
    rows = order.shape[0]
    part = rows // ring
    total = raw[0, :rows, :].astype(jnp.float32)
    for j in range(1, plane):
        total = total + raw[j, :rows, :].astype(jnp.float32)
    lines = [raw[j, rows:, :] for j in range(plane)]
    high, low = two_terms(total)
    sources = ((order, high), (order, low), (route, jnp.concatenate(lines, axis=0)))
    for i, (matrix, source) in enumerate(sources):
        chosen = choose(matrix[...], source).astype(out.dtype)
        size = chosen.shape[0] // ring
        for z in range(ring):
            out[z, i * part : i * part + size, :] = chosen[z * size : (z + 1) * size, :]


def reduce_kernel(got, take, spread, out):
    ring = got.shape[0]
    part = take.shape[0] // KINDS
    extra = spread.shape[0] // ring
    total = got[0, :part, :].astype(jnp.float32) + got[0, part : 2 * part, :].astype(jnp.float32)
    for z in range(1, ring):
        total = total + (
            got[z, :part, :].astype(jnp.float32) + got[z, part : 2 * part, :].astype(jnp.float32)
        )
    high, low = two_terms(total)
    lows = choose(spread[...], low)
    squares = jnp.sum(total * total) + jnp.zeros((extra, total.shape[1]), jnp.float32)
    parts = []
    for _ in range(3):
        parts.append(squares.astype(jnp.bfloat16).astype(jnp.float32))
        squares = jnp.where(jnp.abs(parts[-1]) < jnp.inf, squares - parts[-1], 0.0)
    row = lax.broadcasted_iota(jnp.int32, squares.shape, 0)
    lines = jnp.concatenate([got[z, 2 * part :, :] for z in range(ring)], axis=0)
    lines = choose(take[...], lines).astype(out.dtype)
    for z in range(ring):
        block = lows[z * extra : (z + 1) * extra, :]
        for i, value in enumerate(parts):
            block = jnp.where(row == extra - EXTRA + i, value, block)
        out[z, :part, :] = high
        out[z, part : part + extra, :] = block.astype(out.dtype)
        out[z, part + extra :, :] = lines


def stack(every, at, size):
    return jnp.concatenate([every[z, at : at + size, :] for z in range(every.shape[0])], axis=0)


def send_kernel(every, pick, pick_low, out):
    plane, layers, _, wide = out.shape
    ring = every.shape[0]
    part, extra = pick.shape[1] // ring, pick_low.shape[1] // ring
    high, low = stack(every, 0, part), stack(every, part, extra)
    row = lax.broadcasted_iota(jnp.int32, low.shape, 0) % extra
    counted = (row >= extra - EXTRA) & (row < extra - EXTRA + 3)
    squares = jnp.where(counted, low.astype(jnp.float32), 0.0)
    squares = jnp.sum(squares, axis=0, keepdims=True)
    sent = choose(pick[...], high) + choose(pick_low[...], low)
    line = lax.broadcasted_iota(jnp.int32, sent.shape, 0)
    sent = jnp.where(line % SLOT_ROWS == SLOT_ROWS - 1, squares, sent)
    for j in range(plane):
        for layer in range(layers):
            out[j, layer] = sent[j * SLOT_ROWS : (j + 1) * SLOT_ROWS, :]


def step_kernel(element_total, every, got, place, copies, rms):
    part = place.shape[1] // every.shape[0]
    states = every.shape[1] - KINDS * part
    squares = jnp.sum(got[...], axis=0)[SLOT_ROWS - 1 :, :]
    grad_rms = jnp.sqrt(squares / element_total + 1e-06)
    rms[...] = grad_rms
    clip_factor = jnp.minimum(1.0, 1.0 / grad_rms)
    grad = stack(every, 0, part).astype(jnp.float32) * clip_factor
    terms = [stack(every, states + t * part, part).astype(jnp.float32) for t in range(KINDS)]
    param = adamw(terms[0] + terms[1], terms[2], terms[3], grad)[0]
    weights = choose(place[...], param.astype(copies.dtype)).astype(copies.dtype)
    for x in range(copies.shape[0]):
        copies[x] = weights


def shards(micro_grads, master, moment_one, moment_two, owner, slot):
    rows, width = micro_grads.shape[2:]
    capacity, slab = master.shape[1:3]
    ring = lax.axis_size(RING)
    plane = lax.axis_size(PLANE)
    lines = capacity * slab
    wide = width // plane
    layers = lax.axis_size("layer")
    my_z = lax.axis_index(RING)
    part = rows // ring
    plane_lines = plane * SLOT_ROWS
    bf16, f32, i32 = jnp.bfloat16, jnp.float32, jnp.int32
    count = jnp.arange(rows, dtype=i32)
    few = jnp.arange(plane_lines, dtype=i32)

    deal = -(-plane * capacity // ring)
    pair = deal * slab
    home = owner[0] * capacity + slot[0]
    rank = jnp.sum((home[None, :] < home[:, None]).astype(i32), axis=1)
    line = owner[0] * SLOT_ROWS + slot[0] * slab
    member, turn = rank % ring, rank // ring

    def per_row(value):
        return (value[:, None] + jnp.arange(slab, dtype=i32)[None, :]).reshape(rows)

    line_of = per_row(line)
    dealt = per_row(member * part + turn * slab)
    pair_of = per_row(member * pair + turn % deal * slab)
    order = dealt[None, :] == count[:, None]
    place = dealt[:, None] == count[None, :]
    line_at = jnp.sum(jnp.where(order, line_of[None, :], 0), axis=1)
    pick = (my_z * plane_lines + few)[:, None] == line_at[None, :]
    mine = line_of[None, :] == (my_z * plane_lines + few)[:, None]
    pair_at = jnp.sum(jnp.where(mine, pair_of[None, :] + 1, 0), axis=1) - 1
    kind = jnp.arange(KINDS, dtype=i32)[:, None]
    goes = jnp.where(pair_at < 0, -1, pair_at)[None, :]
    goes = jnp.where(goes < 0, -1, (goes // pair * KINDS + kind) * pair + goes % pair)
    chunks = jnp.arange(ring * KINDS * pair, dtype=i32)
    goes = goes.reshape(KINDS, plane, SLOT_ROWS)[:, :, :lines].transpose(1, 0, 2)
    route = goes.reshape(1, plane * KINDS * lines) == chunks[:, None]
    own_line = lax.dynamic_slice_in_dim(line_at, my_z * part, part)
    within = jnp.arange(part, dtype=i32) % pair
    comes = (own_line // plane_lines * KINDS + kind) * pair + within[None, :]
    take = comes.reshape(KINDS * part, 1) == chunks[None, :]
    extra = pair + EXTRA
    special = jnp.arange(ring * extra, dtype=i32)
    spread = special[:, None] == (own_line // plane_lines * extra + within)[None, :]
    low_at = jnp.where(pair_at < 0, -1, pair_at // pair * extra + pair_at % pair)
    pick_low = low_at[:, None] == special[None, :]

    raw = exchange(split(micro_grads[0, 0], master[0], moment_one[0], moment_two[0], plane), PLANE)
    my_slots = lax.axis_index((RING, *PLANE)) * SLOT_ROWS
    my_slots = my_slots + slab * jnp.arange(capacity, dtype=i32)
    keep = jnp.any(line[None, :] == my_slots[:, None], axis=1).astype(i32)
    at = jnp.concatenate([lax.axis_index("layer").astype(i32).reshape(1), keep])
    tables = [t.astype(bf16) for t in (order, route, take, spread, pick, pick_low, place)]
    raw, at, *tables = lax.optimization_barrier((raw, at, *tables))
    order, route, take, spread, pick, pick_low, place = [near(t) for t in tables]
    packed = pl.pallas_call(
        pack_kernel,
        out_shape=pltpu.VMEM((ring, 2 * part + KINDS * pair, wide), bf16),
        in_specs=[VMEM] * 3,
        out_specs=VMEM,
        name="pack",
    )(near(raw), order, route)
    reduced = pl.pallas_call(
        reduce_kernel,
        out_shape=pltpu.VMEM((ring, (1 + KINDS) * part + extra, wide), bf16),
        in_specs=[VMEM] * 3,
        out_specs=VMEM,
        name="reduce",
    )(near(exchange(packed, RING)), take, spread)
    every = exchange(reduced, RING)

    sent = pl.pallas_call(
        send_kernel,
        out_shape=pltpu.VMEM((plane, layers, SLOT_ROWS, wide), f32),
        in_specs=[VMEM] * 3,
        out_specs=VMEM,
        name="send",
    )(near(every), pick, pick_low)
    got = exchange(sent.reshape(plane * layers, SLOT_ROWS, wide), (*PLANE, "layer"))

    copies, rms = pl.pallas_call(
        lambda *refs: step_kernel(float(layers * rows * width), *refs),
        out_shape=(
            pltpu.VMEM((lax.axis_size(HALF), rows, wide), bf16),
            jax.ShapeDtypeStruct((1, wide), f32),
        ),
        in_specs=[VMEM] * 3,
        out_specs=(VMEM, VMEM),
        name="step",
    )(near(every), near(got), place)
    core = lax.axis_index("c")
    halves, got, rms = lax.optimization_barrier((exchange(copies, HALF), got, rms))
    others = lax.ppermute(halves, "c", [(0, 1), (1, 0)])

    *new, weights = pl.pallas_call(
        own_kernel,
        out_shape=(jax.ShapeDtypeStruct(master.shape[1:], f32),) * 3
        + (jax.ShapeDtypeStruct((rows, width), bf16),),
        in_specs=[SMEM] * 2 + [VMEM] * 6,
        out_specs=(VMEM, VMEM, VMEM, ANY),
        scratch_shapes=[
            pltpu.VMEM((3, SLOT_ROWS, width), f32),
            pltpu.VMEM((SLOT_ROWS, width), f32),
            pltpu.SemaphoreType.DMA(halves.shape[:1]),
        ],
        name="own",
    )(
        at,
        core.reshape(1),
        near(got),
        near(rms),
        *[near(o[0]) for o in (master, moment_one, moment_two)],
        near(halves),
    )
    others, weights = lax.optimization_barrier((others, weights))
    weights = join(1 - core, others, weights)
    return (new[0][None], new[1][None], new[2][None], weights[None], rms[0, 0])


def solution(mesh):
    ring = mesh.shape["dp"] // math.prod(PLANE_SHAPE)
    devices = mesh.devices.reshape(ring, *PLANE_SHAPE, mesh.shape["layer"])
    split_mesh = Mesh(devices, (RING, *PLANE, "layer"))
    dp = (RING, *PLANE)
    in_specs = (
        P("layer", dp, None, None),
        P("layer", dp, None, None),
        P("layer", dp, None, None),
        P("layer", dp, None, None),
        P("layer", None),
        P("layer", None),
    )
    out_specs = (
        P("layer", dp, None, None),
        P("layer", dp, None, None),
        P("layer", dp, None, None),
        P("layer", None, None),
        P(),
    )
    return jax.shard_map(
        shards, mesh=split_mesh, in_specs=in_specs, out_specs=out_specs, check_vma=False
    )
```

```python
import math

import jax
import jax.numpy as jnp
from jax import lax
from jax.experimental import pallas as pl
from jax.experimental.pallas import tpu as pltpu
from jax.sharding import Mesh
from jax.sharding import PartitionSpec as P

beta_one = 0.9
beta_two = 0.95
learn_rate = 0.0003
decay_rate = 0.1
adam_eps = 1e-08
step_number = 100.0

RING = "z"
PLANE = ("pair", "x", "c")
PLANE_SHAPE = (2, 4, 2)
HALF = ("pair", "x")
SLOT_ROWS = 8
KINDS = 4
EXTRA = 4


def adamw(param, first, second, grad):
    first_new = beta_one * first + (1.0 - beta_one) * grad
    second_new = beta_two * second + (1.0 - beta_two) * grad * grad
    corr_one = 1.0 - beta_one**step_number
    corr_two = 1.0 - beta_two**step_number
    update = (
        first_new / corr_one / (jnp.sqrt(second_new / corr_two) + adam_eps) + decay_rate * param
    )
    return (param - learn_rate * update, first_new, second_new)


def exchange(chunks, axis):
    return lax.all_to_all(chunks, axis, 0, 0, tiled=True)


def two_terms(value):
    high = value.astype(jnp.bfloat16)
    return high, (value - high.astype(jnp.float32)).astype(jnp.bfloat16)


def choose(matrix, values):
    return jnp.dot(matrix, values, preferred_element_type=jnp.float32)


VMEM = pl.BlockSpec(memory_space=pltpu.VMEM)
SMEM = pl.BlockSpec(memory_space=pltpu.SMEM)
ANY = pl.BlockSpec(memory_space=pl.ANY)


def near(value):
    return pltpu.with_memory_space_constraint(value, pltpu.VMEM)


def fill_rows(rows, states):
    capacity, slab, _ = states[0].shape
    for i, state in enumerate(states):
        for s in range(capacity):
            rows[i, s * slab : (s + 1) * slab, :] = state[s]
        rows[i, capacity * slab :, :] = jnp.ones_like(rows[i, capacity * slab :, :])


def split_kernel(grads, master, first, second, out, rows, tight):
    plane, total, wide = out.shape
    count = grads.shape[0]
    lines = (total - count) // KINDS
    for k in range(plane):
        out[k, :count, :] = grads[:, k * wide : (k + 1) * wide]
    fill_rows(rows, (master, first, second))
    high, low = two_terms(rows[0])
    values = (high.astype(jnp.float32), low.astype(jnp.float32), rows[1], rows[2])
    for t, value in enumerate(values):
        tight[t * lines : (t + 1) * lines, :] = value[:lines]
    terms = tight[...].astype(jnp.bfloat16)
    for k in range(plane):
        out[k, count:, :] = terms[:, k * wide : (k + 1) * wide]


def split(grads, master, first, second, plane):
    count, width = grads.shape
    capacity, slab, _ = master.shape
    lines = KINDS * capacity * slab
    steps = 2
    part = width // steps
    state = pl.BlockSpec((capacity, slab, part), lambda i: (0, 0, i))
    return pl.pallas_call(
        split_kernel,
        grid=(steps,),
        out_shape=jax.ShapeDtypeStruct((plane, count + lines, width // plane), grads.dtype),
        in_specs=[pl.BlockSpec((count, part), lambda i: (0, i)), state, state, state],
        out_specs=pl.BlockSpec(
            (plane // steps, count + lines, width // plane), lambda i: (i, 0, 0)
        ),
        scratch_shapes=[
            pltpu.VMEM((3, SLOT_ROWS, part), jnp.float32),
            pltpu.VMEM((lines, part), jnp.float32),
        ],
        name="split",
    )(grads, master, first, second)


def join_kernel(core, strips, *refs):
    out, sem = refs[-2:]
    count, _, wide = strips.shape
    moves = [
        pltpu.make_async_copy(
            strips.at[i],
            out.at[:, pl.ds(pl.multiple_of((2 * i + core[0]) * wide, wide), wide)],
            sem.at[i],
        )
        for i in range(count)
    ]
    for move in moves:
        move.start()
    for move in moves:
        move.wait()


def join(core, strips, *before):
    count, rows, wide = strips.shape
    return pl.pallas_call(
        join_kernel,
        out_shape=jax.ShapeDtypeStruct((rows, 2 * count * wide), strips.dtype),
        in_specs=[SMEM, VMEM] + [ANY] * len(before),
        out_specs=ANY,
        scratch_shapes=[pltpu.SemaphoreType.DMA((count,))],
        input_output_aliases={2: 0} if before else {},
        name="join",
    )(core.reshape(1), near(strips), *before)


def own_kernel(at, got, rms, master, first, second, *refs):
    outs, rows, grads = refs[:3], refs[3], refs[4]
    wide = got.shape[2]
    count = grads.shape[1] // wide
    layers = got.shape[0] // count
    for k in range(count):
        grads[:, k * wide : (k + 1) * wide] = got[k * layers + at[0]]
    fill_rows(rows, (master, first, second))
    clip_factor = jnp.minimum(1.0, 1.0 / rms[:, :1])
    new = adamw(rows[0], rows[1], rows[2], grads[...] * clip_factor)
    capacity, slab, _ = master.shape
    for i, (out, old) in enumerate(zip(outs, (master, first, second), strict=True)):
        rows[i] = new[i]
        for s in range(capacity):
            out[s] = jnp.where(at[1 + s] > 0, rows[i, s * slab : (s + 1) * slab, :], old[s])


def pack_kernel(raw, order, route, out):
    plane = raw.shape[0]
    ring = out.shape[0]
    rows = order.shape[0]
    part = rows // ring
    total = raw[0, :rows, :].astype(jnp.float32)
    for j in range(1, plane):
        total = total + raw[j, :rows, :].astype(jnp.float32)
    lines = [raw[j, rows:, :] for j in range(plane)]
    high, low = two_terms(total)
    sources = ((order, high), (order, low), (route, jnp.concatenate(lines, axis=0)))
    for i, (matrix, source) in enumerate(sources):
        chosen = choose(matrix[...], source).astype(out.dtype)
        size = chosen.shape[0] // ring
        for z in range(ring):
            out[z, i * part : i * part + size, :] = chosen[z * size : (z + 1) * size, :]


def reduce_kernel(got, take, spread, out):
    ring = got.shape[0]
    part = take.shape[0] // KINDS
    extra = spread.shape[0] // ring
    total = got[0, :part, :].astype(jnp.float32) + got[0, part : 2 * part, :].astype(jnp.float32)
    for z in range(1, ring):
        total = total + (
            got[z, :part, :].astype(jnp.float32) + got[z, part : 2 * part, :].astype(jnp.float32)
        )
    high, low = two_terms(total)
    lows = choose(spread[...], low)
    squares = jnp.sum(total * total) + jnp.zeros((extra, total.shape[1]), jnp.float32)
    parts = []
    for _ in range(3):
        parts.append(squares.astype(jnp.bfloat16).astype(jnp.float32))
        squares = jnp.where(jnp.abs(parts[-1]) < jnp.inf, squares - parts[-1], 0.0)
    row = lax.broadcasted_iota(jnp.int32, squares.shape, 0)
    lines = jnp.concatenate([got[z, 2 * part :, :] for z in range(ring)], axis=0)
    lines = choose(take[...], lines).astype(out.dtype)
    for z in range(ring):
        block = lows[z * extra : (z + 1) * extra, :]
        for i, value in enumerate(parts):
            block = jnp.where(row == extra - EXTRA + i, value, block)
        out[z, :part, :] = high
        out[z, part : part + extra, :] = block.astype(out.dtype)
        out[z, part + extra :, :] = lines


def stack(every, at, size):
    return jnp.concatenate([every[z, at : at + size, :] for z in range(every.shape[0])], axis=0)


def send_kernel(every, pick, pick_low, out):
    plane, layers, _, wide = out.shape
    ring = every.shape[0]
    part, extra = pick.shape[1] // ring, pick_low.shape[1] // ring
    high, low = stack(every, 0, part), stack(every, part, extra)
    row = lax.broadcasted_iota(jnp.int32, low.shape, 0) % extra
    counted = (row >= extra - EXTRA) & (row < extra - EXTRA + 3)
    squares = jnp.where(counted, low.astype(jnp.float32), 0.0)
    squares = jnp.sum(squares, axis=0, keepdims=True)
    sent = choose(pick[...], high) + choose(pick_low[...], low)
    line = lax.broadcasted_iota(jnp.int32, sent.shape, 0)
    sent = jnp.where(line % SLOT_ROWS == SLOT_ROWS - 1, squares, sent)
    for j in range(plane):
        for layer in range(layers):
            out[j, layer] = sent[j * SLOT_ROWS : (j + 1) * SLOT_ROWS, :]


def step_kernel(element_total, every, got, place, copies, rms):
    part = place.shape[1] // every.shape[0]
    states = every.shape[1] - KINDS * part
    squares = jnp.sum(got[...], axis=0)[SLOT_ROWS - 1 :, :]
    grad_rms = jnp.sqrt(squares / element_total + 1e-06)
    rms[...] = grad_rms
    clip_factor = jnp.minimum(1.0, 1.0 / grad_rms)
    grad = stack(every, 0, part).astype(jnp.float32) * clip_factor
    terms = [stack(every, states + t * part, part).astype(jnp.float32) for t in range(KINDS)]
    param = adamw(terms[0] + terms[1], terms[2], terms[3], grad)[0]
    weights = choose(place[...], param.astype(copies.dtype)).astype(copies.dtype)
    for x in range(copies.shape[0]):
        copies[x] = weights


def shards(micro_grads, master, moment_one, moment_two, owner, slot):
    rows, width = micro_grads.shape[2:]
    capacity, slab = master.shape[1:3]
    ring = lax.axis_size(RING)
    plane = lax.axis_size(PLANE)
    lines = capacity * slab
    wide = width // plane
    layers = lax.axis_size("layer")
    my_z = lax.axis_index(RING)
    part = rows // ring
    plane_lines = plane * SLOT_ROWS
    bf16, f32, i32 = jnp.bfloat16, jnp.float32, jnp.int32
    count = jnp.arange(rows, dtype=i32)
    few = jnp.arange(plane_lines, dtype=i32)

    deal = -(-plane * capacity // ring)
    pair = deal * slab
    home = owner[0] * capacity + slot[0]
    rank = jnp.sum((home[None, :] < home[:, None]).astype(i32), axis=1)
    line = owner[0] * SLOT_ROWS + slot[0] * slab
    member, turn = rank % ring, rank // ring

    def per_row(value):
        return (value[:, None] + jnp.arange(slab, dtype=i32)[None, :]).reshape(rows)

    line_of = per_row(line)
    dealt = per_row(member * part + turn * slab)
    pair_of = per_row(member * pair + turn % deal * slab)
    order = dealt[None, :] == count[:, None]
    place = dealt[:, None] == count[None, :]
    line_at = jnp.sum(jnp.where(order, line_of[None, :], 0), axis=1)
    pick = (my_z * plane_lines + few)[:, None] == line_at[None, :]
    mine = line_of[None, :] == (my_z * plane_lines + few)[:, None]
    pair_at = jnp.sum(jnp.where(mine, pair_of[None, :] + 1, 0), axis=1) - 1
    kind = jnp.arange(KINDS, dtype=i32)[:, None]
    goes = jnp.where(pair_at < 0, -1, pair_at)[None, :]
    goes = jnp.where(goes < 0, -1, (goes // pair * KINDS + kind) * pair + goes % pair)
    chunks = jnp.arange(ring * KINDS * pair, dtype=i32)
    goes = goes.reshape(KINDS, plane, SLOT_ROWS)[:, :, :lines].transpose(1, 0, 2)
    route = goes.reshape(1, plane * KINDS * lines) == chunks[:, None]
    own_line = lax.dynamic_slice_in_dim(line_at, my_z * part, part)
    within = jnp.arange(part, dtype=i32) % pair
    comes = (own_line // plane_lines * KINDS + kind) * pair + within[None, :]
    take = comes.reshape(KINDS * part, 1) == chunks[None, :]
    extra = pair + EXTRA
    special = jnp.arange(ring * extra, dtype=i32)
    spread = special[:, None] == (own_line // plane_lines * extra + within)[None, :]
    low_at = jnp.where(pair_at < 0, -1, pair_at // pair * extra + pair_at % pair)
    pick_low = low_at[:, None] == special[None, :]

    raw = exchange(split(micro_grads[0, 0], master[0], moment_one[0], moment_two[0], plane), PLANE)
    my_slots = lax.axis_index((RING, *PLANE)) * SLOT_ROWS
    my_slots = my_slots + slab * jnp.arange(capacity, dtype=i32)
    keep = jnp.any(line[None, :] == my_slots[:, None], axis=1).astype(i32)
    at = jnp.concatenate([lax.axis_index("layer").astype(i32).reshape(1), keep])
    tables = [t.astype(bf16) for t in (order, route, take, spread, pick, pick_low, place)]
    raw, at, *tables = lax.optimization_barrier((raw, at, *tables))
    order, route, take, spread, pick, pick_low, place = [near(t) for t in tables]
    packed = pl.pallas_call(
        pack_kernel,
        out_shape=pltpu.VMEM((ring, 2 * part + KINDS * pair, wide), bf16),
        in_specs=[VMEM] * 3,
        out_specs=VMEM,
        name="pack",
    )(near(raw), order, route)
    reduced = pl.pallas_call(
        reduce_kernel,
        out_shape=pltpu.VMEM((ring, (1 + KINDS) * part + extra, wide), bf16),
        in_specs=[VMEM] * 3,
        out_specs=VMEM,
        name="reduce",
    )(near(exchange(packed, RING)), take, spread)
    every = exchange(reduced, RING)

    sent = pl.pallas_call(
        send_kernel,
        out_shape=pltpu.VMEM((plane, layers, SLOT_ROWS, wide), f32),
        in_specs=[VMEM] * 3,
        out_specs=VMEM,
        name="send",
    )(near(every), pick, pick_low)
    got = exchange(sent.reshape(plane * layers, SLOT_ROWS, wide), (*PLANE, "layer"))

    copies, rms = pl.pallas_call(
        lambda *refs: step_kernel(float(layers * rows * width), *refs),
        out_shape=(
            pltpu.VMEM((lax.axis_size(HALF), rows, wide), bf16),
            pltpu.VMEM((1, wide), f32),
        ),
        in_specs=[VMEM] * 3,
        out_specs=(VMEM, VMEM),
        name="step",
    )(near(every), near(got), place)
    core = lax.axis_index("c")
    halves, got, rms = lax.optimization_barrier((exchange(copies, HALF), got, rms))
    others = lax.ppermute(halves, "c", [(0, 1), (1, 0)])
    weights = join(core, halves)

    new = pl.pallas_call(
        own_kernel,
        out_shape=(jax.ShapeDtypeStruct(master.shape[1:], f32),) * 3,
        in_specs=[SMEM] + [VMEM] * 5,
        out_specs=(VMEM,) * 3,
        scratch_shapes=[
            pltpu.VMEM((3, SLOT_ROWS, width), f32),
            pltpu.VMEM((SLOT_ROWS, width), f32),
        ],
        name="own",
    )(at, near(got), near(rms), *[near(o[0]) for o in (master, moment_one, moment_two)])
    others, weights = lax.optimization_barrier((others, weights))
    weights = join(1 - core, others, weights)
    return (new[0][None], new[1][None], new[2][None], weights[None], rms[0, 0])


def solution(mesh):
    ring = mesh.shape["dp"] // math.prod(PLANE_SHAPE)
    devices = mesh.devices.reshape(ring, *PLANE_SHAPE, mesh.shape["layer"])
    split_mesh = Mesh(devices, (RING, *PLANE, "layer"))
    dp = (RING, *PLANE)
    in_specs = (
        P("layer", dp, None, None),
        P("layer", dp, None, None),
        P("layer", dp, None, None),
        P("layer", dp, None, None),
        P("layer", None),
        P("layer", None),
    )
    out_specs = (
        P("layer", dp, None, None),
        P("layer", dp, None, None),
        P("layer", dp, None, None),
        P("layer", None, None),
        P(),
    )
    return jax.shard_map(
        shards, mesh=split_mesh, in_specs=in_specs, out_specs=out_specs, check_vma=False
    )
```
